32 devices in a mesh: grp: 2 (over x), rows: 16 (over z, y, core).
Axes of the slice: x: 2, y: 2, z: 4, core: 2. Of those that a mesh axis runs over, the one named last changes fastest.
Arguments:
- histories: float32 [4096, 384], P(('grp', 'rows')), parts along dimension 0, may hold values from -6 to 6
- modal_map: float32 [4096, 8192], P(('grp', 'rows')), parts along dimension 0, may hold values from -0.1875 to 0.1875
- recovery: float32 [8192, 8192], P(('grp', 'rows')), parts along dimension 0, may hold values from -0.0625 to 0.0625
Outputs:
- responses: float32 [8192, 384], P(('grp', 'rows')), parts along dimension 0
- peak_response: float32 [4, 8192], P(None, ('grp', 'rows')), parts along dimension 1
- rms_response: float32 [4, 8192], P(None, ('grp', 'rows')), parts along dimension 1
The draws below stay inside these ranges and needn't reach their ends.
There are 2 independent parts, one for each index of `grp`. The reference program is written for one: setup_inputs(seed, part) draws one part's arguments, and reference() takes and returns one part's arrays. A program takes and returns all parts, laid end to end along the dimension named above; each array names one. Nothing has to cross between parts.
All inputs are finite; a program needn't handle non-finite values.
Results may differ from the reference program's by a relative error of at most 0.000071.
Values sent between devices are 32-bit elements; how exact they have to be, the bound alone decides.
A program may use at most 64 MiB of HBM per device.

```python
import jax
import jax.numpy as jnp
from jax import lax

MODES = 8192
COUPLED = 2048
CASES = 4
STEPS = 96
OUTPUTS = 4096
TIME = 384


def raised(drawn, stream_key, source, target, parts, factor):
    owner, partner = [(jnp.arange(drawn.shape[axis_at]) // (drawn.shape[axis_at] // parts)).reshape([-1 if axis == axis_at else 1 for axis in range(drawn.ndim)]) for axis_at in (source, target)]
    chosen = jax.random.permutation(stream_key, parts)[partner]
    strong = (owner == chosen) | (owner == (partner + parts // 2) % parts)
    return jnp.where(strong, factor * drawn, drawn)


def block_scale(rng, shape, split, smallest, high):
    factor_of = 1.0
    for dim, shards_of in split:
        draws = jax.random.uniform(jax.random.fold_in(jax.random.fold_in(rng, 6), dim), (shards_of,), jnp.float32, smallest / len(split), high / len(split))
        factor_of = factor_of * jnp.repeat(jnp.exp(draws), shape[dim] // shards_of).reshape((-1,) + (1,) * (len(shape) - 1 - dim))
    return factor_of


def bell_draw(stream_key, shape, spread, most, split=(), held_as=jnp.bfloat16):
    values = jax.random.normal(stream_key, shape, jnp.float32) * spread
    if len(split) > 0:
        values = block_scale(stream_key, shape, split, -0.22, 0.18) * values
    return jnp.clip(values, min=-most, max=most).astype(held_as)


def gaussian_with(own_key, extent, deviation, bound, shards, heavy, dtype=jnp.bfloat16):
    drawn = deviation * jax.random.normal(own_key, extent, jnp.float32)
    if shards:
        drawn = drawn * block_scale(own_key, extent, shards, -0.22, 0.18)
    return jnp.clip(raised(drawn, jax.random.fold_in(own_key, 3), *heavy), -bound, bound).astype(dtype)


def setup_inputs(seed: int = 0, part: int = 0) -> dict:
    streams_of = jax.random.split(jax.random.key(seed), 4)
    part_keys = jax.random.split(jax.random.fold_in(streams_of[3], part), 4)
    return {
        "histories": bell_draw(part_keys[0], (COUPLED, TIME), 1.0, 6.0, ((0, 16),), jnp.float32),
        "modal_map": gaussian_with(part_keys[1], (COUPLED, MODES), COUPLED ** -0.5, 0.1875, ((0, 16),), (0, 1, 16, 2.0), jnp.float32),
        "recovery": bell_draw(part_keys[2], (OUTPUTS, MODES), MODES ** -0.5, 0.0625, ((0, 16),), jnp.float32),
    }


epsilon = 1e-06

def reference(histories, modal_map, recovery):
    modal_rows = lax.dot_general(modal_map, histories, (((0,), (0,)), ((), ())), precision=lax.Precision.HIGHEST, preferred_element_type=jnp.float32)
    responses = jnp.dot(recovery, modal_rows, precision=lax.Precision.HIGHEST, preferred_element_type=jnp.float32)
    by_case = responses.reshape(responses.shape[0], CASES, STEPS)
    peak_response = lax.optimization_barrier(jnp.max(jnp.abs(by_case), axis=2)).T
    rms_response = jnp.sqrt(lax.optimization_barrier(jnp.mean(by_case * by_case, axis=2)) + epsilon).T
    return (responses, peak_response, rms_response)
```

```python
import functools

import jax
import jax.numpy as jnp
from jax import lax
from jax.experimental import pallas as pl
from jax.experimental.pallas import tpu as pltpu
from jax.sharding import PartitionSpec as P

CASES = 4
SUBS = 2
epsilon = 1e-06
MESH = pl.DeviceIdType.MESH


def split(x):
    high = x.astype(jnp.bfloat16)
    return high, (x - high.astype(jnp.float32)).astype(jnp.bfloat16)


def dot3(a, b, dims):
    mul = functools.partial(
        lax.dot_general, dimension_numbers=(dims, ((), ())), preferred_element_type=jnp.float32
    )
    return mul(a[0], b[0]) + (mul(a[0], b[1]) + mul(a[1], b[0]))


def ring_position(chips, chip):
    if chips == 8:
        z, y = chip // 2, chip % 2
        return y * (chips - 1 - 2 * z) + z
    return chip


def chip_at(chips, position):
    if chips == 8:
        y = position // 4
        return (y * (chips - 1 - 2 * position) + position) * 2 + y
    return position


def kernel(
    chips, ways, h_ref, m_ref, r_ref, out_ref,
    hist, hist_hi, hist_lo, m_buf, r_buf, part, landed, rows, acc, acc_other,
    local_sem, pair_send, pair_recv, m_local, m_send, m_recv, rs_send, rs_recv, ag_send, ag_recv,
):
    me = lax.axis_index("rows")
    core = me % 2
    partner = me + 1 - 2 * core
    pos = ring_position(chips, me // 2)
    after = chip_at(chips, (pos + 1) % chips) * 2 + core
    before = chip_at(chips, (pos + chips - 1) % chips) * 2 + core
    targets = (after, before)
    signs = (1, -1)

    modes, outs = h_ref.shape[0], r_ref.shape[0]
    half = m_ref.shape[1] // 2
    block = half // chips
    unit = block // ways
    piece = unit // SUBS
    cuts = SUBS if piece % 128 == 0 else 1
    width = unit // cuts

    def at(p):
        return (p + 2 * chips) % chips

    def cols(base, b, d, start=0, size=unit):
        return pl.ds(pl.multiple_of(base + b * block + d * unit + start, 128), size)

    def remote(src, dst, send, recv, to):
        return pltpu.make_async_remote_copy(
            src_ref=src, dst_ref=dst, send_sem=send, recv_sem=recv,
            device_id={"rows": to}, device_id_type=MESH,
        )

    def sum_block(k, d):
        return at(pos - signs[d] * (k + 1))

    def m_copy(k, d):
        b = sum_block(k, d)
        return remote(
            m_ref.at[:, cols((1 - core) * half, b, d)],
            m_buf.at[pl.ds(modes, modes), cols(0, b, d)],
            m_send.at[d, k], m_recv.at[d, k], partner,
        )

    def own_m(k, d):
        b = sum_block(k, d)
        return pltpu.make_async_copy(
            m_ref.at[:, cols(core * half, b, d)],
            m_buf.at[pl.ds(0, modes), cols(0, b, d)], m_local.at[d, k],
        )

    def rs_copy(k, d, j):
        view = (d, k, pl.ds(j * piece, piece))
        return remote(part.at[view], landed.at[view], rs_send.at[d, k, j], rs_recv.at[d, k, j], targets[d])

    def ag_copy(s, d, j, arrives=False):
        b = at(pos - signs[d] * (s + 1 if arrives else s))
        view = (b, d, pl.ds(j * piece, piece))
        return remote(rows.at[view], rows.at[view], ag_send.at[d, s, j], ag_recv.at[d, s, j], targets[d])

    own_h = pltpu.make_async_copy(h_ref, hist.at[pl.ds(0, modes)], local_sem.at[0])
    own_r = pltpu.make_async_copy(
        r_ref.at[:, pl.ds(pl.multiple_of(core * half, 128), half)],
        r_buf.at[pl.ds(0, outs)], local_sem.at[1],
    )
    h_copy = remote(h_ref, hist.at[pl.ds(modes, modes)], pair_send.at[0], pair_recv.at[0], partner)
    r_copy = remote(
        r_ref.at[:, pl.ds(pl.multiple_of((1 - core) * half, 128), half)],
        r_buf.at[pl.ds(outs, outs)], pair_send.at[1], pair_recv.at[1], partner,
    )
    acc_copy = remote(acc.at[pl.ds(outs, outs)], acc_other, pair_send.at[2], pair_recv.at[2], partner)

    own_h.start()
    for d in range(ways):
        own_m(0, d).start()
    barrier = pltpu.get_barrier_semaphore()
    for other in (after, before, partner):
        pl.semaphore_signal(barrier, inc=1, device_id={"rows": other}, device_id_type=MESH)
    pl.semaphore_wait(barrier, 3)

    h_copy.start()
    for d in range(ways):
        m_copy(0, d).start()

    @pl.loop(1, chips)
    def _(k):
        for d in range(ways):
            own_m(k, d).start()
            m_copy(k, d).start()

    own_h.wait()
    hist_hi[pl.ds(0, modes)], hist_lo[pl.ds(0, modes)] = split(hist[pl.ds(0, modes)])
    h_copy.wait_recv()
    hist_hi[pl.ds(modes, modes)], hist_lo[pl.ds(modes, modes)] = split(hist[pl.ds(modes, modes)])

    def shapes_here(k, d):
        own_m(k, d).wait()
        m_copy(k, d).wait_recv()

    def partial_rows(k, d, start=0, size=unit):
        shapes = split(m_buf[:, cols(0, sum_block(k, d), d, start, size)])
        return dot3(shapes, (hist_hi[...], hist_lo[...]), ((0,), (0,)))

    for cut in range(cuts):
        for d in range(ways):
            if cut == 0:
                shapes_here(0, d)
            start = cut * width
            part[d, 0, pl.ds(start, width)] = partial_rows(0, d, start, width)
            for j in range(cut * SUBS // cuts, (cut + 1) * SUBS // cuts):
                rs_copy(0, d, j).start()

    own_r.start()
    r_copy.start()

    @pl.loop(1, chips - 1)
    def _(k):
        for d in range(ways):
            shapes_here(k, d)
            part[d, k] = partial_rows(k, d)
        for j in range(SUBS):
            for d in range(ways):
                rs_copy(k - 1, d, j).wait_recv()
                view = (d, k, pl.ds(j * piece, piece))
                part[view] = part[view] + landed[d, k - 1, pl.ds(j * piece, piece)]
                rs_copy(k, d, j).start()

    last = chips - 1
    for d in range(ways):
        shapes_here(last, d)
        rows[pos, d] = partial_rows(last, d)
    for j in range(SUBS):
        for d in range(ways):
            rs_copy(last - 1, d, j).wait_recv()
            view = (pos, d, pl.ds(j * piece, piece))
            rows[view] = rows[view] + landed[d, last - 1, pl.ds(j * piece, piece)]
            ag_copy(0, d, j).start()

    own_r.wait()
    r_copy.wait_recv()

    def recovered(b, d):
        return dot3(split(r_buf[:, cols(0, b, d)]), split(rows[b, d]), ((1,), (0,)))

    acc[...] = recovered(pos, 0)
    for d in range(1, ways):
        acc[...] += recovered(pos, d)

    @pl.loop(0, chips - 2)
    def _(s):
        for j in range(SUBS):
            for d in range(ways):
                ag_copy(s, d, j, arrives=True).wait_recv()
                ag_copy(s + 1, d, j).start()
        for d in range(ways):
            acc[...] += recovered(at(pos - signs[d] * (s + 1)), d)

    for cut in range(cuts):
        for d in range(ways):
            for j in range(cut * SUBS // cuts, (cut + 1) * SUBS // cuts):
                ag_copy(chips - 2, d, j, arrives=True).wait_recv()
            b, start = at(pos - signs[d] * (chips - 1)), cut * width
            weights = split(r_buf[:, cols(0, b, d, start, width)])
            finished = split(rows[b, d, pl.ds(start, width)])
            final = cut == cuts - 1 and d == ways - 1
            for base in (outs, 0):
                own = tuple(w[base : base + outs] for w in weights)
                acc[pl.ds(base, outs)] += dot3(own, finished, ((1,), (0,)))
                if final and base:
                    acc_copy.start()

    h_copy.wait_send()
    r_copy.wait_send()

    @pl.loop(0, chips)
    def _(k):
        for d in range(ways):
            m_copy(k, d).wait_send()

    @pl.loop(0, chips - 1)
    def _(k):
        for d in range(ways):
            for j in range(SUBS):
                rs_copy(k, d, j).wait_send()
                ag_copy(k, d, j).wait_send()

    acc_copy.wait()
    out_ref[...] = acc[pl.ds(0, outs)] + acc_other[...]


def statistics(found_ref, out_ref, peak_ref, rms_ref):
    responses = found_ref[...]
    out_ref[...] = responses
    by_time = responses.T
    steps = by_time.shape[0] // CASES
    for k in range(CASES):
        case = by_time[k * steps : (k + 1) * steps]
        peak_ref[k : k + 1] = jnp.max(jnp.abs(case), axis=0, keepdims=True)
        mean = jnp.sum(case * case, axis=0, keepdims=True) / steps
        rms_ref[k : k + 1] = jnp.sqrt(mean + epsilon)


ACROSS, INWARD, OUTWARD = range(3)
H_ACROSS, H_RELAY, SHARE, PARTIAL, REDUCE, ROOT, GATHER, RECOVER, REDUCED, GATHERED = range(10)
ALONG_FIRST, ACROSS_FIRST = range(2)
GROUPS = (ACROSS_FIRST, ACROSS_FIRST, ALONG_FIRST, ACROSS_FIRST)
PIECES = 8
ORDERS = (
    (
        (0,), (3, 2, 1, 1), (4, 2, 1, 6, 1, ()), (3, 2, 1, 0), (4, 2, 1, 1, 1, ()), (3, 2, 0, 1), (4, 2, 1, 5, 0, ()),
        (3, 2, 0, 0), (4, 2, 0, 6, 1, ()), (4, 2, 1, 2, 0, ()), (1,), (4, 2, 0, 1, 1, ()), (2, 0, 1),
        (4, 2, 0, 5, 1, (0,)), (8, 2, 1, 6, 1), (4, 2, 0, 2, 1, (0,)), (8, 2, 1, 1, 1), (8, 2, 1, 5, 0), (2, 0, 0),
        (4, 2, 1, 3, 1, ()), (8, 2, 0, 6, 1), (8, 2, 1, 2, 0), (4, 2, 0, 0, 1, ()), (3, 0, 0, 1), (8, 2, 0, 1, 1),
        (4, 0, 0, 6, 1, ()), (2, 1, 1), (8, 2, 0, 5, 1), (4, 0, 0, 4, 1, ()), (8, 2, 0, 2, 1), (4, 0, 0, 5, 1, ()),
        (3, 0, 0, 0), (8, 2, 1, 3, 1), (4, 0, 0, 1, 1, ()), (2, 1, 0), (8, 2, 0, 0, 1), (4, 0, 0, 7, 1, ()),
        (8, 0, 0, 6, 1), (3, 1, 0, 1), (4, 1, 0, 4, 1, ()), (8, 0, 0, 4, 1), (6, 2, 0, 6, 0), (4, 1, 0, 5, 1, ()),
        (8, 0, 0, 5, 1), (2, 3, 1), (4, 1, 0, 6, 1, ()), (3, 1, 0, 0), (8, 0, 0, 1, 1), (4, 1, 0, 3, 1, ()),
        (8, 0, 0, 7, 1), (5, 0, 0, 3, (1,)), (4, 1, 0, 7, 1, ()), (6, 0, 0, 3, 0), (8, 1, 0, 4, 1),
        (5, 0, 0, 2, (1,)), (4, 2, 0, 4, 1, ()), (9, 2, 0, 6, 0), (6, 0, 0, 2, 0), (8, 1, 0, 5, 1),
        (4, 2, 1, 4, 1, ()), (3, 3, 0, 1), (2, 3, 0), (8, 1, 0, 6, 1), (5, 0, 0, 0, (1,)), (7, 0, 0, 0),
        (6, 0, 0, 0, 1), (8, 1, 0, 3, 1), (4, 3, 0, 6, 1, ()), (8, 1, 0, 7, 1), (4, 3, 0, 4, 1, ()), (9, 0, 0, 3, 0),
        (4, 2, 0, 7, 0, ()), (8, 2, 0, 4, 1), (5, 1, 0, 2, (1,)), (4, 3, 0, 5, 1, ()), (9, 0, 0, 2, 0),
        (6, 1, 0, 2, 0), (8, 2, 1, 4, 1), (3, 3, 0, 0), (5, 1, 0, 1, (1,)), (4, 3, 0, 1, 1, ()), (6, 1, 0, 1, 0),
        (9, 0, 0, 0, 1), (4, 2, 1, 7, 1, (0,)), (6, 0, 0, 6, 0), (8, 3, 0, 6, 1), (5, 1, 0, 0, (1,)), (7, 1, 0, 0),
        (4, 3, 0, 7, 1, ()), (6, 1, 0, 0, 0), (8, 3, 0, 4, 1), (8, 2, 0, 7, 0), (6, 1, 0, 1, 1), (6, 0, 0, 0, 0),
        (8, 3, 0, 5, 1), (9, 1, 0, 2, 0), (4, 2, 1, 0, 1, ()), (6, 0, 0, 7, 0), (8, 3, 0, 1, 1), (9, 1, 0, 1, 0),
        (5, 3, 0, 3, (1,)), (6, 0, 1, 3, 1), (6, 3, 0, 3, 0), (8, 2, 1, 7, 1), (9, 0, 0, 6, 0), (7, 0, 1, 0),
        (6, 1, 1, 0, 1), (6, 1, 0, 3, 0), (8, 3, 0, 7, 1), (9, 1, 0, 0, 0), (5, 3, 0, 2, (1,)), (6, 1, 1, 2, 1),
        (6, 3, 0, 2, 0), (9, 1, 0, 1, 1), (9, 0, 0, 0, 0), (6, 3, 0, 3, 1), (6, 3, 1, 1, 0), (8, 2, 1, 0, 1),
        (9, 0, 0, 7, 0), (7, 1, 1, 0), (5, 2, 0, 3, (1,)), (6, 2, 0, 3, 1), (6, 2, 0, 3, 0), (9, 0, 1, 3, 1),
        (9, 3, 0, 3, 0), (5, 3, 0, 0, (1,)), (6, 3, 0, 0, 1), (6, 3, 0, 0, 0), (9, 1, 1, 0, 1), (9, 1, 0, 3, 0),
        (7, 3, 0, 0), (6, 3, 1, 2, 1), (6, 1, 0, 6, 0), (9, 1, 1, 2, 1), (9, 3, 0, 2, 0), (6, 0, 0, 2, 1),
        (6, 3, 1, 6, 0), (9, 3, 0, 3, 1), (9, 3, 1, 1, 0), (7, 3, 1, 0), (6, 0, 1, 2, 1), (6, 0, 1, 4, 0),
        (9, 2, 0, 3, 1), (9, 2, 0, 3, 0), (6, 1, 0, 2, 1), (6, 1, 1, 7, 0), (9, 3, 0, 0, 1), (9, 3, 0, 0, 0),
        (7, 1, 1, 1), (6, 1, 1, 3, 1), (6, 1, 1, 5, 0), (9, 3, 1, 2, 1), (9, 1, 0, 6, 0), (6, 3, 1, 0, 1),
        (6, 3, 0, 4, 0), (9, 0, 0, 2, 1), (9, 3, 1, 6, 0), (6, 2, 0, 4, 0), (9, 0, 1, 2, 1), (9, 0, 1, 4, 0),
        (7, 1, 0, 1), (6, 2, 1, 7, 0), (9, 1, 0, 2, 1), (9, 1, 1, 7, 0), (6, 3, 0, 7, 0), (9, 1, 1, 3, 1),
        (9, 1, 1, 5, 0), (7, 2, 1, 1), (6, 3, 1, 5, 0), (9, 3, 1, 0, 1), (9, 3, 0, 4, 0), (7, 2, 0, 1), (7, 2, 1, 0),
        (6, 2, 1, 0, 0), (9, 2, 0, 4, 0), (7, 3, 1, 1), (7, 0, 0, 1), (9, 2, 1, 7, 0), (7, 3, 0, 1), (7, 0, 1, 1),
        (9, 3, 0, 7, 0), (7, 2, 0, 0), (9, 3, 1, 5, 0), (9, 2, 1, 0, 0),
    ),
    (
        (0,), (3, 2, 1, 1), (4, 2, 1, 5, 1, ()), (3, 2, 1, 0), (3, 2, 0, 1), (4, 2, 0, 7, 1, ()), (2, 0, 1),
        (3, 2, 0, 0), (4, 2, 1, 6, 1, (2,)), (1,), (4, 2, 1, 2, 0, (1,)), (8, 2, 1, 5, 1), (4, 2, 0, 6, 1, (2,)),
        (4, 2, 1, 1, 0, (1, 2)), (3, 0, 0, 1), (8, 2, 0, 7, 1), (2, 0, 0), (8, 2, 1, 6, 1), (4, 2, 0, 5, 1, (2,)),
        (5, 2, 0, 1, (0, 1, 2)), (6, 2, 0, 1, 1), (6, 2, 0, 1, 2), (8, 2, 1, 2, 0), (6, 2, 0, 1, 0), (8, 2, 0, 6, 1),
        (5, 2, 0, 2, (0, 1, 2)), (6, 2, 0, 2, 1), (6, 2, 0, 2, 2), (8, 2, 1, 1, 0), (6, 2, 0, 2, 0), (6, 2, 0, 6, 2),
        (3, 0, 0, 0), (2, 1, 1), (8, 2, 0, 5, 1), (4, 0, 0, 6, 1, (2,)), (6, 2, 0, 5, 2), (6, 2, 1, 1, 1),
        (6, 2, 1, 1, 2), (9, 2, 0, 1, 1), (9, 2, 0, 1, 2), (4, 0, 0, 4, 1, (2,)), (6, 2, 1, 2, 2), (9, 2, 0, 1, 0),
        (9, 2, 0, 2, 1), (9, 2, 0, 2, 2), (4, 0, 0, 5, 1, (2,)), (2, 1, 0), (5, 0, 0, 1, (1, 2)), (9, 2, 0, 6, 2),
        (6, 0, 0, 1, 2), (9, 2, 0, 2, 0), (6, 0, 0, 1, 1), (8, 0, 0, 6, 1), (4, 0, 0, 3, 2, (1,)), (9, 2, 0, 5, 2),
        (3, 1, 0, 1), (4, 0, 0, 7, 1, (2,)), (9, 2, 1, 1, 1), (4, 0, 0, 2, 2, (1,)), (9, 2, 1, 1, 2), (6, 0, 0, 1, 0),
        (4, 1, 0, 4, 1, (2,)), (8, 0, 0, 4, 1), (6, 0, 0, 6, 2), (9, 2, 1, 2, 2), (6, 0, 0, 6, 0),
        (4, 1, 0, 5, 1, (2,)), (3, 1, 0, 0), (8, 0, 0, 5, 1), (9, 0, 0, 1, 2), (4, 0, 0, 0, 2, (1,)), (2, 3, 1),
        (4, 1, 0, 6, 1, (2,)), (6, 0, 1, 1, 2), (9, 0, 0, 1, 1), (5, 1, 0, 3, (1, 2)), (8, 0, 0, 3, 2),
        (6, 1, 0, 3, 1), (6, 1, 0, 3, 2), (8, 0, 0, 7, 1), (8, 0, 0, 2, 2), (4, 1, 0, 7, 1, (2,)),
        (4, 1, 0, 2, 2, (1,)), (9, 0, 0, 1, 0), (2, 3, 0), (8, 1, 0, 4, 1), (9, 0, 0, 6, 2), (6, 2, 1, 2, 1),
        (4, 1, 0, 1, 2, (1,)), (9, 0, 0, 6, 0), (8, 1, 0, 5, 1), (8, 0, 0, 0, 2), (3, 3, 0, 1), (6, 1, 0, 4, 2),
        (6, 0, 0, 0, 1), (8, 1, 0, 6, 1), (9, 0, 1, 1, 2), (4, 2, 0, 4, 0, (2,)), (4, 1, 0, 0, 2, (1,)),
        (4, 3, 0, 6, 1, (2,)), (9, 1, 0, 3, 1), (9, 1, 0, 3, 2), (6, 1, 0, 4, 0), (6, 2, 1, 5, 2),
        (4, 3, 0, 4, 1, (2,)), (8, 1, 0, 7, 1), (8, 1, 0, 2, 2), (3, 3, 0, 0), (6, 0, 0, 0, 0), (6, 0, 0, 7, 2),
        (4, 3, 0, 5, 1, (2,)), (9, 2, 1, 2, 1), (8, 1, 0, 1, 2), (4, 2, 1, 4, 1, (0, 2)), (6, 0, 0, 7, 0),
        (5, 3, 0, 1, (1, 2)), (9, 0, 0, 0, 1), (4, 3, 0, 3, 2, (1,)), (9, 1, 0, 4, 2), (6, 3, 0, 1, 0),
        (6, 1, 1, 4, 2), (4, 2, 1, 7, 1, (2,)), (8, 2, 0, 4, 0), (8, 1, 0, 0, 2), (8, 3, 0, 6, 1),
        (4, 3, 0, 2, 2, (1,)), (4, 3, 0, 7, 1, (2,)), (9, 1, 0, 4, 0), (8, 3, 0, 4, 1), (4, 2, 1, 3, 0, (1, 2)),
        (9, 2, 1, 5, 2), (6, 1, 0, 1, 1), (8, 3, 0, 5, 1), (6, 1, 0, 1, 0), (9, 0, 0, 0, 0), (9, 0, 0, 7, 2),
        (6, 3, 1, 1, 2), (6, 3, 1, 1, 1), (4, 2, 1, 0, 0, (1, 2)), (8, 2, 1, 4, 1), (9, 0, 0, 7, 0), (8, 3, 0, 3, 2),
        (4, 2, 0, 3, 2, (0,)), (4, 3, 0, 0, 2, (1,)), (6, 0, 1, 3, 1), (8, 2, 1, 7, 1), (6, 0, 1, 3, 0),
        (9, 3, 0, 1, 0), (9, 1, 1, 4, 2), (6, 1, 0, 6, 2), (6, 1, 0, 6, 0), (6, 1, 1, 0, 1), (8, 3, 0, 2, 2),
        (8, 3, 0, 7, 1), (8, 2, 1, 3, 0), (5, 2, 0, 0, (0, 1, 2)), (6, 2, 0, 0, 1), (6, 3, 1, 6, 2), (6, 1, 1, 0, 0),
        (9, 1, 0, 1, 1), (9, 1, 0, 1, 0), (9, 3, 1, 1, 2), (6, 1, 1, 2, 1), (6, 0, 1, 4, 2), (6, 0, 1, 4, 0),
        (9, 3, 1, 1, 1), (8, 2, 1, 0, 0), (8, 2, 0, 3, 2), (6, 3, 0, 3, 1), (6, 1, 1, 7, 2), (6, 1, 1, 7, 0),
        (7, 2, 0, 0), (8, 3, 0, 0, 2), (9, 0, 1, 3, 1), (9, 0, 1, 3, 0), (6, 2, 0, 3, 1), (6, 2, 0, 7, 0),
        (9, 1, 1, 0, 1), (6, 1, 1, 5, 2), (7, 1, 1, 1), (9, 1, 0, 6, 2), (9, 1, 0, 6, 0), (6, 3, 0, 0, 1),
        (6, 2, 0, 3, 0), (9, 2, 0, 0, 1), (6, 3, 0, 4, 2), (9, 3, 1, 6, 2), (9, 1, 1, 0, 0), (6, 3, 1, 2, 1),
        (6, 3, 0, 4, 0), (7, 0, 0, 0), (9, 1, 1, 2, 1), (9, 0, 1, 4, 2), (9, 0, 1, 4, 0), (6, 2, 0, 4, 2),
        (7, 2, 0, 1), (6, 2, 1, 7, 1), (6, 2, 1, 7, 2), (6, 3, 1, 2, 0), (7, 0, 1, 0), (9, 3, 0, 3, 1),
        (9, 1, 1, 7, 2), (9, 1, 1, 7, 0), (6, 0, 0, 2, 1), (6, 1, 1, 5, 0), (6, 3, 0, 7, 2), (7, 1, 0, 0),
        (9, 2, 0, 3, 1), (9, 2, 0, 7, 0), (9, 1, 1, 5, 2), (6, 0, 1, 2, 1), (6, 3, 0, 7, 0), (6, 3, 1, 5, 2),
        (7, 1, 1, 0), (9, 3, 0, 0, 1), (9, 2, 0, 3, 0), (9, 3, 0, 4, 2), (7, 2, 1, 0), (6, 2, 1, 0, 2),
        (6, 2, 1, 3, 1), (6, 3, 1, 6, 0), (7, 3, 0, 0), (9, 3, 1, 2, 1), (9, 3, 0, 4, 0), (9, 2, 0, 4, 2),
        (7, 0, 0, 1), (6, 3, 0, 2, 1), (6, 0, 0, 5, 2), (7, 1, 0, 1), (9, 2, 1, 7, 1), (9, 3, 1, 2, 0), (7, 0, 1, 1),
        (9, 2, 1, 7, 2), (6, 3, 1, 4, 1), (7, 3, 1, 1), (6, 0, 1, 5, 2), (9, 0, 0, 2, 1), (7, 2, 1, 1),
        (9, 1, 1, 5, 0), (9, 3, 0, 7, 2), (9, 0, 1, 2, 1), (7, 3, 0, 1), (9, 3, 0, 7, 0), (9, 3, 1, 5, 2),
        (9, 2, 1, 3, 1), (7, 3, 1, 0), (9, 2, 1, 0, 2), (9, 3, 1, 6, 0), (9, 3, 0, 2, 1), (9, 0, 0, 5, 2),
        (9, 3, 1, 4, 1), (9, 0, 1, 5, 2),
    ),
)


def grid_kernel(
    plan, h_ref, m_ref, r_ref, out_ref,
    hist, hist_hi, hist_lo, m_wide, m_tall, r_buf, part, landed, rows, acc, acc_other,
    local_sem, pair_send, pair_recv, m_local, m_send, m_recv, rs_send, rs_recv, ag_send, ag_recv,
):
    groups, pieces, orders = plan
    count = len(groups)
    me = lax.axis_index("rows")
    core, y, z = me % 2, (me // 2) % 2, me // 4
    side = z // 2
    middle = (z + side) % 2
    inner, outer = z + 1 - 2 * side, z - 1 + 2 * side

    def device(at_z, at_y, at_core):
        return (at_z * 2 + at_y) * 2 + at_core

    partner = device(z, y, 1 - core)
    across, diagonal = device(z, 1 - y, core), device(z, 1 - y, 1 - core)
    target = (across, device(inner, y, core), device(outer, y, core))
    heading = (0, 1 + side, 2 - side)
    came = (0, 2 - side, 1 + side)

    modes, outs = h_ref.shape[0], r_ref.shape[0]
    half = m_ref.shape[1] // 2
    span = half // (2 * count)
    piece = span // pieces

    wide = [q for q in range(count) if groups[q] == ALONG_FIRST]
    tall = [q for q in range(count) if groups[q] == ACROSS_FIRST]

    def line(dy):
        return 1 - y if dy else y

    def place(j):
        return j + side * (pieces - 1 - 2 * j)

    def slot(q, dy):
        if groups[q] == ALONG_FIRST:
            return 2 * wide.index(q) + line(dy)
        return 2 * len(wide) + tall.index(q)

    def span_of(j):
        return pl.ds(pl.multiple_of(place(j) * piece, piece), piece)

    def remote(src, dst, send, recv, to):
        return pltpu.make_async_remote_copy(
            src_ref=src, dst_ref=dst, send_sem=send, recv_sem=recv,
            device_id={"rows": to}, device_id_type=MESH,
        )

    def shapes(q, at_core, at_y):
        if groups[q] == ALONG_FIRST:
            return m_ref.at[:, pl.ds(pl.multiple_of(at_core * half + 2 * q * span, 128), 2 * span)]
        return m_ref.at[:, pl.ds(pl.multiple_of(at_core * half + (2 * q + at_y) * span, 128), span)]

    def held(q, source):
        source = pl.ds(source * modes, modes)
        if groups[q] == ALONG_FIRST:
            return m_wide.at[wide.index(q), source]
        return m_tall.at[tall.index(q), source]

    def own_m(q):
        return pltpu.make_async_copy(shapes(q, core, y), held(q, 0), m_local.at[q])

    def m_pair(q):
        return remote(shapes(q, 1 - core, y), held(q, 1), m_send.at[q, 0, 0], m_recv.at[q, 0, 0], partner)

    def halved(h):
        return pl.ds(pl.multiple_of((h + side * (1 - 2 * h)) * (span // 2), 128), span // 2)

    def m_across(q, h):
        start = (h + side * (1 - 2 * h)) * (span // 2)
        return tuple(
            remote(
                m_ref.at[:, pl.ds(pl.multiple_of(at_core * half + (2 * q + 1 - y) * span + start, 128), span // 2)],
                m_tall.at[tall.index(q), pl.ds(source * modes, modes), halved(h)],
                m_send.at[q, h, source - 1], m_recv.at[q, h, source - 1], to,
            )
            for source, to, at_core in ((2, across, core), (3, diagonal, 1 - core))
        )

    own_h = pltpu.make_async_copy(h_ref, hist.at[pl.ds(0, modes)], local_sem.at[0])
    h_pair = remote(h_ref, hist.at[pl.ds(modes, modes)], pair_send.at[0], pair_recv.at[0], partner)
    h_across = remote(h_ref, hist.at[pl.ds(2 * modes, modes)], pair_send.at[1], pair_recv.at[1], across)
    h_relay = remote(
        hist.at[pl.ds(2 * modes, modes)], hist.at[pl.ds(3 * modes, modes)],
        pair_send.at[2], pair_recv.at[2], partner,
    )
    own_r = pltpu.make_async_copy(
        r_ref.at[:, pl.ds(pl.multiple_of(core * half, 128), half)],
        r_buf.at[pl.ds(0, outs)], local_sem.at[1],
    )
    r_copy = remote(
        r_ref.at[:, pl.ds(pl.multiple_of((1 - core) * half, 128), half)],
        r_buf.at[pl.ds(outs, outs)], pair_send.at[3], pair_recv.at[3], partner,
    )
    acc_copy = remote(acc.at[pl.ds(outs, outs)], acc_other, pair_send.at[4], pair_recv.at[4], partner)

    def rs_copy(q, dy, j, to, d):
        k = slot(q, dy)
        return remote(
            part.at[k, span_of(j)], landed.at[k, d, span_of(j)],
            rs_send.at[k, place(j), d], rs_recv.at[k, place(j), d], target[to],
        )

    def ag_copy(q, dy, j, to):
        k = 2 * q + line(dy)
        view = rows.at[k, span_of(j)]
        return remote(
            view, view, ag_send.at[k, place(j), heading[to]], ag_recv.at[k, place(j)], target[to]
        )

    def hist_ready(first, size):
        here = pl.ds(first * modes, size * modes)
        hist_hi[here], hist_lo[here] = split(hist[here])

    def run(order):
        seen = set()

        def once(key):
            fresh = key not in seen
            seen.add(key)
            return fresh

        def row_ready(q, dy, j):
            if once((ROOT, q, dy, j)):
                ag_copy(q, dy, j, ACROSS).wait_recv()

        def summed(q, dy, j, kids):
            total = part[slot(q, dy), span_of(j)]
            for kid in kids:
                rs_copy(q, dy, j, ACROSS, came[kid]).wait_recv()
            for kid in kids:
                total = total + landed[slot(q, dy), came[kid], span_of(j)]
            return total

        recoveries = [op for op in order if op[0] == RECOVER]
        for op in order:
            name, args = op[0], op[1:]
            if name == H_ACROSS:
                h_across.start()
            elif name == H_RELAY:
                h_across.wait_recv()
                h_relay.start()
                own_r.start()
                r_copy.start()
            elif name == SHARE:
                for copy in m_across(*args):
                    copy.start()
            elif name == PARTIAL:
                q, dy, h = args
                if once(PARTIAL):
                    own_h.wait()
                    h_pair.wait_recv()
                    hist_ready(0, 2)
                if once((PARTIAL, q)):
                    own_m(q).wait()
                    m_pair(q).wait_recv()
                if groups[q] == ALONG_FIRST:
                    buf, known = m_wide.at[wide.index(q)], pl.ds(0, 2 * modes)
                    start = line(dy) * span + (h + side * (1 - 2 * h)) * (span // 2)
                    cols = pl.ds(pl.multiple_of(start, 128), span // 2)
                else:
                    if once(SHARE):
                        h_relay.wait_recv()
                        hist_ready(2, 2)
                    for copy in m_across(q, h):
                        copy.wait_recv()
                    buf, known, cols = m_tall.at[tall.index(q)], pl.ds(0, 4 * modes), halved(h)
                part[slot(q, dy), halved(h)] = dot3(
                    split(buf[:, cols]), (hist_hi[known], hist_lo[known]), ((0,), (0,))
                )
            elif name == REDUCE:
                q, dy, j, to, kids = args
                if kids:
                    part[slot(q, dy), span_of(j)] = summed(q, dy, j, kids)
                rs_copy(q, dy, j, to, heading[to]).start()
            elif name == ROOT:
                q, dy, j, kids = args
                seen.add((ROOT, q, dy, j))
                rows[2 * q + line(dy), span_of(j)] = summed(q, dy, j, kids)
            elif name == GATHER:
                row_ready(*args[:3])
                ag_copy(*args).start()
            elif name == REDUCED:
                rs_copy(*args, heading[args[-1]]).wait_send()
            elif name == GATHERED:
                ag_copy(*args).wait_send()
            elif name == RECOVER:
                q, dy, h = args
                for j in range(h * pieces // 2, (h + 1) * pieces // 2):
                    row_ready(q, dy, j)
                if once(RECOVER):
                    own_r.wait()
                    r_copy.wait_recv()
                start = (2 * q + line(dy)) * span + (h + side * (1 - 2 * h)) * (span // 2)
                cols = pl.ds(pl.multiple_of(start, 128), span // 2)
                values = split(rows[2 * q + line(dy), halved(h)])
                for base in (outs, 0):
                    here = pl.ds(base, outs)
                    added = dot3(split(r_buf[here, cols]), values, ((1,), (0,)))
                    acc[here] = added if op is recoveries[0] else acc[here] + added
                    if op is recoveries[-1] and base:
                        acc_copy.start()

    own_h.start()
    for q in wide + tall:
        own_m(q).start()
    barrier = pltpu.get_barrier_semaphore()
    for other in (partner, across, diagonal, target[INWARD]):
        pl.semaphore_signal(barrier, inc=1, device_id={"rows": other}, device_id_type=MESH)

    @pl.when(middle == 1)
    def _():
        pl.semaphore_signal(barrier, inc=1, device_id={"rows": target[OUTWARD]}, device_id_type=MESH)

    pl.semaphore_wait(barrier, 4 + middle)
    h_pair.start()
    for q in wide + tall:
        m_pair(q).start()

    for role in range(2):
        pl.when(middle == role)(functools.partial(run, orders[role]))

    h_pair.wait_send()
    h_across.wait_send()
    h_relay.wait_send()
    r_copy.wait_send()
    for q in range(count):
        m_pair(q).wait_send()
    for q in tall:
        for copy in m_across(q, 0) + m_across(q, 1):
            copy.wait_send()
    acc_copy.wait()
    out_ref[...] = acc[pl.ds(0, outs)] + acc_other[...]


def grid_call(plan, histories, modal_map, recovery):
    modes, time_cols = histories.shape
    outs, dofs = recovery.shape
    groups, pieces, _ = plan
    half, count = dofs // 2, len(groups)
    span = half // (2 * count)
    n_wide, n_tall = groups.count(ALONG_FIRST), groups.count(ACROSS_FIRST)
    slots = 2 * n_wide + n_tall
    f32, dma = jnp.float32, pltpu.SemaphoreType.DMA
    anywhere = pl.BlockSpec(memory_space=pltpu.HBM)
    return pl.pallas_call(
        functools.partial(grid_kernel, plan),
        out_shape=jax.ShapeDtypeStruct((outs, time_cols), f32),
        in_specs=[anywhere, anywhere, anywhere],
        out_specs=pl.BlockSpec(memory_space=pltpu.VMEM),
        scratch_shapes=[
            pltpu.VMEM((4 * modes, time_cols), f32),
            pltpu.VMEM((4 * modes, time_cols), jnp.bfloat16),
            pltpu.VMEM((4 * modes, time_cols), jnp.bfloat16),
            pltpu.VMEM((n_wide, 2 * modes, 2 * span), f32),
            pltpu.VMEM((n_tall, 4 * modes, span), f32),
            pltpu.VMEM((2 * outs, half), f32),
            pltpu.VMEM((slots, span, time_cols), f32),
            pltpu.VMEM((slots, 3, span, time_cols), f32),
            pltpu.VMEM((2 * count, span, time_cols), f32),
            pltpu.VMEM((2 * outs, time_cols), f32),
            pltpu.VMEM((outs, time_cols), f32),
            dma((2,)),
            dma((5,)),
            dma((5,)),
            dma((count,)),
            dma((count, 2, 3)),
            dma((count, 2, 3)),
            dma((slots, pieces, 3)),
            dma((slots, pieces, 3)),
            dma((2 * count, pieces, 3)),
            dma((2 * count, pieces)),
        ],
        compiler_params=pltpu.CompilerParams(
            collective_id=1, has_side_effects=True, vmem_limit_bytes=56 * 2**20
        ),
    )(histories, modal_map, recovery)


def ring_call(chips, histories, modal_map, recovery):
    modes, time_cols = histories.shape
    outs, dofs = recovery.shape
    half = dofs // 2
    block = half // chips
    ways = 2 if block % 256 == 0 else 1
    unit = block // ways
    f32, dma = jnp.float32, pltpu.SemaphoreType.DMA
    vmem, anywhere = pl.BlockSpec(memory_space=pltpu.VMEM), pl.BlockSpec(memory_space=pltpu.HBM)
    return pl.pallas_call(
        functools.partial(kernel, chips, ways),
        out_shape=jax.ShapeDtypeStruct((outs, time_cols), f32),
        in_specs=[anywhere, anywhere, anywhere],
        out_specs=vmem,
        scratch_shapes=[
            pltpu.VMEM((2 * modes, time_cols), f32),
            pltpu.VMEM((2 * modes, time_cols), jnp.bfloat16),
            pltpu.VMEM((2 * modes, time_cols), jnp.bfloat16),
            pltpu.VMEM((2 * modes, half), f32),
            pltpu.VMEM((2 * outs, half), f32),
            pltpu.VMEM((ways, chips - 1, unit, time_cols), f32),
            pltpu.VMEM((ways, chips - 1, unit, time_cols), f32),
            pltpu.VMEM((chips, ways, unit, time_cols), f32),
            pltpu.VMEM((2 * outs, time_cols), f32),
            pltpu.VMEM((outs, time_cols), f32),
            dma((2,)),
            dma((3,)),
            dma((3,)),
            dma((ways, chips)),
            dma((ways, chips)),
            dma((ways, chips)),
            dma((ways, chips - 1, SUBS)),
            dma((ways, chips - 1, SUBS)),
            dma((ways, chips - 1, SUBS)),
            dma((ways, chips - 1, SUBS)),
        ],
        compiler_params=pltpu.CompilerParams(
            collective_id=0, has_side_effects=True, vmem_limit_bytes=50 * 2**20
        ),
    )(histories, modal_map, recovery)


def shards(size, histories, modal_map, recovery):
    chips = size // 2
    time_cols, outs = histories.shape[1], recovery.shape[0]
    f32, vmem = jnp.float32, pl.BlockSpec(memory_space=pltpu.VMEM)
    if chips == 8:
        found = grid_call((GROUPS, PIECES, ORDERS), histories, modal_map, recovery)
    else:
        found = ring_call(chips, histories, modal_map, recovery)
    return pl.pallas_call(
        statistics,
        out_shape=(
            jax.ShapeDtypeStruct((outs, time_cols), f32),
            jax.ShapeDtypeStruct((CASES, outs), f32),
            jax.ShapeDtypeStruct((CASES, outs), f32),
        ),
        in_specs=[vmem], compiler_params=pltpu.CompilerParams(vmem_limit_bytes=8 * 2**20),
        out_specs=(vmem, vmem, vmem),
    )(found)


def solution(mesh):
    return jax.shard_map(
        functools.partial(shards, mesh.shape["rows"]),
        mesh=mesh,
        in_specs=(P(("grp", "rows"), None), P(("grp", "rows"), None), P(("grp", "rows"), None)),
        out_specs=(P(("grp", "rows"), None), P(None, ("grp", "rows")), P(None, ("grp", "rows"))),
        check_vma=False,
    )
```

```python
import functools

import jax
import jax.numpy as jnp
from jax import lax
from jax.experimental import pallas as pl
from jax.experimental.pallas import tpu as pltpu
from jax.sharding import PartitionSpec as P

CASES = 4
SUBS = 2
epsilon = 1e-06
MESH = pl.DeviceIdType.MESH


def split(x):
    high = x.astype(jnp.bfloat16)
    return high, (x - high.astype(jnp.float32)).astype(jnp.bfloat16)


def dot3(a, b, dims):
    mul = functools.partial(
        lax.dot_general, dimension_numbers=(dims, ((), ())), preferred_element_type=jnp.float32
    )
    return mul(a[0], b[0]) + (mul(a[0], b[1]) + mul(a[1], b[0]))


def ring_position(chips, chip):
    if chips == 8:
        z, y = chip // 2, chip % 2
        return y * (chips - 1 - 2 * z) + z
    return chip


def chip_at(chips, position):
    if chips == 8:
        y = position // 4
        return (y * (chips - 1 - 2 * position) + position) * 2 + y
    return position


def kernel(
    chips, ways, h_ref, m_ref, r_ref, out_ref,
    hist, hist_hi, hist_lo, m_buf, r_buf, part, landed, rows, acc, acc_other,
    local_sem, pair_send, pair_recv, m_local, m_send, m_recv, rs_send, rs_recv, ag_send, ag_recv,
):
    me = lax.axis_index("rows")
    core = me % 2
    partner = me + 1 - 2 * core
    pos = ring_position(chips, me // 2)
    after = chip_at(chips, (pos + 1) % chips) * 2 + core
    before = chip_at(chips, (pos + chips - 1) % chips) * 2 + core
    targets = (after, before)
    signs = (1, -1)

    modes, outs = h_ref.shape[0], r_ref.shape[0]
    half = m_ref.shape[1] // 2
    block = half // chips
    unit = block // ways
    piece = unit // SUBS
    cuts = SUBS if piece % 128 == 0 else 1
    width = unit // cuts

    def at(p):
        return (p + 2 * chips) % chips

    def cols(base, b, d, start=0, size=unit):
        return pl.ds(pl.multiple_of(base + b * block + d * unit + start, 128), size)

    def remote(src, dst, send, recv, to):
        return pltpu.make_async_remote_copy(
            src_ref=src, dst_ref=dst, send_sem=send, recv_sem=recv,
            device_id={"rows": to}, device_id_type=MESH,
        )

    def sum_block(k, d):
        return at(pos - signs[d] * (k + 1))

    def m_copy(k, d):
        b = sum_block(k, d)
        return remote(
            m_ref.at[:, cols((1 - core) * half, b, d)],
            m_buf.at[pl.ds(modes, modes), cols(0, b, d)],
            m_send.at[d, k], m_recv.at[d, k], partner,
        )

    def own_m(k, d):
        b = sum_block(k, d)
        return pltpu.make_async_copy(
            m_ref.at[:, cols(core * half, b, d)],
            m_buf.at[pl.ds(0, modes), cols(0, b, d)], m_local.at[d, k],
        )

    def rs_copy(k, d, j):
        view = (d, k, pl.ds(j * piece, piece))
        return remote(part.at[view], landed.at[view], rs_send.at[d, k, j], rs_recv.at[d, k, j], targets[d])

    def ag_copy(s, d, j, arrives=False):
        b = at(pos - signs[d] * (s + 1 if arrives else s))
        view = (b, d, pl.ds(j * piece, piece))
        return remote(rows.at[view], rows.at[view], ag_send.at[d, s, j], ag_recv.at[d, s, j], targets[d])

    own_h = pltpu.make_async_copy(h_ref, hist.at[pl.ds(0, modes)], local_sem.at[0])
    own_r = pltpu.make_async_copy(
        r_ref.at[:, pl.ds(pl.multiple_of(core * half, 128), half)],
        r_buf.at[pl.ds(0, outs)], local_sem.at[1],
    )
    h_copy = remote(h_ref, hist.at[pl.ds(modes, modes)], pair_send.at[0], pair_recv.at[0], partner)
    r_copy = remote(
        r_ref.at[:, pl.ds(pl.multiple_of((1 - core) * half, 128), half)],
        r_buf.at[pl.ds(outs, outs)], pair_send.at[1], pair_recv.at[1], partner,
    )
    acc_copy = remote(acc.at[pl.ds(outs, outs)], acc_other, pair_send.at[2], pair_recv.at[2], partner)

    own_h.start()
    for d in range(ways):
        own_m(0, d).start()
    barrier = pltpu.get_barrier_semaphore()
    for other in (after, before, partner):
        pl.semaphore_signal(barrier, inc=1, device_id={"rows": other}, device_id_type=MESH)
    pl.semaphore_wait(barrier, 3)

    h_copy.start()
    for d in range(ways):
        m_copy(0, d).start()

    @pl.loop(1, chips)
    def _(k):
        for d in range(ways):
            own_m(k, d).start()
            m_copy(k, d).start()

    own_h.wait()
    hist_hi[pl.ds(0, modes)], hist_lo[pl.ds(0, modes)] = split(hist[pl.ds(0, modes)])
    h_copy.wait_recv()
    hist_hi[pl.ds(modes, modes)], hist_lo[pl.ds(modes, modes)] = split(hist[pl.ds(modes, modes)])

    def shapes_here(k, d):
        own_m(k, d).wait()
        m_copy(k, d).wait_recv()

    def partial_rows(k, d, start=0, size=unit):
        shapes = split(m_buf[:, cols(0, sum_block(k, d), d, start, size)])
        return dot3(shapes, (hist_hi[...], hist_lo[...]), ((0,), (0,)))

    for cut in range(cuts):
        for d in range(ways):
            if cut == 0:
                shapes_here(0, d)
            start = cut * width
            part[d, 0, pl.ds(start, width)] = partial_rows(0, d, start, width)
            for j in range(cut * SUBS // cuts, (cut + 1) * SUBS // cuts):
                rs_copy(0, d, j).start()

    own_r.start()
    r_copy.start()

    @pl.loop(1, chips - 1)
    def _(k):
        for d in range(ways):
            shapes_here(k, d)
            part[d, k] = partial_rows(k, d)
        for j in range(SUBS):
            for d in range(ways):
                rs_copy(k - 1, d, j).wait_recv()
                view = (d, k, pl.ds(j * piece, piece))
                part[view] = part[view] + landed[d, k - 1, pl.ds(j * piece, piece)]
                rs_copy(k, d, j).start()

    last = chips - 1
    for d in range(ways):
        shapes_here(last, d)
        rows[pos, d] = partial_rows(last, d)
    for j in range(SUBS):
        for d in range(ways):
            rs_copy(last - 1, d, j).wait_recv()
            view = (pos, d, pl.ds(j * piece, piece))
            rows[view] = rows[view] + landed[d, last - 1, pl.ds(j * piece, piece)]
            ag_copy(0, d, j).start()

    own_r.wait()
    r_copy.wait_recv()

    def recovered(b, d):
        return dot3(split(r_buf[:, cols(0, b, d)]), split(rows[b, d]), ((1,), (0,)))

    acc[...] = recovered(pos, 0)
    for d in range(1, ways):
        acc[...] += recovered(pos, d)

    @pl.loop(0, chips - 2)
    def _(s):
        for j in range(SUBS):
            for d in range(ways):
                ag_copy(s, d, j, arrives=True).wait_recv()
                ag_copy(s + 1, d, j).start()
        for d in range(ways):
            acc[...] += recovered(at(pos - signs[d] * (s + 1)), d)

    for cut in range(cuts):
        for d in range(ways):
            for j in range(cut * SUBS // cuts, (cut + 1) * SUBS // cuts):
                ag_copy(chips - 2, d, j, arrives=True).wait_recv()
            b, start = at(pos - signs[d] * (chips - 1)), cut * width
            weights = split(r_buf[:, cols(0, b, d, start, width)])
            finished = split(rows[b, d, pl.ds(start, width)])
            final = cut == cuts - 1 and d == ways - 1
            for base in (outs, 0):
                own = tuple(w[base : base + outs] for w in weights)
                acc[pl.ds(base, outs)] += dot3(own, finished, ((1,), (0,)))
                if final and base:
                    acc_copy.start()

    h_copy.wait_send()
    r_copy.wait_send()

    @pl.loop(0, chips)
    def _(k):
        for d in range(ways):
            m_copy(k, d).wait_send()

    @pl.loop(0, chips - 1)
    def _(k):
        for d in range(ways):
            for j in range(SUBS):
                rs_copy(k, d, j).wait_send()
                ag_copy(k, d, j).wait_send()

    acc_copy.wait()
    out_ref[...] = acc[pl.ds(0, outs)] + acc_other[...]


def statistics(found_ref, out_ref, peak_ref, rms_ref):
    responses = found_ref[...]
    out_ref[...] = responses
    by_time = responses.T
    steps = by_time.shape[0] // CASES
    for k in range(CASES):
        case = by_time[k * steps : (k + 1) * steps]
        peak_ref[k : k + 1] = jnp.max(jnp.abs(case), axis=0, keepdims=True)
        mean = jnp.sum(case * case, axis=0, keepdims=True) / steps
        rms_ref[k : k + 1] = jnp.sqrt(mean + epsilon)


ACROSS, INWARD, OUTWARD = range(3)
H_ACROSS, H_RELAY, SHARE, PARTIAL, REDUCE, ROOT, GATHER, RECOVER, REDUCED, GATHERED = range(10)
ALONG_FIRST, ACROSS_FIRST = range(2)
GROUPS = (ACROSS_FIRST, ACROSS_FIRST, ALONG_FIRST, ACROSS_FIRST)
PIECES = 8
ORDERS = (
    (
        (0,), (3, 2, 1, 1), (4, 2, 1, 6, 1, ()), (3, 2, 1, 0), (4, 2, 1, 1, 1, ()), (3, 2, 0, 1), (4, 2, 1, 5, 0, ()),
        (3, 2, 0, 0), (4, 2, 0, 6, 1, ()), (4, 2, 1, 2, 0, ()), (1,), (4, 2, 0, 1, 1, ()), (2, 0, 1),
        (4, 2, 0, 5, 1, (0,)), (8, 2, 1, 6, 1), (4, 2, 0, 2, 1, (0,)), (8, 2, 1, 1, 1), (8, 2, 1, 5, 0), (2, 0, 0),
        (4, 2, 1, 3, 1, ()), (8, 2, 0, 6, 1), (8, 2, 1, 2, 0), (4, 2, 0, 0, 1, ()), (3, 0, 0, 1), (8, 2, 0, 1, 1),
        (4, 0, 0, 6, 1, ()), (2, 1, 1), (8, 2, 0, 5, 1), (4, 0, 0, 4, 1, ()), (8, 2, 0, 2, 1), (4, 0, 0, 5, 1, ()),
        (3, 0, 0, 0), (8, 2, 1, 3, 1), (4, 0, 0, 1, 1, ()), (2, 1, 0), (8, 2, 0, 0, 1), (4, 0, 0, 7, 1, ()),
        (8, 0, 0, 6, 1), (3, 1, 0, 1), (4, 1, 0, 4, 1, ()), (8, 0, 0, 4, 1), (6, 2, 0, 6, 0), (4, 1, 0, 5, 1, ()),
        (8, 0, 0, 5, 1), (2, 3, 1), (4, 1, 0, 6, 1, ()), (3, 1, 0, 0), (8, 0, 0, 1, 1), (4, 1, 0, 3, 1, ()),
        (8, 0, 0, 7, 1), (5, 0, 0, 3, (1,)), (4, 1, 0, 7, 1, ()), (6, 0, 0, 3, 0), (8, 1, 0, 4, 1),
        (5, 0, 0, 2, (1,)), (4, 2, 0, 4, 1, ()), (9, 2, 0, 6, 0), (6, 0, 0, 2, 0), (8, 1, 0, 5, 1),
        (4, 2, 1, 4, 1, ()), (3, 3, 0, 1), (2, 3, 0), (8, 1, 0, 6, 1), (5, 0, 0, 0, (1,)), (7, 0, 0, 0),
        (6, 0, 0, 0, 1), (8, 1, 0, 3, 1), (4, 3, 0, 6, 1, ()), (8, 1, 0, 7, 1), (4, 3, 0, 4, 1, ()), (9, 0, 0, 3, 0),
        (4, 2, 0, 7, 0, ()), (8, 2, 0, 4, 1), (5, 1, 0, 2, (1,)), (4, 3, 0, 5, 1, ()), (9, 0, 0, 2, 0),
        (6, 1, 0, 2, 0), (8, 2, 1, 4, 1), (3, 3, 0, 0), (5, 1, 0, 1, (1,)), (4, 3, 0, 1, 1, ()), (6, 1, 0, 1, 0),
        (9, 0, 0, 0, 1), (4, 2, 1, 7, 1, (0,)), (6, 0, 0, 6, 0), (8, 3, 0, 6, 1), (5, 1, 0, 0, (1,)), (7, 1, 0, 0),
        (4, 3, 0, 7, 1, ()), (6, 1, 0, 0, 0), (8, 3, 0, 4, 1), (8, 2, 0, 7, 0), (6, 1, 0, 1, 1), (6, 0, 0, 0, 0),
        (8, 3, 0, 5, 1), (9, 1, 0, 2, 0), (4, 2, 1, 0, 1, ()), (6, 0, 0, 7, 0), (8, 3, 0, 1, 1), (9, 1, 0, 1, 0),
        (5, 3, 0, 3, (1,)), (6, 0, 1, 3, 1), (6, 3, 0, 3, 0), (8, 2, 1, 7, 1), (9, 0, 0, 6, 0), (7, 0, 1, 0),
        (6, 1, 1, 0, 1), (6, 1, 0, 3, 0), (8, 3, 0, 7, 1), (9, 1, 0, 0, 0), (5, 3, 0, 2, (1,)), (6, 1, 1, 2, 1),
        (6, 3, 0, 2, 0), (9, 1, 0, 1, 1), (9, 0, 0, 0, 0), (6, 3, 0, 3, 1), (6, 3, 1, 1, 0), (8, 2, 1, 0, 1),
        (9, 0, 0, 7, 0), (7, 1, 1, 0), (5, 2, 0, 3, (1,)), (6, 2, 0, 3, 1), (6, 2, 0, 3, 0), (9, 0, 1, 3, 1),
        (9, 3, 0, 3, 0), (5, 3, 0, 0, (1,)), (6, 3, 0, 0, 1), (6, 3, 0, 0, 0), (9, 1, 1, 0, 1), (9, 1, 0, 3, 0),
        (7, 3, 0, 0), (6, 3, 1, 2, 1), (6, 1, 0, 6, 0), (9, 1, 1, 2, 1), (9, 3, 0, 2, 0), (6, 0, 0, 2, 1),
        (6, 3, 1, 6, 0), (9, 3, 0, 3, 1), (9, 3, 1, 1, 0), (7, 3, 1, 0), (6, 0, 1, 2, 1), (6, 0, 1, 4, 0),
        (9, 2, 0, 3, 1), (9, 2, 0, 3, 0), (6, 1, 0, 2, 1), (6, 1, 1, 7, 0), (9, 3, 0, 0, 1), (9, 3, 0, 0, 0),
        (7, 1, 1, 1), (6, 1, 1, 3, 1), (6, 1, 1, 5, 0), (9, 3, 1, 2, 1), (9, 1, 0, 6, 0), (6, 3, 1, 0, 1),
        (6, 3, 0, 4, 0), (9, 0, 0, 2, 1), (9, 3, 1, 6, 0), (6, 2, 0, 4, 0), (9, 0, 1, 2, 1), (9, 0, 1, 4, 0),
        (7, 1, 0, 1), (6, 2, 1, 7, 0), (9, 1, 0, 2, 1), (9, 1, 1, 7, 0), (6, 3, 0, 7, 0), (9, 1, 1, 3, 1),
        (9, 1, 1, 5, 0), (7, 2, 1, 1), (6, 3, 1, 5, 0), (9, 3, 1, 0, 1), (9, 3, 0, 4, 0), (7, 2, 0, 1), (7, 2, 1, 0),
        (6, 2, 1, 0, 0), (9, 2, 0, 4, 0), (7, 3, 1, 1), (7, 0, 0, 1), (9, 2, 1, 7, 0), (7, 3, 0, 1), (7, 0, 1, 1),
        (9, 3, 0, 7, 0), (7, 2, 0, 0), (9, 3, 1, 5, 0), (9, 2, 1, 0, 0),
    ),
    (
        (0,), (3, 2, 1, 1), (4, 2, 1, 5, 1, ()), (3, 2, 1, 0), (3, 2, 0, 1), (4, 2, 0, 7, 1, ()), (2, 0, 1),
        (3, 2, 0, 0), (4, 2, 1, 6, 1, (2,)), (1,), (4, 2, 1, 2, 0, (1,)), (8, 2, 1, 5, 1), (4, 2, 0, 6, 1, (2,)),
        (4, 2, 1, 1, 0, (1, 2)), (3, 0, 0, 1), (8, 2, 0, 7, 1), (2, 0, 0), (8, 2, 1, 6, 1), (4, 2, 0, 5, 1, (2,)),
        (5, 2, 0, 1, (0, 1, 2)), (6, 2, 0, 1, 1), (6, 2, 0, 1, 2), (8, 2, 1, 2, 0), (6, 2, 0, 1, 0), (8, 2, 0, 6, 1),
        (5, 2, 0, 2, (0, 1, 2)), (6, 2, 0, 2, 1), (6, 2, 0, 2, 2), (8, 2, 1, 1, 0), (6, 2, 0, 2, 0), (6, 2, 0, 6, 2),
        (3, 0, 0, 0), (2, 1, 1), (8, 2, 0, 5, 1), (4, 0, 0, 6, 1, (2,)), (6, 2, 0, 5, 2), (6, 2, 1, 1, 1),
        (6, 2, 1, 1, 2), (9, 2, 0, 1, 1), (9, 2, 0, 1, 2), (4, 0, 0, 4, 1, (2,)), (6, 2, 1, 2, 2), (9, 2, 0, 1, 0),
        (9, 2, 0, 2, 1), (9, 2, 0, 2, 2), (4, 0, 0, 5, 1, (2,)), (2, 1, 0), (5, 0, 0, 1, (1, 2)), (9, 2, 0, 6, 2),
        (6, 0, 0, 1, 2), (9, 2, 0, 2, 0), (6, 0, 0, 1, 1), (8, 0, 0, 6, 1), (4, 0, 0, 3, 2, (1,)), (9, 2, 0, 5, 2),
        (3, 1, 0, 1), (4, 0, 0, 7, 1, (2,)), (9, 2, 1, 1, 1), (4, 0, 0, 2, 2, (1,)), (9, 2, 1, 1, 2), (6, 0, 0, 1, 0),
        (4, 1, 0, 4, 1, (2,)), (8, 0, 0, 4, 1), (6, 0, 0, 6, 2), (9, 2, 1, 2, 2), (6, 0, 0, 6, 0),
        (4, 1, 0, 5, 1, (2,)), (3, 1, 0, 0), (8, 0, 0, 5, 1), (9, 0, 0, 1, 2), (4, 0, 0, 0, 2, (1,)), (2, 3, 1),
        (4, 1, 0, 6, 1, (2,)), (6, 0, 1, 1, 2), (9, 0, 0, 1, 1), (5, 1, 0, 3, (1, 2)), (8, 0, 0, 3, 2),
        (6, 1, 0, 3, 1), (6, 1, 0, 3, 2), (8, 0, 0, 7, 1), (8, 0, 0, 2, 2), (4, 1, 0, 7, 1, (2,)),
        (4, 1, 0, 2, 2, (1,)), (9, 0, 0, 1, 0), (2, 3, 0), (8, 1, 0, 4, 1), (9, 0, 0, 6, 2), (6, 2, 1, 2, 1),
        (4, 1, 0, 1, 2, (1,)), (9, 0, 0, 6, 0), (8, 1, 0, 5, 1), (8, 0, 0, 0, 2), (3, 3, 0, 1), (6, 1, 0, 4, 2),
        (6, 0, 0, 0, 1), (8, 1, 0, 6, 1), (9, 0, 1, 1, 2), (4, 2, 0, 4, 0, (2,)), (4, 1, 0, 0, 2, (1,)),
        (4, 3, 0, 6, 1, (2,)), (9, 1, 0, 3, 1), (9, 1, 0, 3, 2), (6, 1, 0, 4, 0), (6, 2, 1, 5, 2),
        (4, 3, 0, 4, 1, (2,)), (8, 1, 0, 7, 1), (8, 1, 0, 2, 2), (3, 3, 0, 0), (6, 0, 0, 0, 0), (6, 0, 0, 7, 2),
        (4, 3, 0, 5, 1, (2,)), (9, 2, 1, 2, 1), (8, 1, 0, 1, 2), (4, 2, 1, 4, 1, (0, 2)), (6, 0, 0, 7, 0),
        (5, 3, 0, 1, (1, 2)), (9, 0, 0, 0, 1), (4, 3, 0, 3, 2, (1,)), (9, 1, 0, 4, 2), (6, 3, 0, 1, 0),
        (6, 1, 1, 4, 2), (4, 2, 1, 7, 1, (2,)), (8, 2, 0, 4, 0), (8, 1, 0, 0, 2), (8, 3, 0, 6, 1),
        (4, 3, 0, 2, 2, (1,)), (4, 3, 0, 7, 1, (2,)), (9, 1, 0, 4, 0), (8, 3, 0, 4, 1), (4, 2, 1, 3, 0, (1, 2)),
        (9, 2, 1, 5, 2), (6, 1, 0, 1, 1), (8, 3, 0, 5, 1), (6, 1, 0, 1, 0), (9, 0, 0, 0, 0), (9, 0, 0, 7, 2),
        (6, 3, 1, 1, 2), (6, 3, 1, 1, 1), (4, 2, 1, 0, 0, (1, 2)), (8, 2, 1, 4, 1), (9, 0, 0, 7, 0), (8, 3, 0, 3, 2),
        (4, 2, 0, 3, 2, (0,)), (4, 3, 0, 0, 2, (1,)), (6, 0, 1, 3, 1), (8, 2, 1, 7, 1), (6, 0, 1, 3, 0),
        (9, 3, 0, 1, 0), (9, 1, 1, 4, 2), (6, 1, 0, 6, 2), (6, 1, 0, 6, 0), (6, 1, 1, 0, 1), (8, 3, 0, 2, 2),
        (8, 3, 0, 7, 1), (8, 2, 1, 3, 0), (5, 2, 0, 0, (0, 1, 2)), (6, 2, 0, 0, 1), (6, 3, 1, 6, 2), (6, 1, 1, 0, 0),
        (9, 1, 0, 1, 1), (9, 1, 0, 1, 0), (9, 3, 1, 1, 2), (6, 1, 1, 2, 1), (6, 0, 1, 4, 2), (6, 0, 1, 4, 0),
        (9, 3, 1, 1, 1), (8, 2, 1, 0, 0), (8, 2, 0, 3, 2), (6, 3, 0, 3, 1), (6, 1, 1, 7, 2), (6, 1, 1, 7, 0),
        (7, 2, 0, 0), (8, 3, 0, 0, 2), (9, 0, 1, 3, 1), (9, 0, 1, 3, 0), (6, 2, 0, 3, 1), (6, 2, 0, 7, 0),
        (9, 1, 1, 0, 1), (6, 1, 1, 5, 2), (7, 1, 1, 1), (9, 1, 0, 6, 2), (9, 1, 0, 6, 0), (6, 3, 0, 0, 1),
        (6, 2, 0, 3, 0), (9, 2, 0, 0, 1), (6, 3, 0, 4, 2), (9, 3, 1, 6, 2), (9, 1, 1, 0, 0), (6, 3, 1, 2, 1),
        (6, 3, 0, 4, 0), (7, 0, 0, 0), (9, 1, 1, 2, 1), (9, 0, 1, 4, 2), (9, 0, 1, 4, 0), (6, 2, 0, 4, 2),
        (7, 2, 0, 1), (6, 2, 1, 7, 1), (6, 2, 1, 7, 2), (6, 3, 1, 2, 0), (7, 0, 1, 0), (9, 3, 0, 3, 1),
        (9, 1, 1, 7, 2), (9, 1, 1, 7, 0), (6, 0, 0, 2, 1), (6, 1, 1, 5, 0), (6, 3, 0, 7, 2), (7, 1, 0, 0),
        (9, 2, 0, 3, 1), (9, 2, 0, 7, 0), (9, 1, 1, 5, 2), (6, 0, 1, 2, 1), (6, 3, 0, 7, 0), (6, 3, 1, 5, 2),
        (7, 1, 1, 0), (9, 3, 0, 0, 1), (9, 2, 0, 3, 0), (9, 3, 0, 4, 2), (7, 2, 1, 0), (6, 2, 1, 0, 2),
        (6, 2, 1, 3, 1), (6, 3, 1, 6, 0), (7, 3, 0, 0), (9, 3, 1, 2, 1), (9, 3, 0, 4, 0), (9, 2, 0, 4, 2),
        (7, 0, 0, 1), (6, 3, 0, 2, 1), (6, 0, 0, 5, 2), (7, 1, 0, 1), (9, 2, 1, 7, 1), (9, 3, 1, 2, 0), (7, 0, 1, 1),
        (9, 2, 1, 7, 2), (6, 3, 1, 4, 1), (7, 3, 1, 1), (6, 0, 1, 5, 2), (9, 0, 0, 2, 1), (7, 2, 1, 1),
        (9, 1, 1, 5, 0), (9, 3, 0, 7, 2), (9, 0, 1, 2, 1), (7, 3, 0, 1), (9, 3, 0, 7, 0), (9, 3, 1, 5, 2),
        (9, 2, 1, 3, 1), (7, 3, 1, 0), (9, 2, 1, 0, 2), (9, 3, 1, 6, 0), (9, 3, 0, 2, 1), (9, 0, 0, 5, 2),
        (9, 3, 1, 4, 1), (9, 0, 1, 5, 2),
    ),
)


def grid_kernel(
    plan, h_ref, m_ref, r_ref, out_ref,
    hist, hist_hi, hist_lo, m_wide, m_tall, r_buf, part, landed, rows, acc, acc_other,
    local_sem, pair_send, pair_recv, m_local, m_send, m_recv, rs_send, rs_recv, ag_send, ag_recv,
):
    groups, pieces, orders = plan
    count = len(groups)
    me = lax.axis_index("rows")
    core, y, z = me % 2, (me // 2) % 2, me // 4
    side = z // 2
    middle = (z + side) % 2
    inner, outer = z + 1 - 2 * side, z - 1 + 2 * side

    def device(at_z, at_y, at_core):
        return (at_z * 2 + at_y) * 2 + at_core

    partner = device(z, y, 1 - core)
    across, diagonal = device(z, 1 - y, core), device(z, 1 - y, 1 - core)
    target = (across, device(inner, y, core), device(outer, y, core))
    heading = (0, 1 + side, 2 - side)
    came = (0, 2 - side, 1 + side)

    modes, outs = h_ref.shape[0], r_ref.shape[0]
    half = m_ref.shape[1] // 2
    span = half // (2 * count)
    piece = span // pieces

    wide = [q for q in range(count) if groups[q] == ALONG_FIRST]
    tall = [q for q in range(count) if groups[q] == ACROSS_FIRST]

    def line(dy):
        return 1 - y if dy else y

    def place(j):
        return j + side * (pieces - 1 - 2 * j)

    def slot(q, dy):
        if groups[q] == ALONG_FIRST:
            return 2 * wide.index(q) + line(dy)
        return 2 * len(wide) + tall.index(q)

    def span_of(j):
        return pl.ds(pl.multiple_of(place(j) * piece, piece), piece)

    def remote(src, dst, send, recv, to):
        return pltpu.make_async_remote_copy(
            src_ref=src, dst_ref=dst, send_sem=send, recv_sem=recv,
            device_id={"rows": to}, device_id_type=MESH,
        )

    def shapes(q, at_core, at_y):
        if groups[q] == ALONG_FIRST:
            return m_ref.at[:, pl.ds(pl.multiple_of(at_core * half + 2 * q * span, 128), 2 * span)]
        return m_ref.at[:, pl.ds(pl.multiple_of(at_core * half + (2 * q + at_y) * span, 128), span)]

    def held(q, source):
        source = pl.ds(source * modes, modes)
        if groups[q] == ALONG_FIRST:
            return m_wide.at[wide.index(q), source]
        return m_tall.at[tall.index(q), source]

    def own_m(q):
        return pltpu.make_async_copy(shapes(q, core, y), held(q, 0), m_local.at[q])

    def m_pair(q):
        return remote(shapes(q, 1 - core, y), held(q, 1), m_send.at[q, 0, 0], m_recv.at[q, 0, 0], partner)

    def halved(h):
        return pl.ds(pl.multiple_of((h + side * (1 - 2 * h)) * (span // 2), 128), span // 2)

    def m_across(q, h):
        start = (h + side * (1 - 2 * h)) * (span // 2)
        return tuple(
            remote(
                m_ref.at[:, pl.ds(pl.multiple_of(at_core * half + (2 * q + 1 - y) * span + start, 128), span // 2)],
                m_tall.at[tall.index(q), pl.ds(source * modes, modes), halved(h)],
                m_send.at[q, h, source - 1], m_recv.at[q, h, source - 1], to,
            )
            for source, to, at_core in ((2, across, core), (3, diagonal, 1 - core))
        )

    own_h = pltpu.make_async_copy(h_ref, hist.at[pl.ds(0, modes)], local_sem.at[0])
    h_pair = remote(h_ref, hist.at[pl.ds(modes, modes)], pair_send.at[0], pair_recv.at[0], partner)
    h_across = remote(h_ref, hist.at[pl.ds(2 * modes, modes)], pair_send.at[1], pair_recv.at[1], across)
    h_relay = remote(
        hist.at[pl.ds(2 * modes, modes)], hist.at[pl.ds(3 * modes, modes)],
        pair_send.at[2], pair_recv.at[2], partner,
    )
    own_r = pltpu.make_async_copy(
        r_ref.at[:, pl.ds(pl.multiple_of(core * half, 128), half)],
        r_buf.at[pl.ds(0, outs)], local_sem.at[1],
    )
    r_copy = remote(
        r_ref.at[:, pl.ds(pl.multiple_of((1 - core) * half, 128), half)],
        r_buf.at[pl.ds(outs, outs)], pair_send.at[3], pair_recv.at[3], partner,
    )
    acc_copy = remote(acc.at[pl.ds(outs, outs)], acc_other, pair_send.at[4], pair_recv.at[4], partner)

    def rs_copy(q, dy, j, to, d):
        k = slot(q, dy)
        return remote(
            part.at[k, span_of(j)], landed.at[k, d, span_of(j)],
            rs_send.at[k, place(j), d], rs_recv.at[k, place(j), d], target[to],
        )

    def ag_copy(q, dy, j, to):
        k = 2 * q + line(dy)
        view = rows.at[k, span_of(j)]
        return remote(
            view, view, ag_send.at[k, place(j), heading[to]], ag_recv.at[k, place(j)], target[to]
        )

    def hist_ready(first, size):
        here = pl.ds(first * modes, size * modes)
        hist_hi[here], hist_lo[here] = split(hist[here])

    def run(order):
        seen = set()

        def once(key):
            fresh = key not in seen
            seen.add(key)
            return fresh

        def row_ready(q, dy, j):
            if once((ROOT, q, dy, j)):
                ag_copy(q, dy, j, ACROSS).wait_recv()

        def summed(q, dy, j, kids):
            total = part[slot(q, dy), span_of(j)]
            for kid in kids:
                rs_copy(q, dy, j, ACROSS, came[kid]).wait_recv()
            for kid in kids:
                total = total + landed[slot(q, dy), came[kid], span_of(j)]
            return total

        recoveries = [op for op in order if op[0] == RECOVER]
        for op in order:
            name, args = op[0], op[1:]
            if name == H_ACROSS:
                h_across.start()
            elif name == H_RELAY:
                h_across.wait_recv()
                h_relay.start()
                own_r.start()
                r_copy.start()
            elif name == SHARE:
                for copy in m_across(*args):
                    copy.start()
            elif name == PARTIAL:
                q, dy, h = args
                if once(PARTIAL):
                    own_h.wait()
                    h_pair.wait_recv()
                    hist_ready(0, 2)
                if once((PARTIAL, q)):
                    own_m(q).wait()
                    m_pair(q).wait_recv()
                if groups[q] == ALONG_FIRST:
                    buf, known = m_wide.at[wide.index(q)], pl.ds(0, 2 * modes)
                    start = line(dy) * span + (h + side * (1 - 2 * h)) * (span // 2)
                    cols = pl.ds(pl.multiple_of(start, 128), span // 2)
                else:
                    if once(SHARE):
                        h_relay.wait_recv()
                        hist_ready(2, 2)
                    for copy in m_across(q, h):
                        copy.wait_recv()
                    buf, known, cols = m_tall.at[tall.index(q)], pl.ds(0, 4 * modes), halved(h)
                part[slot(q, dy), halved(h)] = dot3(
                    split(buf[:, cols]), (hist_hi[known], hist_lo[known]), ((0,), (0,))
                )
            elif name == REDUCE:
                q, dy, j, to, kids = args
                if kids:
                    part[slot(q, dy), span_of(j)] = summed(q, dy, j, kids)
                rs_copy(q, dy, j, to, heading[to]).start()
            elif name == ROOT:
                q, dy, j, kids = args
                seen.add((ROOT, q, dy, j))
                rows[2 * q + line(dy), span_of(j)] = summed(q, dy, j, kids)
            elif name == GATHER:
                row_ready(*args[:3])
                ag_copy(*args).start()
            elif name == REDUCED:
                rs_copy(*args, heading[args[-1]]).wait_send()
            elif name == GATHERED:
                ag_copy(*args).wait_send()
            elif name == RECOVER:
                q, dy, h = args
                for j in range(h * pieces // 2, (h + 1) * pieces // 2):
                    row_ready(q, dy, j)
                if once(RECOVER):
                    own_r.wait()
                    r_copy.wait_recv()
                start = (2 * q + line(dy)) * span + (h + side * (1 - 2 * h)) * (span // 2)
                cols = pl.ds(pl.multiple_of(start, 128), span // 2)
                values = split(rows[2 * q + line(dy), halved(h)])
                for base in (outs, 0):
                    here = pl.ds(base, outs)
                    added = dot3(split(r_buf[here, cols]), values, ((1,), (0,)))
                    acc[here] = added if op is recoveries[0] else acc[here] + added
                    if op is recoveries[-1] and base:
                        acc_copy.start()

    own_h.start()
    for q in wide + tall:
        own_m(q).start()
    barrier = pltpu.get_barrier_semaphore()
    for other in (partner, across, diagonal, target[INWARD]):
        pl.semaphore_signal(barrier, inc=1, device_id={"rows": other}, device_id_type=MESH)

    @pl.when(middle == 1)
    def _():
        pl.semaphore_signal(barrier, inc=1, device_id={"rows": target[OUTWARD]}, device_id_type=MESH)

    pl.semaphore_wait(barrier, 4 + middle)
    h_pair.start()
    for q in wide + tall:
        m_pair(q).start()

    for role in range(2):
        pl.when(middle == role)(functools.partial(run, orders[role]))

    h_pair.wait_send()
    h_across.wait_send()
    h_relay.wait_send()
    r_copy.wait_send()
    for q in range(count):
        m_pair(q).wait_send()
    for q in tall:
        for copy in m_across(q, 0) + m_across(q, 1):
            copy.wait_send()
    acc_copy.wait()
    acc_other[...] = acc[pl.ds(0, outs)] + acc_other[...]
    found = pltpu.make_async_copy(acc_other, out_ref, local_sem.at[0])
    found.start()
    found.wait()


def grid_call(plan, histories, modal_map, recovery):
    modes, time_cols = histories.shape
    outs, dofs = recovery.shape
    groups, pieces, _ = plan
    half, count = dofs // 2, len(groups)
    span = half // (2 * count)
    n_wide, n_tall = groups.count(ALONG_FIRST), groups.count(ACROSS_FIRST)
    slots = 2 * n_wide + n_tall
    f32, dma = jnp.float32, pltpu.SemaphoreType.DMA
    anywhere = pl.BlockSpec(memory_space=pltpu.HBM)
    return pl.pallas_call(
        functools.partial(grid_kernel, plan),
        out_shape=jax.ShapeDtypeStruct((outs, time_cols), f32),
        in_specs=[anywhere, anywhere, anywhere],
        out_specs=pl.BlockSpec(memory_space=pl.ANY),
        scratch_shapes=[
            pltpu.VMEM((4 * modes, time_cols), f32),
            pltpu.VMEM((4 * modes, time_cols), jnp.bfloat16),
            pltpu.VMEM((4 * modes, time_cols), jnp.bfloat16),
            pltpu.VMEM((n_wide, 2 * modes, 2 * span), f32),
            pltpu.VMEM((n_tall, 4 * modes, span), f32),
            pltpu.VMEM((2 * outs, half), f32),
            pltpu.VMEM((slots, span, time_cols), f32),
            pltpu.VMEM((slots, 3, span, time_cols), f32),
            pltpu.VMEM((2 * count, span, time_cols), f32),
            pltpu.VMEM((2 * outs, time_cols), f32),
            pltpu.VMEM((outs, time_cols), f32),
            dma((2,)),
            dma((5,)),
            dma((5,)),
            dma((count,)),
            dma((count, 2, 3)),
            dma((count, 2, 3)),
            dma((slots, pieces, 3)),
            dma((slots, pieces, 3)),
            dma((2 * count, pieces, 3)),
            dma((2 * count, pieces)),
        ],
        compiler_params=pltpu.CompilerParams(
            collective_id=1, has_side_effects=True, vmem_limit_bytes=52 * 2**20
        ),
    )(histories, modal_map, recovery)


def ring_call(chips, histories, modal_map, recovery):
    modes, time_cols = histories.shape
    outs, dofs = recovery.shape
    half = dofs // 2
    block = half // chips
    ways = 2 if block % 256 == 0 else 1
    unit = block // ways
    f32, dma = jnp.float32, pltpu.SemaphoreType.DMA
    vmem, anywhere = pl.BlockSpec(memory_space=pltpu.VMEM), pl.BlockSpec(memory_space=pltpu.HBM)
    return pl.pallas_call(
        functools.partial(kernel, chips, ways),
        out_shape=jax.ShapeDtypeStruct((outs, time_cols), f32),
        in_specs=[anywhere, anywhere, anywhere],
        out_specs=vmem,
        scratch_shapes=[
            pltpu.VMEM((2 * modes, time_cols), f32),
            pltpu.VMEM((2 * modes, time_cols), jnp.bfloat16),
            pltpu.VMEM((2 * modes, time_cols), jnp.bfloat16),
            pltpu.VMEM((2 * modes, half), f32),
            pltpu.VMEM((2 * outs, half), f32),
            pltpu.VMEM((ways, chips - 1, unit, time_cols), f32),
            pltpu.VMEM((ways, chips - 1, unit, time_cols), f32),
            pltpu.VMEM((chips, ways, unit, time_cols), f32),
            pltpu.VMEM((2 * outs, time_cols), f32),
            pltpu.VMEM((outs, time_cols), f32),
            dma((2,)),
            dma((3,)),
            dma((3,)),
            dma((ways, chips)),
            dma((ways, chips)),
            dma((ways, chips)),
            dma((ways, chips - 1, SUBS)),
            dma((ways, chips - 1, SUBS)),
            dma((ways, chips - 1, SUBS)),
            dma((ways, chips - 1, SUBS)),
        ],
        compiler_params=pltpu.CompilerParams(
            collective_id=0, has_side_effects=True, vmem_limit_bytes=50 * 2**20
        ),
    )(histories, modal_map, recovery)


def shards(size, histories, modal_map, recovery):
    chips = size // 2
    time_cols, outs = histories.shape[1], recovery.shape[0]
    f32, vmem = jnp.float32, pl.BlockSpec(memory_space=pltpu.VMEM)
    if chips == 8:
        found = grid_call((GROUPS, PIECES, ORDERS), histories, modal_map, recovery)
    else:
        found = ring_call(chips, histories, modal_map, recovery)
    return pl.pallas_call(
        statistics,
        out_shape=(
            jax.ShapeDtypeStruct((outs, time_cols), f32),
            jax.ShapeDtypeStruct((CASES, outs), f32),
            jax.ShapeDtypeStruct((CASES, outs), f32),
        ),
        in_specs=[vmem], compiler_params=pltpu.CompilerParams(vmem_limit_bytes=8 * 2**20),
        out_specs=(vmem, vmem, vmem),
    )(found)


def solution(mesh):
    return jax.shard_map(
        functools.partial(shards, mesh.shape["rows"]),
        mesh=mesh,
        in_specs=(P(("grp", "rows"), None), P(("grp", "rows"), None), P(("grp", "rows"), None)),
        out_specs=(P(("grp", "rows"), None), P(None, ("grp", "rows")), P(None, ("grp", "rows"))),
        check_vma=False,
    )
```

```python
import functools

import jax
import jax.numpy as jnp
from jax import lax
from jax.experimental import pallas as pl
from jax.experimental.pallas import tpu as pltpu
from jax.sharding import PartitionSpec as P

CASES = 4
SUBS = 2
epsilon = 1e-06
MESH = pl.DeviceIdType.MESH


def split(x):
    high = x.astype(jnp.bfloat16)
    return high, (x - high.astype(jnp.float32)).astype(jnp.bfloat16)


def dot3(a, b, dims):
    mul = functools.partial(
        lax.dot_general, dimension_numbers=(dims, ((), ())), preferred_element_type=jnp.float32
    )
    return mul(a[0], b[0]) + (mul(a[0], b[1]) + mul(a[1], b[0]))


def ring_position(chips, chip):
    if chips == 8:
        z, y = chip // 2, chip % 2
        return y * (chips - 1 - 2 * z) + z
    return chip


def chip_at(chips, position):
    if chips == 8:
        y = position // 4
        return (y * (chips - 1 - 2 * position) + position) * 2 + y
    return position


def kernel(
    chips, ways, h_ref, m_ref, r_ref, out_ref,
    hist, hist_hi, hist_lo, m_buf, r_buf, part, landed, rows, acc, acc_other,
    local_sem, pair_send, pair_recv, m_local, m_send, m_recv, rs_send, rs_recv, ag_send, ag_recv,
):
    me = lax.axis_index("rows")
    core = me % 2
    partner = me + 1 - 2 * core
    pos = ring_position(chips, me // 2)
    after = chip_at(chips, (pos + 1) % chips) * 2 + core
    before = chip_at(chips, (pos + chips - 1) % chips) * 2 + core
    targets = (after, before)
    signs = (1, -1)

    modes, outs = h_ref.shape[0], r_ref.shape[0]
    half = m_ref.shape[1] // 2
    block = half // chips
    unit = block // ways
    piece = unit // SUBS
    cuts = SUBS if piece % 128 == 0 else 1
    width = unit // cuts

    def at(p):
        return (p + 2 * chips) % chips

    def cols(base, b, d, start=0, size=unit):
        return pl.ds(pl.multiple_of(base + b * block + d * unit + start, 128), size)

    def remote(src, dst, send, recv, to):
        return pltpu.make_async_remote_copy(
            src_ref=src, dst_ref=dst, send_sem=send, recv_sem=recv,
            device_id={"rows": to}, device_id_type=MESH,
        )

    def sum_block(k, d):
        return at(pos - signs[d] * (k + 1))

    def m_copy(k, d):
        b = sum_block(k, d)
        return remote(
            m_ref.at[:, cols((1 - core) * half, b, d)],
            m_buf.at[pl.ds(modes, modes), cols(0, b, d)],
            m_send.at[d, k], m_recv.at[d, k], partner,
        )

    def own_m(k, d):
        b = sum_block(k, d)
        return pltpu.make_async_copy(
            m_ref.at[:, cols(core * half, b, d)],
            m_buf.at[pl.ds(0, modes), cols(0, b, d)], m_local.at[d, k],
        )

    def rs_copy(k, d, j):
        view = (d, k, pl.ds(j * piece, piece))
        return remote(part.at[view], landed.at[view], rs_send.at[d, k, j], rs_recv.at[d, k, j], targets[d])

    def ag_copy(s, d, j, arrives=False):
        b = at(pos - signs[d] * (s + 1 if arrives else s))
        view = (b, d, pl.ds(j * piece, piece))
        return remote(rows.at[view], rows.at[view], ag_send.at[d, s, j], ag_recv.at[d, s, j], targets[d])

    own_h = pltpu.make_async_copy(h_ref, hist.at[pl.ds(0, modes)], local_sem.at[0])
    own_r = pltpu.make_async_copy(
        r_ref.at[:, pl.ds(pl.multiple_of(core * half, 128), half)],
        r_buf.at[pl.ds(0, outs)], local_sem.at[1],
    )
    h_copy = remote(h_ref, hist.at[pl.ds(modes, modes)], pair_send.at[0], pair_recv.at[0], partner)
    r_copy = remote(
        r_ref.at[:, pl.ds(pl.multiple_of((1 - core) * half, 128), half)],
        r_buf.at[pl.ds(outs, outs)], pair_send.at[1], pair_recv.at[1], partner,
    )
    acc_copy = remote(acc.at[pl.ds(outs, outs)], acc_other, pair_send.at[2], pair_recv.at[2], partner)

    own_h.start()
    for d in range(ways):
        own_m(0, d).start()
    barrier = pltpu.get_barrier_semaphore()
    for other in (after, before, partner):
        pl.semaphore_signal(barrier, inc=1, device_id={"rows": other}, device_id_type=MESH)
    pl.semaphore_wait(barrier, 3)

    h_copy.start()
    for d in range(ways):
        m_copy(0, d).start()

    @pl.loop(1, chips)
    def _(k):
        for d in range(ways):
            own_m(k, d).start()
            m_copy(k, d).start()

    own_h.wait()
    hist_hi[pl.ds(0, modes)], hist_lo[pl.ds(0, modes)] = split(hist[pl.ds(0, modes)])
    h_copy.wait_recv()
    hist_hi[pl.ds(modes, modes)], hist_lo[pl.ds(modes, modes)] = split(hist[pl.ds(modes, modes)])

    def shapes_here(k, d):
        own_m(k, d).wait()
        m_copy(k, d).wait_recv()

    def partial_rows(k, d, start=0, size=unit):
        shapes = split(m_buf[:, cols(0, sum_block(k, d), d, start, size)])
        return dot3(shapes, (hist_hi[...], hist_lo[...]), ((0,), (0,)))

    for cut in range(cuts):
        for d in range(ways):
            if cut == 0:
                shapes_here(0, d)
            start = cut * width
            part[d, 0, pl.ds(start, width)] = partial_rows(0, d, start, width)
            for j in range(cut * SUBS // cuts, (cut + 1) * SUBS // cuts):
                rs_copy(0, d, j).start()

    own_r.start()
    r_copy.start()

    @pl.loop(1, chips - 1)
    def _(k):
        for d in range(ways):
            shapes_here(k, d)
            part[d, k] = partial_rows(k, d)
        for j in range(SUBS):
            for d in range(ways):
                rs_copy(k - 1, d, j).wait_recv()
                view = (d, k, pl.ds(j * piece, piece))
                part[view] = part[view] + landed[d, k - 1, pl.ds(j * piece, piece)]
                rs_copy(k, d, j).start()

    last = chips - 1
    for d in range(ways):
        shapes_here(last, d)
        rows[pos, d] = partial_rows(last, d)
    for j in range(SUBS):
        for d in range(ways):
            rs_copy(last - 1, d, j).wait_recv()
            view = (pos, d, pl.ds(j * piece, piece))
            rows[view] = rows[view] + landed[d, last - 1, pl.ds(j * piece, piece)]
            ag_copy(0, d, j).start()

    own_r.wait()
    r_copy.wait_recv()

    def recovered(b, d):
        return dot3(split(r_buf[:, cols(0, b, d)]), split(rows[b, d]), ((1,), (0,)))

    acc[...] = recovered(pos, 0)
    for d in range(1, ways):
        acc[...] += recovered(pos, d)

    @pl.loop(0, chips - 2)
    def _(s):
        for j in range(SUBS):
            for d in range(ways):
                ag_copy(s, d, j, arrives=True).wait_recv()
                ag_copy(s + 1, d, j).start()
        for d in range(ways):
            acc[...] += recovered(at(pos - signs[d] * (s + 1)), d)

    for cut in range(cuts):
        for d in range(ways):
            for j in range(cut * SUBS // cuts, (cut + 1) * SUBS // cuts):
                ag_copy(chips - 2, d, j, arrives=True).wait_recv()
            b, start = at(pos - signs[d] * (chips - 1)), cut * width
            weights = split(r_buf[:, cols(0, b, d, start, width)])
            finished = split(rows[b, d, pl.ds(start, width)])
            final = cut == cuts - 1 and d == ways - 1
            for base in (outs, 0):
                own = tuple(w[base : base + outs] for w in weights)
                acc[pl.ds(base, outs)] += dot3(own, finished, ((1,), (0,)))
                if final and base:
                    acc_copy.start()

    h_copy.wait_send()
    r_copy.wait_send()

    @pl.loop(0, chips)
    def _(k):
        for d in range(ways):
            m_copy(k, d).wait_send()

    @pl.loop(0, chips - 1)
    def _(k):
        for d in range(ways):
            for j in range(SUBS):
                rs_copy(k, d, j).wait_send()
                ag_copy(k, d, j).wait_send()

    acc_copy.wait()
    out_ref[...] = acc[pl.ds(0, outs)] + acc_other[...]


def statistics(found_ref, out_ref, peak_ref, rms_ref):
    responses = found_ref[...]
    out_ref[...] = responses
    by_time = responses.T
    steps = by_time.shape[0] // CASES
    for k in range(CASES):
        case = by_time[k * steps : (k + 1) * steps]
        peak_ref[k : k + 1] = jnp.max(jnp.abs(case), axis=0, keepdims=True)
        mean = jnp.sum(case * case, axis=0, keepdims=True) / steps
        rms_ref[k : k + 1] = jnp.sqrt(mean + epsilon)


ACROSS, INWARD, OUTWARD = range(3)
H_ACROSS, H_RELAY, SHARE, PARTIAL, REDUCE, ROOT, GATHER, RECOVER, REDUCED, GATHERED = range(10)
ALONG_FIRST, ACROSS_FIRST = range(2)
GROUPS = (ACROSS_FIRST, ACROSS_FIRST, ALONG_FIRST, ACROSS_FIRST, ACROSS_FIRST, ACROSS_FIRST, ACROSS_FIRST, ALONG_FIRST)
PIECES = 4
ORDERS = (
    (
        (0,), (3, 2, 1), (4, 2, 1, 2, 1, ()), (3, 2, 0), (4, 2, 0, 2, 1, ()), (3, 7, 1), (4, 2, 1, 3, 0, ()),
        (3, 7, 0), (4, 2, 1, 1, 1, ()), (4, 2, 1, 0, 0, ()), (1,), (4, 2, 0, 1, 1, ()), (2, 0), (4, 2, 0, 3, 1, (0,)),
        (8, 2, 1, 2, 1), (4, 2, 0, 0, 1, (0,)), (8, 2, 0, 2, 1), (8, 2, 1, 3, 0), (2, 1), (4, 7, 0, 2, 1, ()),
        (8, 2, 1, 1, 1), (8, 2, 1, 0, 0), (4, 7, 1, 3, 1, ()), (3, 0, 0), (8, 2, 0, 1, 1), (4, 0, 0, 3, 1, ()),
        (2, 3), (8, 2, 0, 3, 1), (4, 0, 0, 2, 1, ()), (8, 2, 0, 0, 1), (4, 0, 0, 1, 1, ()), (3, 1, 0),
        (8, 7, 0, 2, 1), (4, 1, 0, 3, 1, ()), (2, 4), (8, 7, 1, 3, 1), (4, 1, 0, 2, 1, ()), (8, 0, 0, 3, 1),
        (7, 2, 0), (4, 1, 0, 1, 1, ()), (3, 3, 0), (8, 0, 0, 2, 1), (2, 5), (4, 3, 0, 2, 1, ()), (8, 0, 0, 1, 1),
        (4, 3, 0, 3, 1, ()), (3, 4, 0), (8, 1, 0, 3, 1), (5, 0, 0, 0, (1,)), (4, 4, 0, 2, 1, ()), (2, 6),
        (8, 1, 0, 2, 1), (4, 4, 0, 3, 1, ()), (8, 1, 0, 1, 1), (4, 4, 0, 0, 1, ()), (3, 5, 0), (8, 3, 0, 2, 1),
        (5, 1, 0, 0, (1,)), (4, 5, 0, 2, 1, ()), (6, 0, 0, 0, 0), (8, 3, 0, 3, 1), (4, 5, 0, 3, 1, ()),
        (6, 1, 0, 0, 0), (8, 4, 0, 2, 1), (3, 6, 0), (4, 5, 0, 0, 1, ()), (6, 1, 0, 1, 0), (8, 4, 0, 3, 1),
        (5, 3, 0, 1, (1,)), (4, 6, 0, 2, 1, ()), (6, 3, 0, 1, 0), (8, 4, 0, 0, 1), (5, 3, 0, 0, (1,)),
        (6, 0, 1, 0, 1), (6, 3, 0, 0, 0), (8, 5, 0, 2, 1), (9, 0, 0, 0, 0), (4, 6, 0, 3, 1, ()), (6, 1, 0, 2, 0),
        (8, 5, 0, 3, 1), (5, 4, 0, 1, (1,)), (9, 1, 0, 0, 0), (4, 6, 0, 0, 1, ()), (6, 4, 0, 1, 0), (8, 5, 0, 0, 1),
        (9, 1, 0, 1, 0), (6, 3, 1, 0, 1), (6, 0, 0, 2, 0), (8, 6, 0, 2, 1), (5, 5, 0, 1, (1,)), (9, 3, 0, 1, 0),
        (4, 7, 0, 3, 1, ()), (6, 5, 0, 1, 0), (9, 0, 1, 0, 1), (9, 3, 0, 0, 0), (4, 7, 1, 0, 1, ()), (6, 2, 0, 2, 0),
        (8, 6, 0, 3, 1), (9, 1, 0, 2, 0), (4, 7, 1, 2, 1, ()), (6, 4, 0, 0, 0), (8, 6, 0, 0, 1), (5, 6, 0, 1, (1,)),
        (9, 4, 0, 1, 0), (6, 5, 1, 1, 1), (6, 4, 0, 3, 0), (9, 3, 1, 0, 1), (9, 0, 0, 2, 0), (7, 2, 1),
        (4, 7, 1, 1, 1, ()), (6, 5, 0, 0, 0), (8, 7, 0, 3, 1), (9, 5, 0, 1, 0), (6, 1, 1, 0, 1), (6, 0, 1, 3, 0),
        (8, 7, 1, 0, 1), (7, 0, 1), (9, 2, 0, 2, 0), (6, 3, 1, 1, 1), (6, 6, 0, 1, 0), (8, 7, 1, 2, 1),
        (9, 4, 0, 0, 0), (6, 4, 1, 1, 1), (6, 5, 0, 3, 0), (9, 5, 1, 1, 1), (9, 4, 0, 3, 0), (7, 0, 0),
        (4, 7, 0, 1, 1, ()), (8, 7, 1, 1, 1), (6, 6, 0, 3, 0), (9, 5, 0, 0, 0), (6, 6, 0, 1, 1), (9, 1, 1, 0, 1),
        (5, 7, 0, 0, (1,)), (9, 0, 1, 3, 0), (6, 7, 0, 0, 0), (6, 7, 0, 0, 1), (9, 3, 1, 1, 1), (6, 5, 1, 2, 0),
        (9, 6, 0, 1, 0), (7, 5, 1), (6, 0, 0, 3, 1), (9, 4, 1, 1, 1), (6, 3, 0, 3, 0), (9, 5, 0, 3, 0),
        (6, 5, 1, 3, 1), (8, 7, 0, 1, 1), (6, 1, 1, 3, 0), (9, 6, 0, 3, 0), (7, 1, 1), (6, 5, 0, 2, 1), (7, 5, 0),
        (9, 6, 0, 1, 1), (6, 3, 1, 2, 0), (9, 7, 0, 0, 0), (7, 3, 1), (9, 7, 0, 0, 1), (6, 4, 1, 2, 0),
        (9, 5, 1, 2, 0), (7, 1, 0), (7, 4, 1), (9, 0, 0, 3, 1), (6, 7, 0, 1, 0), (9, 3, 0, 3, 0), (7, 3, 0),
        (9, 5, 1, 3, 1), (6, 6, 0, 2, 0), (9, 1, 1, 3, 0), (7, 4, 0), (7, 6, 0), (9, 5, 0, 2, 1), (6, 7, 0, 2, 0),
        (9, 3, 1, 2, 0), (7, 7, 0), (9, 4, 1, 2, 0), (7, 6, 1), (9, 7, 0, 1, 0), (7, 7, 1), (9, 6, 0, 2, 0),
        (9, 7, 0, 2, 0),
    ),
    (
        (0,), (3, 2, 1), (4, 2, 1, 0, 1, ()), (3, 2, 0), (3, 7, 1), (2, 0), (3, 7, 0), (4, 2, 1, 2, 1, (2,)), (1,),
        (4, 2, 0, 2, 1, (2,)), (4, 2, 1, 3, 0, (1,)), (8, 2, 1, 0, 1), (4, 2, 1, 1, 0, (1, 2)), (3, 0, 0), (2, 1),
        (8, 2, 1, 2, 1), (4, 2, 0, 3, 1, (0, 2)), (5, 2, 0, 1, (0, 1, 2)), (8, 2, 0, 2, 1), (6, 2, 0, 1, 1),
        (6, 2, 0, 1, 2), (8, 2, 1, 3, 0), (6, 2, 0, 1, 0), (5, 2, 0, 0, (1, 2)), (6, 2, 0, 0, 2), (6, 2, 0, 0, 1),
        (8, 2, 1, 1, 0), (6, 2, 0, 0, 0), (4, 7, 1, 3, 1, (2,)), (6, 2, 0, 2, 2), (3, 1, 0), (6, 2, 0, 2, 0),
        (4, 0, 0, 3, 1, (2,)), (8, 2, 0, 3, 1), (6, 2, 0, 3, 2), (7, 2, 0), (6, 2, 1, 1, 2), (2, 3), (9, 2, 0, 1, 1),
        (9, 2, 0, 1, 2), (4, 0, 0, 2, 1, (2,)), (6, 2, 1, 0, 2), (6, 2, 1, 0, 1), (9, 2, 0, 1, 0), (9, 2, 0, 0, 2),
        (9, 2, 0, 0, 1), (4, 0, 0, 0, 2, (1,)), (4, 1, 0, 3, 1, (2,)), (8, 7, 1, 3, 1), (9, 2, 0, 2, 2),
        (5, 0, 0, 1, (1, 2)), (9, 2, 0, 0, 0), (6, 0, 0, 1, 2), (2, 4), (6, 0, 0, 1, 1), (8, 0, 0, 3, 1),
        (9, 2, 0, 3, 2), (7, 2, 1), (9, 2, 0, 2, 0), (6, 2, 1, 3, 2), (4, 1, 0, 2, 1, (2,)), (9, 2, 1, 1, 2),
        (8, 0, 0, 2, 1), (3, 3, 0), (4, 1, 0, 0, 2, (1,)), (4, 3, 0, 2, 1, (2,)), (9, 2, 1, 0, 2), (9, 2, 1, 0, 1),
        (2, 5), (6, 0, 0, 2, 2), (4, 3, 0, 3, 1, (2,)), (8, 0, 0, 0, 2), (8, 1, 0, 3, 1), (5, 1, 0, 1, (1, 2)),
        (6, 1, 0, 1, 2), (6, 1, 0, 1, 1), (3, 4, 0), (9, 0, 0, 1, 2), (9, 0, 0, 1, 1), (4, 3, 0, 1, 2, (1,)),
        (4, 4, 0, 2, 1, (2,)), (2, 6), (9, 2, 1, 3, 2), (8, 1, 0, 2, 1), (4, 3, 0, 0, 2, (1,)), (4, 4, 0, 3, 1, (2,)),
        (8, 1, 0, 0, 2), (8, 3, 0, 2, 1), (3, 5, 0), (6, 1, 0, 2, 2), (4, 5, 0, 2, 1, (2,)), (9, 0, 0, 2, 2),
        (8, 3, 0, 3, 1), (4, 4, 0, 1, 2, (1,)), (4, 7, 0, 2, 0, (2,)), (4, 5, 0, 3, 1, (2,)), (9, 1, 0, 1, 2),
        (9, 1, 0, 1, 1), (5, 4, 0, 0, (1, 2)), (6, 4, 0, 0, 2), (6, 4, 0, 0, 1), (6, 0, 0, 1, 0), (8, 3, 0, 1, 2),
        (8, 4, 0, 2, 1), (3, 6, 0), (4, 5, 0, 1, 2, (1,)), (6, 0, 0, 2, 0), (4, 6, 0, 2, 1, (2,)), (8, 3, 0, 0, 2),
        (8, 4, 0, 3, 1), (5, 5, 0, 0, (1, 2)), (6, 5, 0, 0, 2), (6, 5, 0, 0, 1), (6, 1, 0, 1, 0), (9, 1, 0, 2, 2),
        (8, 5, 0, 2, 1), (6, 4, 0, 3, 2), (6, 0, 1, 0, 1), (6, 0, 1, 0, 0), (8, 4, 0, 1, 2), (8, 7, 0, 2, 0),
        (8, 5, 0, 3, 1), (4, 6, 0, 1, 2, (1,)), (4, 6, 0, 3, 1, (2,)), (6, 1, 0, 2, 0), (9, 4, 0, 0, 2),
        (9, 4, 0, 0, 1), (9, 0, 0, 1, 0), (6, 5, 0, 3, 2), (6, 4, 0, 0, 0), (6, 3, 1, 0, 1), (8, 5, 0, 1, 2),
        (9, 0, 0, 2, 0), (8, 6, 0, 2, 1), (7, 0, 1), (6, 0, 1, 3, 2), (6, 3, 1, 0, 0), (4, 7, 0, 3, 1, (2,)),
        (9, 5, 0, 0, 2), (9, 5, 0, 0, 1), (9, 1, 0, 1, 0), (5, 6, 0, 0, (1, 2)), (6, 0, 1, 1, 2), (6, 6, 0, 0, 1),
        (6, 6, 0, 0, 0), (9, 4, 0, 3, 2), (9, 0, 1, 0, 1), (9, 0, 1, 0, 0), (6, 6, 0, 0, 2), (4, 7, 1, 0, 0, (1, 2)),
        (4, 7, 1, 2, 1, (0, 2)), (8, 6, 0, 1, 2), (8, 6, 0, 3, 1), (9, 1, 0, 2, 0), (6, 3, 1, 3, 0), (6, 5, 1, 1, 1),
        (9, 5, 0, 3, 2), (9, 4, 0, 0, 0), (9, 3, 1, 0, 1), (6, 6, 1, 0, 2), (6, 6, 0, 3, 2), (6, 4, 0, 3, 0),
        (6, 6, 1, 0, 1), (9, 0, 1, 3, 2), (9, 3, 1, 0, 0), (8, 7, 0, 3, 1), (4, 7, 0, 0, 2, (0, 1)),
        (4, 7, 1, 1, 0, (1, 2)), (6, 1, 1, 0, 1), (9, 0, 1, 1, 2), (9, 6, 0, 0, 1), (9, 6, 0, 0, 0), (6, 5, 1, 2, 2),
        (6, 5, 0, 0, 0), (6, 3, 1, 1, 1), (9, 6, 0, 0, 2), (8, 7, 1, 0, 0), (8, 7, 1, 2, 1), (6, 3, 0, 3, 2),
        (6, 5, 1, 1, 0), (6, 4, 1, 1, 1), (9, 3, 1, 3, 0), (9, 5, 1, 1, 1), (9, 6, 1, 0, 2), (7, 1, 1),
        (6, 1, 1, 3, 2), (6, 1, 1, 3, 0), (5, 7, 0, 1, (0, 2)), (9, 6, 0, 3, 2), (9, 4, 0, 3, 0), (9, 6, 1, 0, 1),
        (6, 7, 0, 1, 1), (7, 3, 1), (6, 3, 1, 2, 2), (6, 3, 1, 2, 0), (6, 6, 0, 1, 1), (8, 7, 0, 0, 2),
        (8, 7, 1, 1, 0), (9, 1, 1, 0, 1), (7, 4, 1), (6, 4, 1, 2, 2), (6, 6, 0, 1, 0), (6, 7, 0, 0, 1),
        (9, 5, 1, 2, 2), (9, 5, 0, 0, 0), (9, 3, 1, 1, 1), (6, 7, 0, 1, 2), (6, 7, 0, 2, 0), (6, 1, 0, 3, 1),
        (7, 0, 0), (9, 3, 0, 3, 2), (9, 5, 1, 1, 0), (9, 4, 1, 1, 1), (7, 6, 0), (6, 6, 0, 2, 2), (6, 3, 0, 2, 1),
        (6, 4, 1, 1, 0), (7, 5, 1), (9, 1, 1, 3, 2), (9, 1, 1, 3, 0), (9, 7, 0, 1, 1), (7, 7, 0), (6, 7, 0, 2, 2),
        (6, 7, 0, 3, 0), (6, 6, 1, 1, 1), (7, 5, 0), (9, 3, 1, 2, 2), (9, 3, 1, 2, 0), (9, 6, 0, 1, 1), (7, 1, 0),
        (6, 4, 1, 2, 0), (6, 7, 0, 3, 2), (6, 7, 1, 2, 1), (9, 4, 1, 2, 2), (9, 6, 0, 1, 0), (9, 7, 0, 0, 1),
        (7, 3, 0), (6, 7, 0, 0, 0), (9, 7, 0, 1, 2), (9, 7, 0, 2, 0), (9, 1, 0, 3, 1), (6, 7, 1, 3, 2), (7, 6, 1),
        (9, 6, 0, 2, 2), (9, 3, 0, 2, 1), (9, 4, 1, 1, 0), (7, 4, 0), (9, 7, 0, 2, 2), (9, 7, 0, 3, 0),
        (9, 6, 1, 1, 1), (7, 7, 1), (9, 4, 1, 2, 0), (9, 7, 0, 3, 2), (9, 7, 1, 2, 1), (9, 7, 0, 0, 0),
        (9, 7, 1, 3, 2),
    ),
)


def grid_kernel(
    plan, h_ref, m_ref, r_ref, out_ref,
    hist, hist_hi, hist_lo, m_wide, m_tall, r_buf, part, landed, rows, acc, acc_other,
    local_sem, pair_send, pair_recv, m_local, m_send, m_recv, rs_send, rs_recv, ag_send, ag_recv,
):
    groups, pieces, orders = plan
    count = len(groups)
    me = lax.axis_index("rows")
    core, y, z = me % 2, (me // 2) % 2, me // 4
    side = z // 2
    middle = (z + side) % 2
    inner, outer = z + 1 - 2 * side, z - 1 + 2 * side

    def device(at_z, at_y, at_core):
        return (at_z * 2 + at_y) * 2 + at_core

    partner = device(z, y, 1 - core)
    across, diagonal = device(z, 1 - y, core), device(z, 1 - y, 1 - core)
    target = (across, device(inner, y, core), device(outer, y, core))
    heading = (0, 1 + side, 2 - side)
    came = (0, 2 - side, 1 + side)

    modes, outs = h_ref.shape[0], r_ref.shape[0]
    half = m_ref.shape[1] // 2
    span = half // (2 * count)
    piece = span // pieces

    wide = [q for q in range(count) if groups[q] == ALONG_FIRST]
    tall = [q for q in range(count) if groups[q] == ACROSS_FIRST]

    def line(dy):
        return 1 - y if dy else y

    def place(j):
        return j + side * (pieces - 1 - 2 * j)

    def slot(q, dy):
        if groups[q] == ALONG_FIRST:
            return 2 * wide.index(q) + line(dy)
        return 2 * len(wide) + tall.index(q)

    def span_of(j):
        return pl.ds(pl.multiple_of(place(j) * piece, piece), piece)

    def remote(src, dst, send, recv, to):
        return pltpu.make_async_remote_copy(
            src_ref=src, dst_ref=dst, send_sem=send, recv_sem=recv,
            device_id={"rows": to}, device_id_type=MESH,
        )

    def shapes(q, at_core, at_y):
        if groups[q] == ALONG_FIRST:
            return m_ref.at[:, pl.ds(pl.multiple_of(at_core * half + 2 * q * span, 128), 2 * span)]
        return m_ref.at[:, pl.ds(pl.multiple_of(at_core * half + (2 * q + at_y) * span, 128), span)]

    def held(q, source):
        source = pl.ds(source * modes, modes)
        if groups[q] == ALONG_FIRST:
            return m_wide.at[wide.index(q), source]
        return m_tall.at[tall.index(q), source]

    def own_m(q):
        return pltpu.make_async_copy(shapes(q, core, y), held(q, 0), m_local.at[q])

    def m_pair(q):
        return remote(shapes(q, 1 - core, y), held(q, 1), m_send.at[q, 0], m_recv.at[q, 0], partner)

    def m_across(q):
        return tuple(
            remote(
                shapes(q, at_core, 1 - y), held(q, source),
                m_send.at[q, source - 1], m_recv.at[q, source - 1], to,
            )
            for source, to, at_core in ((2, across, core), (3, diagonal, 1 - core))
        )

    own_h = pltpu.make_async_copy(h_ref, hist.at[pl.ds(0, modes)], local_sem.at[0])
    h_pair = remote(h_ref, hist.at[pl.ds(modes, modes)], pair_send.at[0], pair_recv.at[0], partner)
    h_across = remote(h_ref, hist.at[pl.ds(2 * modes, modes)], pair_send.at[1], pair_recv.at[1], across)
    h_relay = remote(
        hist.at[pl.ds(2 * modes, modes)], hist.at[pl.ds(3 * modes, modes)],
        pair_send.at[2], pair_recv.at[2], partner,
    )
    own_r = pltpu.make_async_copy(
        r_ref.at[:, pl.ds(pl.multiple_of(core * half, 128), half)],
        r_buf.at[pl.ds(0, outs)], local_sem.at[1],
    )
    r_copy = remote(
        r_ref.at[:, pl.ds(pl.multiple_of((1 - core) * half, 128), half)],
        r_buf.at[pl.ds(outs, outs)], pair_send.at[3], pair_recv.at[3], partner,
    )
    acc_copy = remote(acc.at[pl.ds(outs, outs)], acc_other, pair_send.at[4], pair_recv.at[4], partner)

    def rs_copy(q, dy, j, to, d):
        k = slot(q, dy)
        return remote(
            part.at[k, span_of(j)], landed.at[k, d, span_of(j)],
            rs_send.at[k, place(j), d], rs_recv.at[k, place(j), d], target[to],
        )

    def ag_copy(q, dy, j, to):
        k = 2 * q + line(dy)
        view = rows.at[k, span_of(j)]
        return remote(
            view, view, ag_send.at[k, place(j), heading[to]], ag_recv.at[k, place(j)], target[to]
        )

    def hist_ready(first, size):
        here = pl.ds(first * modes, size * modes)
        hist_hi[here], hist_lo[here] = split(hist[here])

    def run(order):
        seen = set()

        def once(key):
            fresh = key not in seen
            seen.add(key)
            return fresh

        def row_ready(q, dy, j):
            if once((ROOT, q, dy, j)):
                ag_copy(q, dy, j, ACROSS).wait_recv()

        def summed(q, dy, j, kids):
            total = part[slot(q, dy), span_of(j)]
            for kid in kids:
                rs_copy(q, dy, j, ACROSS, came[kid]).wait_recv()
            for kid in kids:
                total = total + landed[slot(q, dy), came[kid], span_of(j)]
            return total

        recoveries = [op for op in order if op[0] == RECOVER]
        for op in order:
            name, args = op[0], op[1:]
            if name == H_ACROSS:
                h_across.start()
            elif name == H_RELAY:
                h_across.wait_recv()
                h_relay.start()
                own_r.start()
                r_copy.start()
            elif name == SHARE:
                for copy in m_across(*args):
                    copy.start()
            elif name == PARTIAL:
                q, dy = args
                if once(PARTIAL):
                    own_h.wait()
                    h_pair.wait_recv()
                    hist_ready(0, 2)
                if once((PARTIAL, q)):
                    own_m(q).wait()
                    m_pair(q).wait_recv()
                if groups[q] == ALONG_FIRST:
                    buf, known = m_wide.at[wide.index(q)], pl.ds(0, 2 * modes)
                    cols = pl.ds(pl.multiple_of(line(dy) * span, 128), span)
                else:
                    if once(SHARE):
                        h_relay.wait_recv()
                        hist_ready(2, 2)
                    for copy in m_across(q):
                        copy.wait_recv()
                    buf, known, cols = m_tall.at[tall.index(q)], pl.ds(0, 4 * modes), pl.ds(0, span)
                part[slot(q, dy)] = dot3(split(buf[:, cols]), (hist_hi[known], hist_lo[known]), ((0,), (0,)))
            elif name == REDUCE:
                q, dy, j, to, kids = args
                if kids:
                    part[slot(q, dy), span_of(j)] = summed(q, dy, j, kids)
                rs_copy(q, dy, j, to, heading[to]).start()
            elif name == ROOT:
                q, dy, j, kids = args
                seen.add((ROOT, q, dy, j))
                rows[2 * q + line(dy), span_of(j)] = summed(q, dy, j, kids)
            elif name == GATHER:
                row_ready(*args[:3])
                ag_copy(*args).start()
            elif name == REDUCED:
                rs_copy(*args, heading[args[-1]]).wait_send()
            elif name == GATHERED:
                ag_copy(*args).wait_send()
            elif name == RECOVER:
                q, dy = args
                for j in range(pieces):
                    row_ready(q, dy, j)
                if once(RECOVER):
                    own_r.wait()
                    r_copy.wait_recv()
                known = 2 * q + line(dy)
                cols = pl.ds(pl.multiple_of(known * span, 128), span)
                values = split(rows[known])
                for base in (outs, 0):
                    here = pl.ds(base, outs)
                    added = dot3(split(r_buf[here, cols]), values, ((1,), (0,)))
                    acc[here] = added if op is recoveries[0] else acc[here] + added
                    if op is recoveries[-1] and base:
                        acc_copy.start()

    own_h.start()
    for q in wide + tall:
        own_m(q).start()
    barrier = pltpu.get_barrier_semaphore()
    for other in (partner, across, diagonal, target[INWARD]):
        pl.semaphore_signal(barrier, inc=1, device_id={"rows": other}, device_id_type=MESH)

    @pl.when(middle == 1)
    def _():
        pl.semaphore_signal(barrier, inc=1, device_id={"rows": target[OUTWARD]}, device_id_type=MESH)

    pl.semaphore_wait(barrier, 4 + middle)
    h_pair.start()
    for q in wide + tall:
        m_pair(q).start()

    for role in range(2):
        pl.when(middle == role)(functools.partial(run, orders[role]))

    h_pair.wait_send()
    h_across.wait_send()
    h_relay.wait_send()
    r_copy.wait_send()
    for q in range(count):
        m_pair(q).wait_send()
    for q in tall:
        for copy in m_across(q):
            copy.wait_send()
    acc_copy.wait()
    acc_other[...] = acc[pl.ds(0, outs)] + acc_other[...]
    found = pltpu.make_async_copy(acc_other, out_ref, local_sem.at[0])
    found.start()
    found.wait()


def grid_call(plan, histories, modal_map, recovery):
    modes, time_cols = histories.shape
    outs, dofs = recovery.shape
    groups, pieces, _ = plan
    half, count = dofs // 2, len(groups)
    span = half // (2 * count)
    n_wide, n_tall = groups.count(ALONG_FIRST), groups.count(ACROSS_FIRST)
    slots = 2 * n_wide + n_tall
    f32, dma = jnp.float32, pltpu.SemaphoreType.DMA
    anywhere = pl.BlockSpec(memory_space=pltpu.HBM)
    return pl.pallas_call(
        functools.partial(grid_kernel, plan),
        out_shape=jax.ShapeDtypeStruct((outs, time_cols), f32),
        in_specs=[anywhere, anywhere, anywhere],
        out_specs=pl.BlockSpec(memory_space=pl.ANY),
        scratch_shapes=[
            pltpu.VMEM((4 * modes, time_cols), f32),
            pltpu.VMEM((4 * modes, time_cols), jnp.bfloat16),
            pltpu.VMEM((4 * modes, time_cols), jnp.bfloat16),
            pltpu.VMEM((n_wide, 2 * modes, 2 * span), f32),
            pltpu.VMEM((n_tall, 4 * modes, span), f32),
            pltpu.VMEM((2 * outs, half), f32),
            pltpu.VMEM((slots, span, time_cols), f32),
            pltpu.VMEM((slots, 3, span, time_cols), f32),
            pltpu.VMEM((2 * count, span, time_cols), f32),
            pltpu.VMEM((2 * outs, time_cols), f32),
            pltpu.VMEM((outs, time_cols), f32),
            dma((2,)),
            dma((5,)),
            dma((5,)),
            dma((count,)),
            dma((count, 3)),
            dma((count, 3)),
            dma((slots, pieces, 3)),
            dma((slots, pieces, 3)),
            dma((2 * count, pieces, 3)),
            dma((2 * count, pieces)),
        ],
        compiler_params=pltpu.CompilerParams(
            collective_id=1, has_side_effects=True, vmem_limit_bytes=52 * 2**20
        ),
    )(histories, modal_map, recovery)


def ring_call(chips, histories, modal_map, recovery):
    modes, time_cols = histories.shape
    outs, dofs = recovery.shape
    half = dofs // 2
    block = half // chips
    ways = 2 if block % 256 == 0 else 1
    unit = block // ways
    f32, dma = jnp.float32, pltpu.SemaphoreType.DMA
    vmem, anywhere = pl.BlockSpec(memory_space=pltpu.VMEM), pl.BlockSpec(memory_space=pltpu.HBM)
    return pl.pallas_call(
        functools.partial(kernel, chips, ways),
        out_shape=jax.ShapeDtypeStruct((outs, time_cols), f32),
        in_specs=[anywhere, anywhere, anywhere],
        out_specs=vmem,
        scratch_shapes=[
            pltpu.VMEM((2 * modes, time_cols), f32),
            pltpu.VMEM((2 * modes, time_cols), jnp.bfloat16),
            pltpu.VMEM((2 * modes, time_cols), jnp.bfloat16),
            pltpu.VMEM((2 * modes, half), f32),
            pltpu.VMEM((2 * outs, half), f32),
            pltpu.VMEM((ways, chips - 1, unit, time_cols), f32),
            pltpu.VMEM((ways, chips - 1, unit, time_cols), f32),
            pltpu.VMEM((chips, ways, unit, time_cols), f32),
            pltpu.VMEM((2 * outs, time_cols), f32),
            pltpu.VMEM((outs, time_cols), f32),
            dma((2,)),
            dma((3,)),
            dma((3,)),
            dma((ways, chips)),
            dma((ways, chips)),
            dma((ways, chips)),
            dma((ways, chips - 1, SUBS)),
            dma((ways, chips - 1, SUBS)),
            dma((ways, chips - 1, SUBS)),
            dma((ways, chips - 1, SUBS)),
        ],
        compiler_params=pltpu.CompilerParams(
            collective_id=0, has_side_effects=True, vmem_limit_bytes=50 * 2**20
        ),
    )(histories, modal_map, recovery)


def shards(size, histories, modal_map, recovery):
    chips = size // 2
    time_cols, outs = histories.shape[1], recovery.shape[0]
    f32, vmem = jnp.float32, pl.BlockSpec(memory_space=pltpu.VMEM)
    if chips == 8:
        found = grid_call((GROUPS, PIECES, ORDERS), histories, modal_map, recovery)
    else:
        found = ring_call(chips, histories, modal_map, recovery)
    return pl.pallas_call(
        statistics,
        out_shape=(
            jax.ShapeDtypeStruct((outs, time_cols), f32),
            jax.ShapeDtypeStruct((CASES, outs), f32),
            jax.ShapeDtypeStruct((CASES, outs), f32),
        ),
        in_specs=[vmem], compiler_params=pltpu.CompilerParams(vmem_limit_bytes=8 * 2**20),
        out_specs=(vmem, vmem, vmem),
    )(found)


def solution(mesh):
    return jax.shard_map(
        functools.partial(shards, mesh.shape["rows"]),
        mesh=mesh,
        in_specs=(P(("grp", "rows"), None), P(("grp", "rows"), None), P(("grp", "rows"), None)),
        out_specs=(P(("grp", "rows"), None), P(None, ("grp", "rows")), P(None, ("grp", "rows"))),
        check_vma=False,
    )
```

```python
import functools

import jax
import jax.numpy as jnp
from jax import lax
from jax.experimental import pallas as pl
from jax.experimental.pallas import tpu as pltpu
from jax.sharding import PartitionSpec as P

CASES = 4
SUBS = 2
epsilon = 1e-06
MESH = pl.DeviceIdType.MESH


def split(x):
    high = x.astype(jnp.bfloat16)
    return high, (x - high.astype(jnp.float32)).astype(jnp.bfloat16)


def dot3(a, b, dims):
    mul = functools.partial(
        lax.dot_general, dimension_numbers=(dims, ((), ())), preferred_element_type=jnp.float32
    )
    return mul(a[0], b[0]) + (mul(a[0], b[1]) + mul(a[1], b[0]))


def ring_position(chips, chip):
    if chips == 8:
        z, y = chip // 2, chip % 2
        return y * (chips - 1 - 2 * z) + z
    return chip


def chip_at(chips, position):
    if chips == 8:
        y = position // 4
        return (y * (chips - 1 - 2 * position) + position) * 2 + y
    return position


def kernel(
    chips, ways, h_ref, m_ref, r_ref, out_ref,
    hist, hist_hi, hist_lo, m_buf, r_buf, part, landed, rows, acc, acc_other,
    local_sem, pair_send, pair_recv, m_local, m_send, m_recv, rs_send, rs_recv, ag_send, ag_recv,
):
    me = lax.axis_index("rows")
    core = me % 2
    partner = me + 1 - 2 * core
    pos = ring_position(chips, me // 2)
    after = chip_at(chips, (pos + 1) % chips) * 2 + core
    before = chip_at(chips, (pos + chips - 1) % chips) * 2 + core
    targets = (after, before)
    signs = (1, -1)

    modes, outs = h_ref.shape[0], r_ref.shape[0]
    half = m_ref.shape[1] // 2
    block = half // chips
    unit = block // ways
    piece = unit // SUBS
    cuts = SUBS if piece % 128 == 0 else 1
    width = unit // cuts

    def at(p):
        return (p + 2 * chips) % chips

    def cols(base, b, d, start=0, size=unit):
        return pl.ds(pl.multiple_of(base + b * block + d * unit + start, 128), size)

    def remote(src, dst, send, recv, to):
        return pltpu.make_async_remote_copy(
            src_ref=src, dst_ref=dst, send_sem=send, recv_sem=recv,
            device_id={"rows": to}, device_id_type=MESH,
        )

    def sum_block(k, d):
        return at(pos - signs[d] * (k + 1))

    def m_copy(k, d):
        b = sum_block(k, d)
        return remote(
            m_ref.at[:, cols((1 - core) * half, b, d)],
            m_buf.at[pl.ds(modes, modes), cols(0, b, d)],
            m_send.at[d, k], m_recv.at[d, k], partner,
        )

    def own_m(k, d):
        b = sum_block(k, d)
        return pltpu.make_async_copy(
            m_ref.at[:, cols(core * half, b, d)],
            m_buf.at[pl.ds(0, modes), cols(0, b, d)], m_local.at[d, k],
        )

    def rs_copy(k, d, j):
        view = (d, k, pl.ds(j * piece, piece))
        return remote(part.at[view], landed.at[view], rs_send.at[d, k, j], rs_recv.at[d, k, j], targets[d])

    def ag_copy(s, d, j, arrives=False):
        b = at(pos - signs[d] * (s + 1 if arrives else s))
        view = (b, d, pl.ds(j * piece, piece))
        return remote(rows.at[view], rows.at[view], ag_send.at[d, s, j], ag_recv.at[d, s, j], targets[d])

    own_h = pltpu.make_async_copy(h_ref, hist.at[pl.ds(0, modes)], local_sem.at[0])
    own_r = pltpu.make_async_copy(
        r_ref.at[:, pl.ds(pl.multiple_of(core * half, 128), half)],
        r_buf.at[pl.ds(0, outs)], local_sem.at[1],
    )
    h_copy = remote(h_ref, hist.at[pl.ds(modes, modes)], pair_send.at[0], pair_recv.at[0], partner)
    r_copy = remote(
        r_ref.at[:, pl.ds(pl.multiple_of((1 - core) * half, 128), half)],
        r_buf.at[pl.ds(outs, outs)], pair_send.at[1], pair_recv.at[1], partner,
    )
    acc_copy = remote(acc.at[pl.ds(outs, outs)], acc_other, pair_send.at[2], pair_recv.at[2], partner)

    own_h.start()
    for d in range(ways):
        own_m(0, d).start()
    barrier = pltpu.get_barrier_semaphore()
    for other in (after, before, partner):
        pl.semaphore_signal(barrier, inc=1, device_id={"rows": other}, device_id_type=MESH)
    pl.semaphore_wait(barrier, 3)

    h_copy.start()
    for d in range(ways):
        m_copy(0, d).start()

    @pl.loop(1, chips)
    def _(k):
        for d in range(ways):
            own_m(k, d).start()
            m_copy(k, d).start()

    own_h.wait()
    hist_hi[pl.ds(0, modes)], hist_lo[pl.ds(0, modes)] = split(hist[pl.ds(0, modes)])
    h_copy.wait_recv()
    hist_hi[pl.ds(modes, modes)], hist_lo[pl.ds(modes, modes)] = split(hist[pl.ds(modes, modes)])

    def shapes_here(k, d):
        own_m(k, d).wait()
        m_copy(k, d).wait_recv()

    def partial_rows(k, d, start=0, size=unit):
        shapes = split(m_buf[:, cols(0, sum_block(k, d), d, start, size)])
        return dot3(shapes, (hist_hi[...], hist_lo[...]), ((0,), (0,)))

    for cut in range(cuts):
        for d in range(ways):
            if cut == 0:
                shapes_here(0, d)
            start = cut * width
            part[d, 0, pl.ds(start, width)] = partial_rows(0, d, start, width)
            for j in range(cut * SUBS // cuts, (cut + 1) * SUBS // cuts):
                rs_copy(0, d, j).start()

    own_r.start()
    r_copy.start()

    @pl.loop(1, chips - 1)
    def _(k):
        for d in range(ways):
            shapes_here(k, d)
            part[d, k] = partial_rows(k, d)
        for j in range(SUBS):
            for d in range(ways):
                rs_copy(k - 1, d, j).wait_recv()
                view = (d, k, pl.ds(j * piece, piece))
                part[view] = part[view] + landed[d, k - 1, pl.ds(j * piece, piece)]
                rs_copy(k, d, j).start()

    last = chips - 1
    for d in range(ways):
        shapes_here(last, d)
        rows[pos, d] = partial_rows(last, d)
    for j in range(SUBS):
        for d in range(ways):
            rs_copy(last - 1, d, j).wait_recv()
            view = (pos, d, pl.ds(j * piece, piece))
            rows[view] = rows[view] + landed[d, last - 1, pl.ds(j * piece, piece)]
            ag_copy(0, d, j).start()

    own_r.wait()
    r_copy.wait_recv()

    def recovered(b, d):
        return dot3(split(r_buf[:, cols(0, b, d)]), split(rows[b, d]), ((1,), (0,)))

    acc[...] = recovered(pos, 0)
    for d in range(1, ways):
        acc[...] += recovered(pos, d)

    @pl.loop(0, chips - 2)
    def _(s):
        for j in range(SUBS):
            for d in range(ways):
                ag_copy(s, d, j, arrives=True).wait_recv()
                ag_copy(s + 1, d, j).start()
        for d in range(ways):
            acc[...] += recovered(at(pos - signs[d] * (s + 1)), d)

    for cut in range(cuts):
        for d in range(ways):
            for j in range(cut * SUBS // cuts, (cut + 1) * SUBS // cuts):
                ag_copy(chips - 2, d, j, arrives=True).wait_recv()
            b, start = at(pos - signs[d] * (chips - 1)), cut * width
            weights = split(r_buf[:, cols(0, b, d, start, width)])
            finished = split(rows[b, d, pl.ds(start, width)])
            final = cut == cuts - 1 and d == ways - 1
            for base in (outs, 0):
                own = tuple(w[base : base + outs] for w in weights)
                acc[pl.ds(base, outs)] += dot3(own, finished, ((1,), (0,)))
                if final and base:
                    acc_copy.start()

    h_copy.wait_send()
    r_copy.wait_send()

    @pl.loop(0, chips)
    def _(k):
        for d in range(ways):
            m_copy(k, d).wait_send()

    @pl.loop(0, chips - 1)
    def _(k):
        for d in range(ways):
            for j in range(SUBS):
                rs_copy(k, d, j).wait_send()
                ag_copy(k, d, j).wait_send()

    acc_copy.wait()
    out_ref[...] = acc[pl.ds(0, outs)] + acc_other[...]


def statistics(found_ref, out_ref, peak_ref, rms_ref):
    responses = found_ref[...]
    out_ref[...] = responses
    by_time = responses.T
    steps = by_time.shape[0] // CASES
    for k in range(CASES):
        case = by_time[k * steps : (k + 1) * steps]
        peak_ref[k : k + 1] = jnp.max(jnp.abs(case), axis=0, keepdims=True)
        mean = jnp.sum(case * case, axis=0, keepdims=True) / steps
        rms_ref[k : k + 1] = jnp.sqrt(mean + epsilon)


ACROSS, INWARD, OUTWARD = range(3)
H_ACROSS, H_RELAY, SHARE, PARTIAL, REDUCE, ROOT, GATHER, RECOVER, REDUCED, GATHERED = range(10)
ALONG_FIRST, ACROSS_FIRST = range(2)
GROUPS = (ACROSS_FIRST, ACROSS_FIRST, ACROSS_FIRST, ALONG_FIRST, ACROSS_FIRST, ACROSS_FIRST, ACROSS_FIRST, ALONG_FIRST)
PIECES = 4
ORDERS = (
    (
        (0,), (3, 3, 1), (4, 3, 1, 3, 1, ()), (3, 3, 0), (4, 3, 0, 3, 1, ()), (3, 7, 1), (4, 3, 1, 2, 0, ()),
        (3, 7, 0), (4, 3, 1, 0, 1, ()), (2, 0), (1,), (4, 3, 1, 1, 1, ()), (4, 3, 0, 2, 1, (0,)), (2, 1),
        (4, 3, 0, 0, 1, ()), (4, 3, 0, 1, 1, ()), (3, 0, 0), (4, 0, 0, 3, 1, ()), (2, 2), (4, 0, 0, 2, 1, ()),
        (4, 0, 0, 1, 1, ()), (3, 1, 0), (4, 1, 0, 2, 1, ()), (2, 4), (4, 1, 0, 3, 1, ()), (3, 2, 0),
        (4, 2, 0, 2, 1, ()), (7, 3, 0), (4, 2, 0, 3, 1, ()), (2, 5), (8, 3, 1, 3, 1), (5, 0, 0, 0, (1,)),
        (4, 2, 0, 0, 1, ()), (3, 4, 0), (8, 3, 0, 3, 1), (8, 3, 1, 2, 0), (4, 4, 0, 2, 1, ()), (8, 3, 1, 0, 1),
        (6, 0, 0, 0, 0), (4, 4, 0, 3, 1, ()), (8, 3, 1, 1, 1), (2, 6), (4, 7, 0, 3, 1, ()), (3, 5, 0),
        (8, 3, 0, 2, 1), (5, 1, 0, 1, (1,)), (4, 5, 0, 2, 1, ()), (8, 3, 0, 0, 1), (4, 4, 0, 0, 1, ()),
        (6, 0, 0, 2, 0), (8, 3, 0, 1, 1), (5, 1, 0, 0, (1,)), (4, 5, 0, 3, 1, ()), (6, 1, 0, 0, 0), (8, 0, 0, 3, 1),
        (3, 6, 0), (5, 2, 0, 1, (1,)), (4, 6, 0, 2, 1, ()), (6, 1, 0, 1, 0), (8, 0, 0, 2, 1), (4, 6, 0, 3, 1, ()),
        (6, 2, 0, 0, 0), (8, 0, 0, 1, 1), (5, 4, 0, 1, (1,)), (4, 7, 1, 2, 1, ()), (6, 4, 0, 1, 0), (8, 1, 0, 2, 1),
        (4, 7, 1, 3, 1, ()), (6, 2, 0, 1, 0), (8, 1, 0, 3, 1), (4, 5, 0, 0, 1, ()), (6, 3, 0, 1, 0), (8, 2, 0, 2, 1),
        (5, 5, 0, 1, (1,)), (4, 7, 0, 2, 1, ()), (6, 3, 0, 2, 0), (8, 2, 0, 3, 1), (4, 7, 1, 1, 1, ()),
        (6, 4, 0, 3, 0), (8, 2, 0, 0, 1), (6, 2, 0, 1, 1), (6, 5, 0, 1, 0), (8, 4, 0, 2, 1), (7, 3, 1),
        (9, 0, 0, 0, 0), (5, 6, 0, 1, (1,)), (6, 0, 1, 0, 1), (6, 6, 0, 1, 0), (8, 4, 0, 3, 1), (5, 6, 0, 0, (1,)),
        (6, 1, 0, 0, 1), (6, 6, 0, 0, 0), (8, 7, 0, 3, 1), (6, 5, 0, 1, 1), (6, 5, 0, 0, 0), (8, 5, 0, 2, 1),
        (6, 1, 0, 1, 1), (4, 7, 1, 0, 0, (1,)), (8, 4, 0, 0, 1), (9, 0, 0, 2, 0), (6, 4, 0, 1, 1), (6, 0, 0, 1, 0),
        (8, 5, 0, 3, 1), (9, 1, 0, 0, 0), (6, 6, 0, 0, 1), (6, 5, 0, 3, 0), (8, 6, 0, 2, 1), (9, 1, 0, 1, 0),
        (5, 7, 0, 0, (0,)), (5, 7, 0, 1, (1,)), (6, 6, 0, 1, 1), (6, 7, 0, 0, 0), (8, 6, 0, 3, 1), (9, 2, 0, 0, 0),
        (7, 2, 0), (6, 7, 0, 1, 1), (6, 2, 0, 2, 0), (8, 7, 1, 2, 1), (9, 4, 0, 1, 0), (7, 0, 1), (6, 7, 0, 0, 1),
        (6, 0, 1, 3, 0), (8, 7, 1, 3, 1), (9, 2, 0, 1, 0), (6, 7, 1, 0, 1), (6, 1, 0, 3, 0), (8, 5, 0, 0, 1),
        (9, 3, 0, 1, 0), (7, 2, 1), (6, 4, 1, 1, 1), (7, 5, 0), (8, 7, 0, 2, 1), (6, 5, 0, 2, 0), (9, 3, 0, 2, 0),
        (7, 0, 0), (6, 0, 0, 3, 1), (7, 1, 0), (8, 7, 1, 1, 1), (6, 1, 0, 2, 0), (9, 4, 0, 3, 0), (7, 4, 0),
        (6, 0, 1, 2, 1), (6, 4, 0, 2, 0), (9, 2, 0, 1, 1), (9, 5, 0, 1, 0), (7, 5, 1), (6, 5, 1, 2, 1),
        (6, 7, 0, 1, 0), (9, 0, 1, 0, 1), (9, 6, 0, 1, 0), (7, 1, 1), (6, 5, 1, 3, 1), (7, 6, 0), (9, 1, 0, 0, 1),
        (6, 6, 0, 2, 0), (9, 6, 0, 0, 0), (7, 4, 1), (6, 1, 1, 3, 1), (6, 7, 0, 2, 0), (9, 5, 0, 1, 1),
        (9, 5, 0, 0, 0), (9, 1, 0, 1, 1), (8, 7, 1, 0, 0), (7, 6, 1), (7, 7, 0), (9, 4, 0, 1, 1), (9, 0, 0, 1, 0),
        (7, 7, 1), (9, 6, 0, 0, 1), (9, 5, 0, 3, 0), (9, 6, 0, 1, 1), (9, 7, 0, 0, 0), (9, 7, 0, 1, 1),
        (9, 2, 0, 2, 0), (9, 7, 0, 0, 1), (9, 0, 1, 3, 0), (9, 7, 1, 0, 1), (9, 1, 0, 3, 0), (9, 4, 1, 1, 1),
        (9, 5, 0, 2, 0), (9, 0, 0, 3, 1), (9, 1, 0, 2, 0), (9, 0, 1, 2, 1), (9, 4, 0, 2, 0), (9, 5, 1, 2, 1),
        (9, 7, 0, 1, 0), (9, 5, 1, 3, 1), (9, 6, 0, 2, 0), (9, 1, 1, 3, 1), (9, 7, 0, 2, 0),
    ),
    (
        (0,), (3, 3, 1), (4, 3, 1, 2, 1, ()), (3, 3, 0), (3, 7, 1), (2, 0), (3, 7, 0), (4, 3, 1, 3, 1, (2,)), (1,),
        (4, 3, 0, 3, 1, (2,)), (4, 7, 0, 0, 0, ()), (4, 3, 1, 0, 0, (1, 2)), (3, 0, 0), (4, 3, 1, 1, 0, (1, 2)),
        (4, 3, 0, 2, 1, (2,)), (2, 1), (5, 3, 0, 0, (0, 1, 2)), (6, 3, 0, 0, 2), (6, 3, 0, 0, 1),
        (5, 3, 0, 1, (0, 1, 2)), (6, 3, 0, 1, 2), (6, 3, 0, 1, 1), (6, 3, 0, 0, 0), (4, 0, 0, 3, 1, (2,)),
        (6, 3, 0, 3, 2), (2, 2), (4, 0, 0, 2, 1, (2,)), (6, 3, 0, 2, 2), (7, 3, 0), (3, 1, 0), (4, 0, 0, 0, 2, (1,)),
        (6, 3, 1, 0, 1), (6, 3, 1, 0, 2), (4, 1, 0, 2, 1, (2,)), (5, 0, 0, 1, (1, 2)), (2, 4), (6, 0, 0, 1, 2),
        (6, 0, 0, 1, 1), (8, 3, 1, 2, 1), (6, 3, 1, 3, 2), (4, 1, 0, 3, 1, (2,)), (3, 2, 0), (4, 1, 0, 1, 2, (1,)),
        (4, 2, 0, 2, 1, (2,)), (8, 3, 1, 3, 1), (2, 5), (6, 0, 0, 2, 2), (4, 2, 0, 3, 1, (2,)), (8, 3, 0, 3, 1),
        (4, 1, 0, 0, 2, (1,)), (8, 7, 0, 0, 0), (3, 4, 0), (4, 4, 0, 2, 1, (2,)), (4, 2, 0, 1, 2, (1,)),
        (8, 3, 1, 0, 0), (2, 6), (4, 4, 0, 3, 1, (2,)), (5, 2, 0, 0, (1, 2)), (6, 2, 0, 0, 2), (8, 3, 1, 1, 0),
        (6, 2, 0, 0, 1), (8, 3, 0, 2, 1), (3, 5, 0), (4, 4, 0, 1, 2, (1,)), (4, 5, 0, 2, 1, (2,)), (9, 3, 0, 0, 2),
        (9, 3, 0, 0, 1), (4, 7, 0, 3, 0, (2,)), (5, 4, 0, 0, (1, 2)), (9, 3, 0, 1, 2), (9, 3, 0, 1, 1),
        (6, 4, 0, 0, 1), (6, 4, 0, 0, 2), (6, 2, 0, 3, 0), (6, 2, 0, 3, 2), (4, 5, 0, 3, 1, (2,)), (8, 0, 0, 3, 1),
        (9, 3, 0, 3, 2), (3, 6, 0), (9, 3, 0, 0, 0), (6, 0, 0, 1, 0), (4, 5, 0, 1, 2, (1,)), (4, 6, 0, 2, 1, (2,)),
        (8, 0, 0, 2, 1), (9, 3, 0, 2, 2), (6, 4, 0, 3, 0), (6, 4, 0, 3, 2), (4, 6, 0, 3, 1, (2,)), (8, 0, 0, 0, 2),
        (9, 3, 1, 0, 1), (6, 3, 0, 1, 0), (6, 2, 1, 3, 2), (6, 2, 1, 3, 1), (9, 3, 1, 0, 2), (8, 1, 0, 2, 1),
        (4, 7, 1, 2, 0, (2,)), (4, 6, 0, 1, 2, (1,)), (4, 7, 1, 3, 1, (0, 2)), (9, 0, 0, 1, 2), (9, 0, 0, 1, 1),
        (6, 3, 0, 2, 0), (4, 6, 0, 0, 2, (1,)), (6, 4, 1, 3, 1), (5, 5, 0, 0, (1, 2)), (9, 3, 1, 3, 2),
        (8, 1, 0, 3, 1), (6, 5, 0, 0, 0), (6, 5, 0, 0, 2), (6, 5, 0, 0, 1), (8, 1, 0, 1, 2), (8, 2, 0, 2, 1),
        (4, 7, 1, 0, 2, (0, 1)), (4, 7, 0, 2, 1, (0, 2)), (4, 7, 1, 1, 0, (2,)), (9, 0, 0, 2, 2), (7, 3, 1),
        (8, 2, 0, 3, 1), (6, 4, 1, 0, 2), (6, 2, 0, 1, 0), (6, 2, 0, 1, 1), (8, 1, 0, 0, 2), (8, 4, 0, 2, 1),
        (6, 5, 0, 3, 2), (6, 0, 1, 0, 0), (6, 0, 1, 0, 1), (8, 2, 0, 1, 2), (8, 4, 0, 3, 1), (4, 7, 0, 1, 2, (0, 1)),
        (6, 1, 0, 0, 1), (6, 1, 0, 0, 0), (9, 2, 0, 0, 2), (9, 2, 0, 0, 1), (7, 2, 0), (6, 2, 0, 2, 2),
        (6, 2, 0, 2, 0), (6, 5, 0, 1, 1), (8, 4, 0, 1, 2), (8, 5, 0, 2, 1), (6, 5, 0, 1, 0), (6, 0, 1, 3, 2),
        (6, 1, 0, 1, 1), (8, 7, 0, 3, 0), (9, 4, 0, 0, 1), (9, 4, 0, 0, 2), (6, 1, 0, 1, 0), (6, 1, 0, 3, 2),
        (6, 4, 0, 1, 1), (9, 2, 0, 3, 0), (9, 2, 0, 3, 2), (7, 2, 1), (8, 5, 0, 3, 1), (7, 5, 0), (6, 5, 0, 2, 2),
        (6, 6, 0, 0, 1), (6, 6, 0, 0, 0), (9, 0, 0, 1, 0), (8, 5, 0, 1, 2), (8, 6, 0, 2, 1), (7, 1, 0),
        (6, 1, 0, 2, 2), (6, 1, 0, 2, 0), (6, 6, 0, 1, 1), (9, 4, 0, 3, 0), (9, 4, 0, 3, 2), (8, 6, 0, 3, 1),
        (7, 4, 0), (6, 4, 0, 2, 2), (6, 7, 0, 1, 1), (6, 7, 0, 1, 0), (9, 3, 0, 1, 0), (9, 2, 1, 3, 2),
        (9, 2, 1, 3, 1), (6, 6, 0, 3, 0), (6, 6, 0, 3, 2), (6, 7, 0, 0, 1), (8, 7, 1, 2, 0), (8, 6, 0, 1, 2),
        (8, 7, 1, 3, 1), (7, 6, 0), (6, 6, 0, 2, 2), (6, 6, 0, 2, 0), (6, 7, 1, 0, 1), (9, 3, 0, 2, 0),
        (8, 6, 0, 0, 2), (9, 4, 1, 3, 1), (6, 7, 0, 2, 0), (6, 7, 0, 2, 2), (6, 4, 1, 1, 1), (9, 5, 0, 0, 0),
        (9, 5, 0, 0, 2), (9, 5, 0, 0, 1), (7, 7, 0), (6, 6, 1, 3, 2), (7, 0, 0), (8, 7, 1, 0, 2), (8, 7, 0, 2, 1),
        (8, 7, 1, 1, 0), (6, 6, 1, 2, 1), (6, 7, 0, 3, 2), (7, 0, 1), (9, 4, 1, 0, 2), (9, 2, 0, 1, 0),
        (9, 2, 0, 1, 1), (7, 7, 1), (6, 7, 1, 3, 2), (7, 4, 1), (9, 5, 0, 3, 2), (9, 0, 1, 0, 0), (9, 0, 1, 0, 1),
        (7, 6, 1), (7, 5, 1), (8, 7, 0, 1, 2), (9, 1, 0, 0, 1), (9, 1, 0, 0, 0), (7, 1, 1), (9, 2, 0, 2, 2),
        (9, 2, 0, 2, 0), (9, 5, 0, 1, 1), (9, 5, 0, 1, 0), (9, 0, 1, 3, 2), (9, 1, 0, 1, 1), (9, 1, 0, 1, 0),
        (9, 1, 0, 3, 2), (9, 4, 0, 1, 1), (9, 5, 0, 2, 2), (9, 6, 0, 0, 1), (9, 6, 0, 0, 0), (9, 1, 0, 2, 2),
        (9, 1, 0, 2, 0), (9, 6, 0, 1, 1), (9, 4, 0, 2, 2), (9, 7, 0, 1, 1), (9, 7, 0, 1, 0), (9, 6, 0, 3, 0),
        (9, 6, 0, 3, 2), (9, 7, 0, 0, 1), (9, 6, 0, 2, 2), (9, 6, 0, 2, 0), (9, 7, 1, 0, 1), (9, 7, 0, 2, 0),
        (9, 7, 0, 2, 2), (9, 4, 1, 1, 1), (9, 6, 1, 3, 2), (9, 6, 1, 2, 1), (9, 7, 0, 3, 2), (9, 7, 1, 3, 2),
    ),
)


def grid_kernel(
    plan, h_ref, m_ref, r_ref, out_ref,
    hist, hist_hi, hist_lo, m_wide, m_tall, r_buf, part, landed, rows, acc, acc_other,
    local_sem, pair_send, pair_recv, m_local, m_send, m_recv, rs_send, rs_recv, ag_send, ag_recv,
):
    groups, pieces, orders = plan
    count = len(groups)
    me = lax.axis_index("rows")
    core, y, z = me % 2, (me // 2) % 2, me // 4
    side = z // 2
    middle = (z + side) % 2
    inner, outer = z + 1 - 2 * side, z - 1 + 2 * side

    def device(at_z, at_y, at_core):
        return (at_z * 2 + at_y) * 2 + at_core

    partner = device(z, y, 1 - core)
    across, diagonal = device(z, 1 - y, core), device(z, 1 - y, 1 - core)
    target = (across, device(inner, y, core), device(outer, y, core))
    heading = (0, 1 + side, 2 - side)
    came = (0, 2 - side, 1 + side)

    modes, outs = h_ref.shape[0], r_ref.shape[0]
    half = m_ref.shape[1] // 2
    span = half // (2 * count)
    piece = span // pieces

    wide = [q for q in range(count) if groups[q] == ALONG_FIRST]
    tall = [q for q in range(count) if groups[q] == ACROSS_FIRST]

    def line(dy):
        return 1 - y if dy else y

    def place(j):
        return j + side * (pieces - 1 - 2 * j)

    def slot(q, dy):
        if groups[q] == ALONG_FIRST:
            return 2 * wide.index(q) + line(dy)
        return 2 * len(wide) + tall.index(q)

    def span_of(j):
        return pl.ds(pl.multiple_of(place(j) * piece, piece), piece)

    def remote(src, dst, send, recv, to):
        return pltpu.make_async_remote_copy(
            src_ref=src, dst_ref=dst, send_sem=send, recv_sem=recv,
            device_id={"rows": to}, device_id_type=MESH,
        )

    def shapes(q, at_core, at_y):
        if groups[q] == ALONG_FIRST:
            return m_ref.at[:, pl.ds(pl.multiple_of(at_core * half + 2 * q * span, 128), 2 * span)]
        return m_ref.at[:, pl.ds(pl.multiple_of(at_core * half + (2 * q + at_y) * span, 128), span)]

    def held(q, source):
        source = pl.ds(source * modes, modes)
        if groups[q] == ALONG_FIRST:
            return m_wide.at[wide.index(q), source]
        return m_tall.at[tall.index(q), source]

    def own_m(q):
        return pltpu.make_async_copy(shapes(q, core, y), held(q, 0), m_local.at[q])

    def m_pair(q):
        return remote(shapes(q, 1 - core, y), held(q, 1), m_send.at[q, 0], m_recv.at[q, 0], partner)

    def m_across(q):
        return tuple(
            remote(
                shapes(q, at_core, 1 - y), held(q, source),
                m_send.at[q, source - 1], m_recv.at[q, source - 1], to,
            )
            for source, to, at_core in ((2, across, core), (3, diagonal, 1 - core))
        )

    own_h = pltpu.make_async_copy(h_ref, hist.at[pl.ds(0, modes)], local_sem.at[0])
    h_pair = remote(h_ref, hist.at[pl.ds(modes, modes)], pair_send.at[0], pair_recv.at[0], partner)
    h_across = remote(h_ref, hist.at[pl.ds(2 * modes, modes)], pair_send.at[1], pair_recv.at[1], across)
    h_relay = remote(
        hist.at[pl.ds(2 * modes, modes)], hist.at[pl.ds(3 * modes, modes)],
        pair_send.at[2], pair_recv.at[2], partner,
    )
    own_r = pltpu.make_async_copy(
        r_ref.at[:, pl.ds(pl.multiple_of(core * half, 128), half)],
        r_buf.at[pl.ds(0, outs)], local_sem.at[1],
    )
    r_copy = remote(
        r_ref.at[:, pl.ds(pl.multiple_of((1 - core) * half, 128), half)],
        r_buf.at[pl.ds(outs, outs)], pair_send.at[3], pair_recv.at[3], partner,
    )
    acc_copy = remote(acc.at[pl.ds(outs, outs)], acc_other, pair_send.at[4], pair_recv.at[4], partner)

    def rs_copy(q, dy, j, to, d):
        k = slot(q, dy)
        return remote(
            part.at[k, span_of(j)], landed.at[k, d, span_of(j)],
            rs_send.at[k, place(j), d], rs_recv.at[k, place(j), d], target[to],
        )

    def ag_copy(q, dy, j, to):
        k = 2 * q + line(dy)
        view = rows.at[k, span_of(j)]
        return remote(
            view, view, ag_send.at[k, place(j), heading[to]], ag_recv.at[k, place(j)], target[to]
        )

    def hist_ready(first, size):
        here = pl.ds(first * modes, size * modes)
        hist_hi[here], hist_lo[here] = split(hist[here])

    def run(order):
        seen = set()

        def once(key):
            fresh = key not in seen
            seen.add(key)
            return fresh

        def row_ready(q, dy, j):
            if once((ROOT, q, dy, j)):
                ag_copy(q, dy, j, ACROSS).wait_recv()

        def summed(q, dy, j, kids):
            total = part[slot(q, dy), span_of(j)]
            for kid in kids:
                rs_copy(q, dy, j, ACROSS, came[kid]).wait_recv()
            for kid in kids:
                total = total + landed[slot(q, dy), came[kid], span_of(j)]
            return total

        recoveries = [op for op in order if op[0] == RECOVER]
        for op in order:
            name, args = op[0], op[1:]
            if name == H_ACROSS:
                h_across.start()
            elif name == H_RELAY:
                h_across.wait_recv()
                h_relay.start()
                own_r.start()
                r_copy.start()
            elif name == SHARE:
                for copy in m_across(*args):
                    copy.start()
            elif name == PARTIAL:
                q, dy = args
                if once(PARTIAL):
                    own_h.wait()
                    h_pair.wait_recv()
                    hist_ready(0, 2)
                if once((PARTIAL, q)):
                    own_m(q).wait()
                    m_pair(q).wait_recv()
                if groups[q] == ALONG_FIRST:
                    buf, known = m_wide.at[wide.index(q)], pl.ds(0, 2 * modes)
                    cols = pl.ds(pl.multiple_of(line(dy) * span, 128), span)
                else:
                    if once(SHARE):
                        h_relay.wait_recv()
                        hist_ready(2, 2)
                    for copy in m_across(q):
                        copy.wait_recv()
                    buf, known, cols = m_tall.at[tall.index(q)], pl.ds(0, 4 * modes), pl.ds(0, span)
                part[slot(q, dy)] = dot3(split(buf[:, cols]), (hist_hi[known], hist_lo[known]), ((0,), (0,)))
            elif name == REDUCE:
                q, dy, j, to, kids = args
                if kids:
                    part[slot(q, dy), span_of(j)] = summed(q, dy, j, kids)
                rs_copy(q, dy, j, to, heading[to]).start()
            elif name == ROOT:
                q, dy, j, kids = args
                seen.add((ROOT, q, dy, j))
                rows[2 * q + line(dy), span_of(j)] = summed(q, dy, j, kids)
            elif name == GATHER:
                row_ready(*args[:3])
                ag_copy(*args).start()
            elif name == REDUCED:
                rs_copy(*args, heading[args[-1]]).wait_send()
            elif name == GATHERED:
                ag_copy(*args).wait_send()
            elif name == RECOVER:
                q, dy = args
                for j in range(pieces):
                    row_ready(q, dy, j)
                if once(RECOVER):
                    own_r.wait()
                    r_copy.wait_recv()
                known = 2 * q + line(dy)
                cols = pl.ds(pl.multiple_of(known * span, 128), span)
                values = split(rows[known])
                for base in (outs, 0):
                    here = pl.ds(base, outs)
                    added = dot3(split(r_buf[here, cols]), values, ((1,), (0,)))
                    acc[here] = added if op is recoveries[0] else acc[here] + added
                    if op is recoveries[-1] and base:
                        acc_copy.start()

    own_h.start()
    for q in wide + tall:
        own_m(q).start()
    barrier = pltpu.get_barrier_semaphore()
    for other in (partner, across, diagonal, target[INWARD]):
        pl.semaphore_signal(barrier, inc=1, device_id={"rows": other}, device_id_type=MESH)

    @pl.when(middle == 1)
    def _():
        pl.semaphore_signal(barrier, inc=1, device_id={"rows": target[OUTWARD]}, device_id_type=MESH)

    pl.semaphore_wait(barrier, 4 + middle)
    h_pair.start()
    for q in wide + tall:
        m_pair(q).start()

    for role in range(2):
        pl.when(middle == role)(functools.partial(run, orders[role]))

    h_pair.wait_send()
    h_across.wait_send()
    h_relay.wait_send()
    r_copy.wait_send()
    for q in range(count):
        m_pair(q).wait_send()
    for q in tall:
        for copy in m_across(q):
            copy.wait_send()
    acc_copy.wait()
    acc_other[...] = acc[pl.ds(0, outs)] + acc_other[...]
    found = pltpu.make_async_copy(acc_other, out_ref, local_sem.at[0])
    found.start()
    found.wait()


def grid_call(plan, histories, modal_map, recovery):
    modes, time_cols = histories.shape
    outs, dofs = recovery.shape
    groups, pieces, _ = plan
    half, count = dofs // 2, len(groups)
    span = half // (2 * count)
    n_wide, n_tall = groups.count(ALONG_FIRST), groups.count(ACROSS_FIRST)
    slots = 2 * n_wide + n_tall
    f32, dma = jnp.float32, pltpu.SemaphoreType.DMA
    anywhere = pl.BlockSpec(memory_space=pltpu.HBM)
    return pl.pallas_call(
        functools.partial(grid_kernel, plan),
        out_shape=jax.ShapeDtypeStruct((outs, time_cols), f32),
        in_specs=[anywhere, anywhere, anywhere],
        out_specs=pl.BlockSpec(memory_space=pl.ANY),
        scratch_shapes=[
            pltpu.VMEM((4 * modes, time_cols), f32),
            pltpu.VMEM((4 * modes, time_cols), jnp.bfloat16),
            pltpu.VMEM((4 * modes, time_cols), jnp.bfloat16),
            pltpu.VMEM((n_wide, 2 * modes, 2 * span), f32),
            pltpu.VMEM((n_tall, 4 * modes, span), f32),
            pltpu.VMEM((2 * outs, half), f32),
            pltpu.VMEM((slots, span, time_cols), f32),
            pltpu.VMEM((slots, 3, span, time_cols), f32),
            pltpu.VMEM((2 * count, span, time_cols), f32),
            pltpu.VMEM((2 * outs, time_cols), f32),
            pltpu.VMEM((outs, time_cols), f32),
            dma((2,)),
            dma((5,)),
            dma((5,)),
            dma((count,)),
            dma((count, 3)),
            dma((count, 3)),
            dma((slots, pieces, 3)),
            dma((slots, pieces, 3)),
            dma((2 * count, pieces, 3)),
            dma((2 * count, pieces)),
        ],
        compiler_params=pltpu.CompilerParams(
            collective_id=1, has_side_effects=True, vmem_limit_bytes=52 * 2**20
        ),
    )(histories, modal_map, recovery)


def ring_call(chips, histories, modal_map, recovery):
    modes, time_cols = histories.shape
    outs, dofs = recovery.shape
    half = dofs // 2
    block = half // chips
    ways = 2 if block % 256 == 0 else 1
    unit = block // ways
    f32, dma = jnp.float32, pltpu.SemaphoreType.DMA
    vmem, anywhere = pl.BlockSpec(memory_space=pltpu.VMEM), pl.BlockSpec(memory_space=pltpu.HBM)
    return pl.pallas_call(
        functools.partial(kernel, chips, ways),
        out_shape=jax.ShapeDtypeStruct((outs, time_cols), f32),
        in_specs=[anywhere, anywhere, anywhere],
        out_specs=vmem,
        scratch_shapes=[
            pltpu.VMEM((2 * modes, time_cols), f32),
            pltpu.VMEM((2 * modes, time_cols), jnp.bfloat16),
            pltpu.VMEM((2 * modes, time_cols), jnp.bfloat16),
            pltpu.VMEM((2 * modes, half), f32),
            pltpu.VMEM((2 * outs, half), f32),
            pltpu.VMEM((ways, chips - 1, unit, time_cols), f32),
            pltpu.VMEM((ways, chips - 1, unit, time_cols), f32),
            pltpu.VMEM((chips, ways, unit, time_cols), f32),
            pltpu.VMEM((2 * outs, time_cols), f32),
            pltpu.VMEM((outs, time_cols), f32),
            dma((2,)),
            dma((3,)),
            dma((3,)),
            dma((ways, chips)),
            dma((ways, chips)),
            dma((ways, chips)),
            dma((ways, chips - 1, SUBS)),
            dma((ways, chips - 1, SUBS)),
            dma((ways, chips - 1, SUBS)),
            dma((ways, chips - 1, SUBS)),
        ],
        compiler_params=pltpu.CompilerParams(
            collective_id=0, has_side_effects=True, vmem_limit_bytes=50 * 2**20
        ),
    )(histories, modal_map, recovery)


def shards(size, histories, modal_map, recovery):
    chips = size // 2
    time_cols, outs = histories.shape[1], recovery.shape[0]
    f32, vmem = jnp.float32, pl.BlockSpec(memory_space=pltpu.VMEM)
    if chips == 8:
        found = grid_call((GROUPS, PIECES, ORDERS), histories, modal_map, recovery)
    else:
        found = ring_call(chips, histories, modal_map, recovery)
    return pl.pallas_call(
        statistics,
        out_shape=(
            jax.ShapeDtypeStruct((outs, time_cols), f32),
            jax.ShapeDtypeStruct((CASES, outs), f32),
            jax.ShapeDtypeStruct((CASES, outs), f32),
        ),
        in_specs=[vmem], compiler_params=pltpu.CompilerParams(vmem_limit_bytes=8 * 2**20),
        out_specs=(vmem, vmem, vmem),
    )(found)


def solution(mesh):
    return jax.shard_map(
        functools.partial(shards, mesh.shape["rows"]),
        mesh=mesh,
        in_specs=(P(("grp", "rows"), None), P(("grp", "rows"), None), P(("grp", "rows"), None)),
        out_specs=(P(("grp", "rows"), None), P(None, ("grp", "rows")), P(None, ("grp", "rows"))),
        check_vma=False,
    )
```

```python
import functools

import jax
import jax.numpy as jnp
from jax import lax
from jax.experimental import pallas as pl
from jax.experimental.pallas import tpu as pltpu
from jax.sharding import PartitionSpec as P

CASES = 4
SUBS = 2
epsilon = 1e-06
MESH = pl.DeviceIdType.MESH


def split(x):
    high = x.astype(jnp.bfloat16)
    return high, (x - high.astype(jnp.float32)).astype(jnp.bfloat16)


def dot3(a, b, dims):
    mul = functools.partial(
        lax.dot_general, dimension_numbers=(dims, ((), ())), preferred_element_type=jnp.float32
    )
    return mul(a[0], b[0]) + (mul(a[0], b[1]) + mul(a[1], b[0]))


def ring_position(chips, chip):
    if chips == 8:
        z, y = chip // 2, chip % 2
        return y * (chips - 1 - 2 * z) + z
    return chip


def chip_at(chips, position):
    if chips == 8:
        y = position // 4
        return (y * (chips - 1 - 2 * position) + position) * 2 + y
    return position


def kernel(
    chips, ways, h_ref, m_ref, r_ref, out_ref,
    hist, hist_hi, hist_lo, m_buf, r_buf, part, landed, rows, acc, acc_other,
    local_sem, pair_send, pair_recv, m_local, m_send, m_recv, rs_send, rs_recv, ag_send, ag_recv,
):
    me = lax.axis_index("rows")
    core = me % 2
    partner = me + 1 - 2 * core
    pos = ring_position(chips, me // 2)
    after = chip_at(chips, (pos + 1) % chips) * 2 + core
    before = chip_at(chips, (pos + chips - 1) % chips) * 2 + core
    targets = (after, before)
    signs = (1, -1)

    modes, outs = h_ref.shape[0], r_ref.shape[0]
    half = m_ref.shape[1] // 2
    block = half // chips
    unit = block // ways
    piece = unit // SUBS
    cuts = SUBS if piece % 128 == 0 else 1
    width = unit // cuts

    def at(p):
        return (p + 2 * chips) % chips

    def cols(base, b, d, start=0, size=unit):
        return pl.ds(pl.multiple_of(base + b * block + d * unit + start, 128), size)

    def remote(src, dst, send, recv, to):
        return pltpu.make_async_remote_copy(
            src_ref=src, dst_ref=dst, send_sem=send, recv_sem=recv,
            device_id={"rows": to}, device_id_type=MESH,
        )

    def sum_block(k, d):
        return at(pos - signs[d] * (k + 1))

    def m_copy(k, d):
        b = sum_block(k, d)
        return remote(
            m_ref.at[:, cols((1 - core) * half, b, d)],
            m_buf.at[pl.ds(modes, modes), cols(0, b, d)],
            m_send.at[d, k], m_recv.at[d, k], partner,
        )

    def own_m(k, d):
        b = sum_block(k, d)
        return pltpu.make_async_copy(
            m_ref.at[:, cols(core * half, b, d)],
            m_buf.at[pl.ds(0, modes), cols(0, b, d)], m_local.at[d, k],
        )

    def rs_copy(k, d, j):
        view = (d, k, pl.ds(j * piece, piece))
        return remote(part.at[view], landed.at[view], rs_send.at[d, k, j], rs_recv.at[d, k, j], targets[d])

    def ag_copy(s, d, j, arrives=False):
        b = at(pos - signs[d] * (s + 1 if arrives else s))
        view = (b, d, pl.ds(j * piece, piece))
        return remote(rows.at[view], rows.at[view], ag_send.at[d, s, j], ag_recv.at[d, s, j], targets[d])

    own_h = pltpu.make_async_copy(h_ref, hist.at[pl.ds(0, modes)], local_sem.at[0])
    own_r = pltpu.make_async_copy(
        r_ref.at[:, pl.ds(pl.multiple_of(core * half, 128), half)],
        r_buf.at[pl.ds(0, outs)], local_sem.at[1],
    )
    h_copy = remote(h_ref, hist.at[pl.ds(modes, modes)], pair_send.at[0], pair_recv.at[0], partner)
    r_copy = remote(
        r_ref.at[:, pl.ds(pl.multiple_of((1 - core) * half, 128), half)],
        r_buf.at[pl.ds(outs, outs)], pair_send.at[1], pair_recv.at[1], partner,
    )
    acc_copy = remote(acc.at[pl.ds(outs, outs)], acc_other, pair_send.at[2], pair_recv.at[2], partner)

    own_h.start()
    for d in range(ways):
        own_m(0, d).start()
    barrier = pltpu.get_barrier_semaphore()
    for other in (after, before, partner):
        pl.semaphore_signal(barrier, inc=1, device_id={"rows": other}, device_id_type=MESH)
    pl.semaphore_wait(barrier, 3)

    h_copy.start()
    for d in range(ways):
        m_copy(0, d).start()

    @pl.loop(1, chips)
    def _(k):
        for d in range(ways):
            own_m(k, d).start()
            m_copy(k, d).start()

    own_h.wait()
    hist_hi[pl.ds(0, modes)], hist_lo[pl.ds(0, modes)] = split(hist[pl.ds(0, modes)])
    h_copy.wait_recv()
    hist_hi[pl.ds(modes, modes)], hist_lo[pl.ds(modes, modes)] = split(hist[pl.ds(modes, modes)])

    def shapes_here(k, d):
        own_m(k, d).wait()
        m_copy(k, d).wait_recv()

    def partial_rows(k, d, start=0, size=unit):
        shapes = split(m_buf[:, cols(0, sum_block(k, d), d, start, size)])
        return dot3(shapes, (hist_hi[...], hist_lo[...]), ((0,), (0,)))

    for cut in range(cuts):
        for d in range(ways):
            if cut == 0:
                shapes_here(0, d)
            start = cut * width
            part[d, 0, pl.ds(start, width)] = partial_rows(0, d, start, width)
            for j in range(cut * SUBS // cuts, (cut + 1) * SUBS // cuts):
                rs_copy(0, d, j).start()

    own_r.start()
    r_copy.start()

    @pl.loop(1, chips - 1)
    def _(k):
        for d in range(ways):
            shapes_here(k, d)
            part[d, k] = partial_rows(k, d)
        for j in range(SUBS):
            for d in range(ways):
                rs_copy(k - 1, d, j).wait_recv()
                view = (d, k, pl.ds(j * piece, piece))
                part[view] = part[view] + landed[d, k - 1, pl.ds(j * piece, piece)]
                rs_copy(k, d, j).start()

    last = chips - 1
    for d in range(ways):
        shapes_here(last, d)
        rows[pos, d] = partial_rows(last, d)
    for j in range(SUBS):
        for d in range(ways):
            rs_copy(last - 1, d, j).wait_recv()
            view = (pos, d, pl.ds(j * piece, piece))
            rows[view] = rows[view] + landed[d, last - 1, pl.ds(j * piece, piece)]
            ag_copy(0, d, j).start()

    own_r.wait()
    r_copy.wait_recv()

    def recovered(b, d):
        return dot3(split(r_buf[:, cols(0, b, d)]), split(rows[b, d]), ((1,), (0,)))

    acc[...] = recovered(pos, 0)
    for d in range(1, ways):
        acc[...] += recovered(pos, d)

    @pl.loop(0, chips - 2)
    def _(s):
        for j in range(SUBS):
            for d in range(ways):
                ag_copy(s, d, j, arrives=True).wait_recv()
                ag_copy(s + 1, d, j).start()
        for d in range(ways):
            acc[...] += recovered(at(pos - signs[d] * (s + 1)), d)

    for cut in range(cuts):
        for d in range(ways):
            for j in range(cut * SUBS // cuts, (cut + 1) * SUBS // cuts):
                ag_copy(chips - 2, d, j, arrives=True).wait_recv()
            b, start = at(pos - signs[d] * (chips - 1)), cut * width
            weights = split(r_buf[:, cols(0, b, d, start, width)])
            finished = split(rows[b, d, pl.ds(start, width)])
            final = cut == cuts - 1 and d == ways - 1
            for base in (outs, 0):
                own = tuple(w[base : base + outs] for w in weights)
                acc[pl.ds(base, outs)] += dot3(own, finished, ((1,), (0,)))
                if final and base:
                    acc_copy.start()

    h_copy.wait_send()
    r_copy.wait_send()

    @pl.loop(0, chips)
    def _(k):
        for d in range(ways):
            m_copy(k, d).wait_send()

    @pl.loop(0, chips - 1)
    def _(k):
        for d in range(ways):
            for j in range(SUBS):
                rs_copy(k, d, j).wait_send()
                ag_copy(k, d, j).wait_send()

    acc_copy.wait()
    out_ref[...] = acc[pl.ds(0, outs)] + acc_other[...]


def statistics(found_ref, out_ref, peak_ref, rms_ref):
    responses = found_ref[...]
    out_ref[...] = responses
    by_time = responses.T
    steps = by_time.shape[0] // CASES
    for k in range(CASES):
        case = by_time[k * steps : (k + 1) * steps]
        peak_ref[k : k + 1] = jnp.max(jnp.abs(case), axis=0, keepdims=True)
        mean = jnp.sum(case * case, axis=0, keepdims=True) / steps
        rms_ref[k : k + 1] = jnp.sqrt(mean + epsilon)


ACROSS, INWARD, OUTWARD = range(3)
H_ACROSS, H_RELAY, SHARE, PARTIAL, REDUCE, ROOT, GATHER, RECOVER, REDUCED, GATHERED = range(10)
ALONG_FIRST, ACROSS_FIRST = range(2)
GROUPS = (ACROSS_FIRST, ACROSS_FIRST, ACROSS_FIRST, ALONG_FIRST, ACROSS_FIRST, ACROSS_FIRST, ACROSS_FIRST, ALONG_FIRST)
PIECES = 4
ORDERS = (
    (
        (0,), (3, 3, 1), (4, 3, 1, 3, 1, ()), (3, 3, 0), (4, 3, 0, 3, 1, ()), (3, 7, 1), (4, 3, 1, 2, 0, ()),
        (3, 7, 0), (4, 3, 1, 0, 1, ()), (2, 0), (1,), (4, 3, 1, 1, 1, ()), (4, 3, 0, 2, 1, (0,)), (2, 1),
        (4, 3, 0, 0, 1, ()), (4, 3, 0, 1, 1, ()), (3, 0, 0), (4, 0, 0, 3, 1, ()), (2, 2), (4, 0, 0, 2, 1, ()),
        (4, 0, 0, 1, 1, ()), (3, 1, 0), (4, 1, 0, 2, 1, ()), (2, 4), (4, 1, 0, 3, 1, ()), (3, 2, 0),
        (4, 2, 0, 2, 1, ()), (7, 3, 0), (4, 2, 0, 3, 1, ()), (2, 5), (8, 3, 1, 3, 1), (5, 0, 0, 0, (1,)),
        (4, 2, 0, 0, 1, ()), (3, 4, 0), (8, 3, 0, 3, 1), (8, 3, 1, 2, 0), (4, 4, 0, 2, 1, ()), (8, 3, 1, 0, 1),
        (6, 0, 0, 0, 0), (4, 4, 0, 3, 1, ()), (8, 3, 1, 1, 1), (2, 6), (4, 7, 0, 3, 1, ()), (3, 5, 0),
        (8, 3, 0, 2, 1), (5, 1, 0, 1, (1,)), (4, 5, 0, 2, 1, ()), (8, 3, 0, 0, 1), (4, 4, 0, 0, 1, ()),
        (6, 0, 0, 2, 0), (8, 3, 0, 1, 1), (5, 1, 0, 0, (1,)), (4, 5, 0, 3, 1, ()), (6, 1, 0, 0, 0), (8, 0, 0, 3, 1),
        (3, 6, 0), (5, 2, 0, 1, (1,)), (4, 6, 0, 2, 1, ()), (6, 1, 0, 1, 0), (8, 0, 0, 2, 1), (4, 6, 0, 3, 1, ()),
        (6, 2, 0, 0, 0), (8, 0, 0, 1, 1), (5, 4, 0, 1, (1,)), (4, 7, 1, 2, 1, ()), (6, 4, 0, 1, 0), (8, 1, 0, 2, 1),
        (4, 7, 1, 3, 1, ()), (6, 2, 0, 1, 0), (8, 1, 0, 3, 1), (4, 5, 0, 0, 1, ()), (6, 3, 0, 1, 0), (8, 2, 0, 2, 1),
        (5, 5, 0, 1, (1,)), (4, 7, 0, 2, 1, ()), (6, 3, 0, 2, 0), (8, 2, 0, 3, 1), (4, 7, 1, 1, 1, ()),
        (6, 4, 0, 3, 0), (8, 2, 0, 0, 1), (6, 2, 0, 1, 1), (6, 5, 0, 1, 0), (8, 4, 0, 2, 1), (7, 3, 1),
        (9, 0, 0, 0, 0), (5, 6, 0, 1, (1,)), (6, 0, 1, 0, 1), (6, 6, 0, 1, 0), (8, 4, 0, 3, 1), (5, 6, 0, 0, (1,)),
        (6, 1, 0, 0, 1), (6, 6, 0, 0, 0), (8, 7, 0, 3, 1), (6, 5, 0, 1, 1), (6, 5, 0, 0, 0), (8, 5, 0, 2, 1),
        (6, 1, 0, 1, 1), (4, 7, 1, 0, 0, (1,)), (8, 4, 0, 0, 1), (9, 0, 0, 2, 0), (6, 4, 0, 1, 1), (6, 0, 0, 1, 0),
        (8, 5, 0, 3, 1), (9, 1, 0, 0, 0), (6, 6, 0, 0, 1), (6, 5, 0, 3, 0), (8, 6, 0, 2, 1), (9, 1, 0, 1, 0),
        (5, 7, 0, 0, (0,)), (5, 7, 0, 1, (1,)), (6, 6, 0, 1, 1), (6, 7, 0, 0, 0), (8, 6, 0, 3, 1), (9, 2, 0, 0, 0),
        (7, 2, 0), (6, 7, 0, 1, 1), (6, 2, 0, 2, 0), (8, 7, 1, 2, 1), (9, 4, 0, 1, 0), (7, 0, 1), (6, 7, 0, 0, 1),
        (6, 0, 1, 3, 0), (8, 7, 1, 3, 1), (9, 2, 0, 1, 0), (6, 7, 1, 0, 1), (6, 1, 0, 3, 0), (8, 5, 0, 0, 1),
        (9, 3, 0, 1, 0), (7, 2, 1), (6, 4, 1, 1, 1), (7, 5, 0), (8, 7, 0, 2, 1), (6, 5, 0, 2, 0), (9, 3, 0, 2, 0),
        (7, 0, 0), (6, 0, 0, 3, 1), (7, 1, 0), (8, 7, 1, 1, 1), (6, 1, 0, 2, 0), (9, 4, 0, 3, 0), (7, 4, 0),
        (6, 0, 1, 2, 1), (6, 4, 0, 2, 0), (9, 2, 0, 1, 1), (9, 5, 0, 1, 0), (7, 5, 1), (6, 5, 1, 2, 1),
        (6, 7, 0, 1, 0), (9, 0, 1, 0, 1), (9, 6, 0, 1, 0), (7, 1, 1), (6, 5, 1, 3, 1), (7, 6, 0), (9, 1, 0, 0, 1),
        (6, 6, 0, 2, 0), (9, 6, 0, 0, 0), (7, 4, 1), (6, 1, 1, 3, 1), (6, 7, 0, 2, 0), (9, 5, 0, 1, 1),
        (9, 5, 0, 0, 0), (9, 1, 0, 1, 1), (8, 7, 1, 0, 0), (7, 6, 1), (7, 7, 0), (9, 4, 0, 1, 1), (9, 0, 0, 1, 0),
        (7, 7, 1), (9, 6, 0, 0, 1), (9, 5, 0, 3, 0), (9, 6, 0, 1, 1), (9, 7, 0, 0, 0), (9, 7, 0, 1, 1),
        (9, 2, 0, 2, 0), (9, 7, 0, 0, 1), (9, 0, 1, 3, 0), (9, 7, 1, 0, 1), (9, 1, 0, 3, 0), (9, 4, 1, 1, 1),
        (9, 5, 0, 2, 0), (9, 0, 0, 3, 1), (9, 1, 0, 2, 0), (9, 0, 1, 2, 1), (9, 4, 0, 2, 0), (9, 5, 1, 2, 1),
        (9, 7, 0, 1, 0), (9, 5, 1, 3, 1), (9, 6, 0, 2, 0), (9, 1, 1, 3, 1), (9, 7, 0, 2, 0),
    ),
    (
        (0,), (3, 3, 1), (4, 3, 1, 2, 1, ()), (3, 3, 0), (3, 7, 1), (2, 0), (3, 7, 0), (4, 3, 1, 3, 1, (2,)), (1,),
        (4, 3, 0, 3, 1, (2,)), (4, 7, 0, 0, 0, ()), (4, 3, 1, 0, 0, (1, 2)), (3, 0, 0), (4, 3, 1, 1, 0, (1, 2)),
        (4, 3, 0, 2, 1, (2,)), (2, 1), (5, 3, 0, 0, (0, 1, 2)), (6, 3, 0, 0, 2), (6, 3, 0, 0, 1),
        (5, 3, 0, 1, (0, 1, 2)), (6, 3, 0, 1, 2), (6, 3, 0, 1, 1), (6, 3, 0, 0, 0), (4, 0, 0, 3, 1, (2,)),
        (6, 3, 0, 3, 2), (2, 2), (4, 0, 0, 2, 1, (2,)), (6, 3, 0, 2, 2), (7, 3, 0), (3, 1, 0), (4, 0, 0, 0, 2, (1,)),
        (6, 3, 1, 0, 1), (6, 3, 1, 0, 2), (4, 1, 0, 2, 1, (2,)), (5, 0, 0, 1, (1, 2)), (2, 4), (6, 0, 0, 1, 2),
        (6, 0, 0, 1, 1), (8, 3, 1, 2, 1), (6, 3, 1, 3, 2), (4, 1, 0, 3, 1, (2,)), (3, 2, 0), (4, 1, 0, 1, 2, (1,)),
        (4, 2, 0, 2, 1, (2,)), (8, 3, 1, 3, 1), (2, 5), (6, 0, 0, 2, 2), (4, 2, 0, 3, 1, (2,)), (8, 3, 0, 3, 1),
        (4, 1, 0, 0, 2, (1,)), (8, 7, 0, 0, 0), (3, 4, 0), (4, 4, 0, 2, 1, (2,)), (4, 2, 0, 1, 2, (1,)),
        (8, 3, 1, 0, 0), (2, 6), (4, 4, 0, 3, 1, (2,)), (5, 2, 0, 0, (1, 2)), (6, 2, 0, 0, 2), (8, 3, 1, 1, 0),
        (6, 2, 0, 0, 1), (8, 3, 0, 2, 1), (3, 5, 0), (4, 4, 0, 1, 2, (1,)), (4, 5, 0, 2, 1, (2,)), (9, 3, 0, 0, 2),
        (9, 3, 0, 0, 1), (4, 7, 0, 3, 0, (2,)), (5, 4, 0, 0, (1, 2)), (9, 3, 0, 1, 2), (9, 3, 0, 1, 1),
        (6, 4, 0, 0, 1), (6, 4, 0, 0, 2), (6, 2, 0, 3, 0), (6, 2, 0, 3, 2), (4, 5, 0, 3, 1, (2,)), (8, 0, 0, 3, 1),
        (9, 3, 0, 3, 2), (3, 6, 0), (9, 3, 0, 0, 0), (6, 0, 0, 1, 0), (4, 5, 0, 1, 2, (1,)), (4, 6, 0, 2, 1, (2,)),
        (8, 0, 0, 2, 1), (9, 3, 0, 2, 2), (6, 4, 0, 3, 0), (6, 4, 0, 3, 2), (4, 6, 0, 3, 1, (2,)), (8, 0, 0, 0, 2),
        (9, 3, 1, 0, 1), (6, 3, 0, 1, 0), (6, 2, 1, 3, 2), (6, 2, 1, 3, 1), (9, 3, 1, 0, 2), (8, 1, 0, 2, 1),
        (4, 7, 1, 2, 0, (2,)), (4, 6, 0, 1, 2, (1,)), (4, 7, 1, 3, 1, (0, 2)), (9, 0, 0, 1, 2), (9, 0, 0, 1, 1),
        (6, 3, 0, 2, 0), (4, 6, 0, 0, 2, (1,)), (6, 4, 1, 3, 1), (5, 5, 0, 0, (1, 2)), (9, 3, 1, 3, 2),
        (8, 1, 0, 3, 1), (6, 5, 0, 0, 0), (6, 5, 0, 0, 2), (6, 5, 0, 0, 1), (8, 1, 0, 1, 2), (8, 2, 0, 2, 1),
        (4, 7, 1, 0, 2, (0, 1)), (4, 7, 0, 2, 1, (0, 2)), (4, 7, 1, 1, 0, (2,)), (9, 0, 0, 2, 2), (7, 3, 1),
        (8, 2, 0, 3, 1), (6, 4, 1, 0, 2), (6, 2, 0, 1, 0), (6, 2, 0, 1, 1), (8, 1, 0, 0, 2), (8, 4, 0, 2, 1),
        (6, 5, 0, 3, 2), (6, 0, 1, 0, 0), (6, 0, 1, 0, 1), (8, 2, 0, 1, 2), (8, 4, 0, 3, 1), (4, 7, 0, 1, 2, (0, 1)),
        (6, 1, 0, 0, 1), (6, 1, 0, 0, 0), (9, 2, 0, 0, 2), (9, 2, 0, 0, 1), (7, 2, 0), (6, 2, 0, 2, 2),
        (6, 2, 0, 2, 0), (6, 5, 0, 1, 1), (8, 4, 0, 1, 2), (8, 5, 0, 2, 1), (6, 5, 0, 1, 0), (6, 0, 1, 3, 2),
        (6, 1, 0, 1, 1), (8, 7, 0, 3, 0), (9, 4, 0, 0, 1), (9, 4, 0, 0, 2), (6, 1, 0, 1, 0), (6, 1, 0, 3, 2),
        (6, 4, 0, 1, 1), (9, 2, 0, 3, 0), (9, 2, 0, 3, 2), (7, 2, 1), (8, 5, 0, 3, 1), (7, 5, 0), (6, 5, 0, 2, 2),
        (6, 6, 0, 0, 1), (6, 6, 0, 0, 0), (9, 0, 0, 1, 0), (8, 5, 0, 1, 2), (8, 6, 0, 2, 1), (7, 1, 0),
        (6, 1, 0, 2, 2), (6, 1, 0, 2, 0), (6, 6, 0, 1, 1), (9, 4, 0, 3, 0), (9, 4, 0, 3, 2), (8, 6, 0, 3, 1),
        (7, 4, 0), (6, 4, 0, 2, 2), (6, 7, 0, 1, 1), (6, 7, 0, 1, 0), (9, 3, 0, 1, 0), (9, 2, 1, 3, 2),
        (9, 2, 1, 3, 1), (6, 6, 0, 3, 0), (6, 6, 0, 3, 2), (6, 7, 0, 0, 1), (8, 7, 1, 2, 0), (8, 6, 0, 1, 2),
        (8, 7, 1, 3, 1), (7, 6, 0), (6, 6, 0, 2, 2), (6, 6, 0, 2, 0), (6, 7, 1, 0, 1), (9, 3, 0, 2, 0),
        (8, 6, 0, 0, 2), (9, 4, 1, 3, 1), (6, 7, 0, 2, 0), (6, 7, 0, 2, 2), (6, 4, 1, 1, 1), (9, 5, 0, 0, 0),
        (9, 5, 0, 0, 2), (9, 5, 0, 0, 1), (7, 7, 0), (6, 6, 1, 3, 2), (7, 0, 0), (8, 7, 1, 0, 2), (8, 7, 0, 2, 1),
        (8, 7, 1, 1, 0), (6, 6, 1, 2, 1), (6, 7, 0, 3, 2), (7, 0, 1), (9, 4, 1, 0, 2), (9, 2, 0, 1, 0),
        (9, 2, 0, 1, 1), (7, 7, 1), (6, 7, 1, 3, 2), (7, 4, 1), (9, 5, 0, 3, 2), (9, 0, 1, 0, 0), (9, 0, 1, 0, 1),
        (7, 6, 1), (7, 5, 1), (8, 7, 0, 1, 2), (9, 1, 0, 0, 1), (9, 1, 0, 0, 0), (7, 1, 1), (9, 2, 0, 2, 2),
        (9, 2, 0, 2, 0), (9, 5, 0, 1, 1), (9, 5, 0, 1, 0), (9, 0, 1, 3, 2), (9, 1, 0, 1, 1), (9, 1, 0, 1, 0),
        (9, 1, 0, 3, 2), (9, 4, 0, 1, 1), (9, 5, 0, 2, 2), (9, 6, 0, 0, 1), (9, 6, 0, 0, 0), (9, 1, 0, 2, 2),
        (9, 1, 0, 2, 0), (9, 6, 0, 1, 1), (9, 4, 0, 2, 2), (9, 7, 0, 1, 1), (9, 7, 0, 1, 0), (9, 6, 0, 3, 0),
        (9, 6, 0, 3, 2), (9, 7, 0, 0, 1), (9, 6, 0, 2, 2), (9, 6, 0, 2, 0), (9, 7, 1, 0, 1), (9, 7, 0, 2, 0),
        (9, 7, 0, 2, 2), (9, 4, 1, 1, 1), (9, 6, 1, 3, 2), (9, 6, 1, 2, 1), (9, 7, 0, 3, 2), (9, 7, 1, 3, 2),
    ),
)


def grid_kernel(
    plan, h_ref, m_ref, r_ref, out_ref,
    hist, hist_hi, hist_lo, m_wide, m_tall, r_buf, part, landed, rows, acc, acc_other,
    local_sem, pair_send, pair_recv, m_local, m_send, m_recv, rs_send, rs_recv, ag_send, ag_recv,
):
    groups, pieces, orders = plan
    count = len(groups)
    me = lax.axis_index("rows")
    core, y, z = me % 2, (me // 2) % 2, me // 4
    side = z // 2
    middle = (z + side) % 2
    inner, outer = z + 1 - 2 * side, z - 1 + 2 * side

    def device(at_z, at_y, at_core):
        return (at_z * 2 + at_y) * 2 + at_core

    partner = device(z, y, 1 - core)
    across, diagonal = device(z, 1 - y, core), device(z, 1 - y, 1 - core)
    target = (across, device(inner, y, core), device(outer, y, core))
    heading = (0, 1 + side, 2 - side)
    came = (0, 2 - side, 1 + side)

    modes, outs = h_ref.shape[0], r_ref.shape[0]
    half = m_ref.shape[1] // 2
    span = half // (2 * count)
    piece = span // pieces

    wide = [q for q in range(count) if groups[q] == ALONG_FIRST]
    tall = [q for q in range(count) if groups[q] == ACROSS_FIRST]

    def line(dy):
        return 1 - y if dy else y

    def place(j):
        return j + side * (pieces - 1 - 2 * j)

    def slot(q, dy):
        if groups[q] == ALONG_FIRST:
            return 2 * wide.index(q) + line(dy)
        return 2 * len(wide) + tall.index(q)

    def span_of(j):
        return pl.ds(pl.multiple_of(place(j) * piece, piece), piece)

    def remote(src, dst, send, recv, to):
        return pltpu.make_async_remote_copy(
            src_ref=src, dst_ref=dst, send_sem=send, recv_sem=recv,
            device_id={"rows": to}, device_id_type=MESH,
        )

    def shapes(q, at_core, at_y):
        if groups[q] == ALONG_FIRST:
            return m_ref.at[:, pl.ds(pl.multiple_of(at_core * half + 2 * q * span, 128), 2 * span)]
        return m_ref.at[:, pl.ds(pl.multiple_of(at_core * half + (2 * q + at_y) * span, 128), span)]

    def held(q, source):
        source = pl.ds(source * modes, modes)
        if groups[q] == ALONG_FIRST:
            return m_wide.at[wide.index(q), source]
        return m_tall.at[tall.index(q), source]

    def own_m(q):
        return pltpu.make_async_copy(shapes(q, core, y), held(q, 0), m_local.at[q])

    def m_pair(q):
        return remote(shapes(q, 1 - core, y), held(q, 1), m_send.at[q, 0], m_recv.at[q, 0], partner)

    def m_across(q):
        return tuple(
            remote(
                shapes(q, at_core, 1 - y), held(q, source),
                m_send.at[q, source - 1], m_recv.at[q, source - 1], to,
            )
            for source, to, at_core in ((2, across, core), (3, diagonal, 1 - core))
        )

    own_h = pltpu.make_async_copy(h_ref, hist.at[pl.ds(0, modes)], local_sem.at[0])
    h_pair = remote(h_ref, hist.at[pl.ds(modes, modes)], pair_send.at[0], pair_recv.at[0], partner)
    h_across = remote(h_ref, hist.at[pl.ds(2 * modes, modes)], pair_send.at[1], pair_recv.at[1], across)
    h_relay = remote(
        hist.at[pl.ds(2 * modes, modes)], hist.at[pl.ds(3 * modes, modes)],
        pair_send.at[2], pair_recv.at[2], partner,
    )
    own_r = pltpu.make_async_copy(
        r_ref.at[:, pl.ds(pl.multiple_of(core * half, 128), half)],
        r_buf.at[pl.ds(0, outs)], local_sem.at[1],
    )
    r_copy = remote(
        r_ref.at[:, pl.ds(pl.multiple_of((1 - core) * half, 128), half)],
        r_buf.at[pl.ds(outs, outs)], pair_send.at[3], pair_recv.at[3], partner,
    )
    acc_copy = remote(acc.at[pl.ds(outs, outs)], acc_other, pair_send.at[4], pair_recv.at[4], partner)

    def rs_copy(q, dy, j, to, d):
        k = slot(q, dy)
        return remote(
            part.at[k, span_of(j)], landed.at[k, d, span_of(j)],
            rs_send.at[k, place(j), d], rs_recv.at[k, place(j), d], target[to],
        )

    def ag_copy(q, dy, j, to):
        k = 2 * q + line(dy)
        view = rows.at[k, span_of(j)]
        return remote(
            view, view, ag_send.at[k, place(j), heading[to]], ag_recv.at[k, place(j)], target[to]
        )

    def hist_ready(first, size):
        here = pl.ds(first * modes, size * modes)
        hist_hi[here], hist_lo[here] = split(hist[here])

    def run(order):
        seen = set()

        def once(key):
            fresh = key not in seen
            seen.add(key)
            return fresh

        def row_ready(q, dy, j):
            if once((ROOT, q, dy, j)):
                ag_copy(q, dy, j, ACROSS).wait_recv()

        def summed(q, dy, j, kids):
            total = part[slot(q, dy), span_of(j)]
            for kid in kids:
                rs_copy(q, dy, j, ACROSS, came[kid]).wait_recv()
            for kid in kids:
                total = total + landed[slot(q, dy), came[kid], span_of(j)]
            return total

        recoveries = [op for op in order if op[0] == RECOVER]
        for op in order:
            name, args = op[0], op[1:]
            if name == H_ACROSS:
                h_across.start()
            elif name == H_RELAY:
                h_across.wait_recv()
                h_relay.start()
                own_r.start()
                r_copy.start()
            elif name == SHARE:
                for copy in m_across(*args):
                    copy.start()
            elif name == PARTIAL:
                q, dy = args
                if once(PARTIAL):
                    own_h.wait()
                    h_pair.wait_recv()
                    hist_ready(0, 2)
                if once((PARTIAL, q)):
                    own_m(q).wait()
                    m_pair(q).wait_recv()
                if groups[q] == ALONG_FIRST:
                    buf, known = m_wide.at[wide.index(q)], pl.ds(0, 2 * modes)
                    cols = pl.ds(pl.multiple_of(line(dy) * span, 128), span)
                else:
                    if once(SHARE):
                        h_relay.wait_recv()
                        hist_ready(2, 2)
                    for copy in m_across(q):
                        copy.wait_recv()
                    buf, known, cols = m_tall.at[tall.index(q)], pl.ds(0, 4 * modes), pl.ds(0, span)
                part[slot(q, dy)] = dot3(split(buf[:, cols]), (hist_hi[known], hist_lo[known]), ((0,), (0,)))
            elif name == REDUCE:
                q, dy, j, to, kids = args
                if kids:
                    part[slot(q, dy), span_of(j)] = summed(q, dy, j, kids)
                rs_copy(q, dy, j, to, heading[to]).start()
            elif name == ROOT:
                q, dy, j, kids = args
                seen.add((ROOT, q, dy, j))
                rows[2 * q + line(dy), span_of(j)] = summed(q, dy, j, kids)
            elif name == GATHER:
                row_ready(*args[:3])
                ag_copy(*args).start()
            elif name == REDUCED:
                rs_copy(*args, heading[args[-1]]).wait_send()
            elif name == GATHERED:
                ag_copy(*args).wait_send()
            elif name == RECOVER:
                q, dy = args
                for j in range(pieces):
                    row_ready(q, dy, j)
                if once(RECOVER):
                    own_r.wait()
                    r_copy.wait_recv()
                known = 2 * q + line(dy)
                cols = pl.ds(pl.multiple_of(known * span, 128), span)
                values = split(rows[known])
                for base in (outs, 0):
                    here = pl.ds(base, outs)
                    added = dot3(split(r_buf[here, cols]), values, ((1,), (0,)))
                    acc[here] = added if op is recoveries[0] else acc[here] + added
                    if op is recoveries[-1] and base:
                        acc_copy.start()

    own_h.start()
    for q in wide + tall:
        own_m(q).start()
    barrier = pltpu.get_barrier_semaphore()
    for other in (partner, across, diagonal, target[INWARD]):
        pl.semaphore_signal(barrier, inc=1, device_id={"rows": other}, device_id_type=MESH)

    @pl.when(middle == 1)
    def _():
        pl.semaphore_signal(barrier, inc=1, device_id={"rows": target[OUTWARD]}, device_id_type=MESH)

    pl.semaphore_wait(barrier, 4 + middle)
    h_pair.start()
    for q in wide + tall:
        m_pair(q).start()

    for role in range(2):
        pl.when(middle == role)(functools.partial(run, orders[role]))

    h_pair.wait_send()
    h_across.wait_send()
    h_relay.wait_send()
    r_copy.wait_send()
    for q in range(count):
        m_pair(q).wait_send()
    for q in tall:
        for copy in m_across(q):
            copy.wait_send()
    acc_copy.wait()
    found = []
    for k in range(2):
        here = pl.ds(k * outs // 2, outs // 2)
        acc_other[here] = acc[here] + acc_other[here]
        found.append(pltpu.make_async_copy(acc_other.at[here], out_ref.at[here], local_sem.at[k]))
        found[k].start()
    for copy in found:
        copy.wait()


def grid_call(plan, histories, modal_map, recovery):
    modes, time_cols = histories.shape
    outs, dofs = recovery.shape
    groups, pieces, _ = plan
    half, count = dofs // 2, len(groups)
    span = half // (2 * count)
    n_wide, n_tall = groups.count(ALONG_FIRST), groups.count(ACROSS_FIRST)
    slots = 2 * n_wide + n_tall
    f32, dma = jnp.float32, pltpu.SemaphoreType.DMA
    anywhere = pl.BlockSpec(memory_space=pltpu.HBM)
    return pl.pallas_call(
        functools.partial(grid_kernel, plan),
        out_shape=jax.ShapeDtypeStruct((outs, time_cols), f32),
        in_specs=[anywhere, anywhere, anywhere],
        out_specs=pl.BlockSpec(memory_space=pl.ANY),
        scratch_shapes=[
            pltpu.VMEM((4 * modes, time_cols), f32),
            pltpu.VMEM((4 * modes, time_cols), jnp.bfloat16),
            pltpu.VMEM((4 * modes, time_cols), jnp.bfloat16),
            pltpu.VMEM((n_wide, 2 * modes, 2 * span), f32),
            pltpu.VMEM((n_tall, 4 * modes, span), f32),
            pltpu.VMEM((2 * outs, half), f32),
            pltpu.VMEM((slots, span, time_cols), f32),
            pltpu.VMEM((slots, 3, span, time_cols), f32),
            pltpu.VMEM((2 * count, span, time_cols), f32),
            pltpu.VMEM((2 * outs, time_cols), f32),
            pltpu.VMEM((outs, time_cols), f32),
            dma((2,)),
            dma((5,)),
            dma((5,)),
            dma((count,)),
            dma((count, 3)),
            dma((count, 3)),
            dma((slots, pieces, 3)),
            dma((slots, pieces, 3)),
            dma((2 * count, pieces, 3)),
            dma((2 * count, pieces)),
        ],
        compiler_params=pltpu.CompilerParams(
            collective_id=1, has_side_effects=True, vmem_limit_bytes=52 * 2**20
        ),
    )(histories, modal_map, recovery)


def ring_call(chips, histories, modal_map, recovery):
    modes, time_cols = histories.shape
    outs, dofs = recovery.shape
    half = dofs // 2
    block = half // chips
    ways = 2 if block % 256 == 0 else 1
    unit = block // ways
    f32, dma = jnp.float32, pltpu.SemaphoreType.DMA
    vmem, anywhere = pl.BlockSpec(memory_space=pltpu.VMEM), pl.BlockSpec(memory_space=pltpu.HBM)
    return pl.pallas_call(
        functools.partial(kernel, chips, ways),
        out_shape=jax.ShapeDtypeStruct((outs, time_cols), f32),
        in_specs=[anywhere, anywhere, anywhere],
        out_specs=vmem,
        scratch_shapes=[
            pltpu.VMEM((2 * modes, time_cols), f32),
            pltpu.VMEM((2 * modes, time_cols), jnp.bfloat16),
            pltpu.VMEM((2 * modes, time_cols), jnp.bfloat16),
            pltpu.VMEM((2 * modes, half), f32),
            pltpu.VMEM((2 * outs, half), f32),
            pltpu.VMEM((ways, chips - 1, unit, time_cols), f32),
            pltpu.VMEM((ways, chips - 1, unit, time_cols), f32),
            pltpu.VMEM((chips, ways, unit, time_cols), f32),
            pltpu.VMEM((2 * outs, time_cols), f32),
            pltpu.VMEM((outs, time_cols), f32),
            dma((2,)),
            dma((3,)),
            dma((3,)),
            dma((ways, chips)),
            dma((ways, chips)),
            dma((ways, chips)),
            dma((ways, chips - 1, SUBS)),
            dma((ways, chips - 1, SUBS)),
            dma((ways, chips - 1, SUBS)),
            dma((ways, chips - 1, SUBS)),
        ],
        compiler_params=pltpu.CompilerParams(
            collective_id=0, has_side_effects=True, vmem_limit_bytes=50 * 2**20
        ),
    )(histories, modal_map, recovery)


def shards(size, histories, modal_map, recovery):
    chips = size // 2
    time_cols, outs = histories.shape[1], recovery.shape[0]
    f32, vmem = jnp.float32, pl.BlockSpec(memory_space=pltpu.VMEM)
    if chips == 8:
        found = grid_call((GROUPS, PIECES, ORDERS), histories, modal_map, recovery)
    else:
        found = ring_call(chips, histories, modal_map, recovery)
    return pl.pallas_call(
        statistics,
        out_shape=(
            jax.ShapeDtypeStruct((outs, time_cols), f32),
            jax.ShapeDtypeStruct((CASES, outs), f32),
            jax.ShapeDtypeStruct((CASES, outs), f32),
        ),
        in_specs=[vmem], compiler_params=pltpu.CompilerParams(vmem_limit_bytes=8 * 2**20),
        out_specs=(vmem, vmem, vmem),
    )(found)


def solution(mesh):
    return jax.shard_map(
        functools.partial(shards, mesh.shape["rows"]),
        mesh=mesh,
        in_specs=(P(("grp", "rows"), None), P(("grp", "rows"), None), P(("grp", "rows"), None)),
        out_specs=(P(("grp", "rows"), None), P(None, ("grp", "rows")), P(None, ("grp", "rows"))),
        check_vma=False,
    )
```
